256 devices in a mesh: row: 8 (over y, core), col: 16 (over z_hi, x), layer: 2 (over z_lo).
Axes of the slice: x: 4, y: 4, z: 8 (z_hi: 4, z_lo: 2; z = z_hi * 2 + z_lo), core: 2. Of those that a mesh axis runs over, the one named last changes fastest.
Arguments:
- tile_values: float32 [8, 32, 2, 6, 128, 128], P('row', ('col', 'layer')), may hold values from -1.8 to 1.8
- tile_rows: int32 [8, 32, 2, 6], P('row', ('col', 'layer')), may hold values from 0 to 255, as said below
- tile_cols: int32 [8, 32, 2, 6], P('row', ('col', 'layer')), may hold values from 0 to 255, as said below
- tile_counts: int32 [8, 32, 2], P('row', ('col', 'layer')), may hold values from 1 to 6, as said below
- out_rows: int32 [8, 16, 2, 12], P('row', 'col'), may hold values from 0 to 255, as said below
- out_cols: int32 [8, 16, 2, 12], P('row', 'col'), may hold values from 0 to 255, as said below
Outputs:
- squared: float32 [8, 32, 12, 128, 128], P('row', ('col', 'layer'))
The draws below stay inside these ranges and needn't reach their ends.
Inputs may be any that keep to these rules, and one draw needn't show every extreme that they name: `tile_rows`: entry [r, s, h, q] lies in row band r (the 32 block rows from r * 32), in a run of 8 block rows whose index is congruent to h modulo 2; within one list [r, s, h] the 6 slots have distinct rows. `tile_cols`: entry [r, s, h, q] lies in sub-band s: block columns s * 8 to s * 8 + 7. Slots q < tile_counts[r, s, h] of list [r, s, h] hold tiles; values and coordinates in later slots mean nothing. Some list holds 6 tiles in every draw. out_rows[r, c, l, o] and out_cols[r, c, l, o] place the o-th kept tile of row band r and sub-band c * 2 + l; the row lies in row band r, the column in that sub-band, and the 12 positions of one [r, c, l] are distinct. `out_cols`: see out_rows.
All inputs are finite; a program needn't handle non-finite values.
Results may differ from the reference program's by a relative error of at most 0.0003.
Values sent between devices are 32-bit elements; how exact they have to be, the bound alone decides.
No kernel may reach another device: no remote copies, remote signals or barrier semaphores. Data moves between devices by JAX's collectives and lax.ppermute only.
A program may use at most 128 MiB of HBM per device.

```python
import jax
import jax.numpy as jnp
from jax import lax

BS = 128
NBS = 8
CAP = 6
OCAP = 12
N_ROW = 8
N_COL = 16
N_LAYER = 2


def layout(key):
    sub_count = N_COL * N_LAYER
    block_count = NBS * sub_count
    band_rows = block_count // N_ROW
    half_rows = band_rows // N_LAYER
    list_shape = (N_ROW, sub_count, N_LAYER)
    list_total = N_ROW * sub_count * N_LAYER
    counts = jax.random.randint(jax.random.fold_in(key, 101), list_shape, 1, CAP + 1)
    chosen = jax.random.randint(jax.random.fold_in(key, 102), (), 0, list_total)
    counts = jnp.where(jnp.arange(list_total).reshape(list_shape) == chosen, CAP, counts).astype(jnp.int32)
    row_scores = jax.random.randint(jax.random.fold_in(key, 103), list_shape + (half_rows,), 0, 4096) * half_rows + jnp.arange(half_rows)
    unused, local_rows = lax.top_k(row_scores, CAP)
    band_block = local_rows // NBS * N_LAYER + jnp.arange(N_LAYER)[None, None, :, None]
    rows = jnp.arange(N_ROW)[:, None, None, None] * band_rows + band_block * NBS + local_rows % NBS
    rows = rows.astype(jnp.int32)
    cols = jnp.arange(sub_count)[None, :, None, None] * NBS + jax.random.randint(jax.random.fold_in(key, 104), list_shape + (CAP,), 0, NBS)
    cols = cols.astype(jnp.int32)
    live_mask = jnp.arange(CAP)[None, None, None, :] < counts[..., None]
    live_rows = jnp.where(live_mask, rows, block_count).reshape(-1)
    occupancy = jnp.zeros((block_count + 1, block_count), jnp.int32).at[live_rows, cols.reshape(-1)].set(1)[:block_count]
    reach = jnp.minimum(jnp.dot(occupancy, occupancy), 1)
    spots = band_rows * NBS
    reach_blocks = reach.reshape(N_ROW, band_rows, sub_count, NBS).transpose(0, 2, 1, 3).reshape(N_ROW, sub_count, spots)
    out_scores = reach_blocks * (1 << 28) + jax.random.randint(jax.random.fold_in(key, 105), (N_ROW, sub_count, spots), 0, 256) * spots + jnp.arange(spots)
    unused_too, picked = lax.top_k(out_scores, OCAP)
    kept_rows = jnp.arange(N_ROW)[:, None, None] * band_rows + picked // NBS
    kept_cols = jnp.arange(sub_count)[None, :, None] * NBS + picked % NBS
    kept_rows = kept_rows.reshape(N_ROW, N_COL, N_LAYER, OCAP).astype(jnp.int32)
    kept_cols = kept_cols.reshape(N_ROW, N_COL, N_LAYER, OCAP).astype(jnp.int32)
    return (rows, cols, counts, kept_rows, kept_cols)


def draw_tile_rows(key, part):
    return layout(key)[0]


def draw_tile_cols(key, part):
    return layout(key)[1]


def draw_tile_counts(key, part):
    return layout(key)[2]


def draw_out_rows(key, part):
    return layout(key)[3]


def draw_out_cols(key, part):
    return layout(key)[4]


def block_levels(own_key, shape, split, smallest, high):
    level = 1.0
    for axis_at, blocks in split:
        draws = jax.random.uniform(jax.random.fold_in(jax.random.fold_in(own_key, 6), axis_at), (blocks,), jnp.float32, smallest / len(split), high / len(split))
        level = level * jnp.repeat(jnp.exp(draws), shape[axis_at] // blocks).reshape((-1,) + (1,) * (len(shape) - 1 - axis_at))
    return level


def noise(own_key, shape, width, bound, cuts=(), kind=jnp.bfloat16):
    values = width * jax.random.normal(own_key, shape, jnp.float32)
    if cuts:
        values = values * block_levels(own_key, shape, cuts, -0.22, 0.18)
    return jnp.clip(values, -bound, bound).astype(kind)


def setup_inputs(seed: int = 0) -> dict:
    splits = jax.random.split(jax.random.key(seed), 7)
    tile_values = noise(splits[0], (N_ROW, N_COL * N_LAYER, N_LAYER, CAP, BS, BS), 0.3, 1.8, ((0, 8), (1, 32)), jnp.float32)
    tile_rows = draw_tile_rows(jax.random.fold_in(splits[6], 71), 0)
    tile_cols = draw_tile_cols(jax.random.fold_in(splits[6], 71), 0)
    tile_counts = draw_tile_counts(jax.random.fold_in(splits[6], 71), 0)
    out_rows = draw_out_rows(jax.random.fold_in(splits[6], 71), 0)
    out_cols = draw_out_cols(jax.random.fold_in(splits[6], 71), 0)
    return dict(tile_values=tile_values, tile_rows=tile_rows, tile_cols=tile_cols, tile_counts=tile_counts, out_rows=out_rows, out_cols=out_cols)


def tile_lookup(tile_rows, tile_cols, tile_counts, block_count):
    slot_ids = jnp.arange(CAP, dtype=jnp.int32)
    is_live = slot_ids[None, None, None, :] < tile_counts[..., None]
    live_rows = jnp.where(is_live, tile_rows, block_count).astype(jnp.int32).reshape(-1)
    live_cols = tile_cols.astype(jnp.int32).reshape(-1)
    tile_ids = jnp.arange(live_rows.shape[0], dtype=jnp.int32)
    blank = jnp.full((block_count + 1, block_count), -1, dtype=jnp.int32)
    return blank.at[live_rows, live_cols].set(tile_ids)[:block_count]


def reference(tile_values, tile_rows, tile_cols, tile_counts, out_rows, out_cols):
    sub_count = N_COL * N_LAYER
    block_count = NBS * sub_count
    lookup = tile_lookup(tile_rows, tile_cols, tile_counts, block_count)
    flat_values = tile_values.reshape(-1, BS, BS)
    offsets = jnp.arange(sub_count, dtype=jnp.int32) * NBS

    def one_target(target):
        row_index, col_index = target
        row_table = lookup[row_index].reshape(sub_count, NBS)
        left_ids = jnp.max(row_table, axis=1)
        inner_index = jnp.argmax(row_table, axis=1).astype(jnp.int32) + offsets
        right_ids = lookup[inner_index, col_index]
        weight = jnp.where((left_ids >= 0) & (right_ids >= 0), 1.0, 0.0).astype(jnp.float32)
        left_tiles = flat_values[jnp.maximum(left_ids, 0)]
        right_tiles = flat_values[jnp.maximum(right_ids, 0)]
        products = jnp.einsum("spq,sqr->spr", left_tiles, right_tiles, precision=lax.Precision.HIGHEST)
        return jnp.sum(products * weight[:, None, None], axis=0)

    rows_grouped = out_rows.astype(jnp.int32).reshape(-1, OCAP)
    cols_grouped = out_cols.astype(jnp.int32).reshape(-1, OCAP)
    result = lax.map(jax.vmap(one_target), (rows_grouped, cols_grouped))
    return result.reshape(N_ROW, N_COL * N_LAYER, OCAP, BS, BS)
```

```python
import functools

import jax
import jax.numpy as jnp
from jax import lax
from jax.experimental import pallas as pl
from jax.experimental.pallas import tpu as pltpu
from jax.sharding import PartitionSpec as P

GROUP = ("col", "layer")
LANES = 128
SLOT_PITCH = 16
ROUND_CAP = 20


def pack_body(tiles_ref, meta_ref, out_ref):
    peers, per_peer, strip, _ = out_ref.shape

    def one_tile(tile, carry):
        for peer in range(peers):
            out_ref[peer, tile] = tiles_ref[tile, peer * strip:(peer + 1) * strip, :]
        return carry

    lax.fori_loop(0, per_peer - 1, one_tile, 0)
    for peer in range(peers):
        out_ref[peer, per_peer - 1] = meta_ref[...]


def plan_body(scalars, strips_ref, send_ref, codes_ref, counts_ref, table, picks, codes_smem, sem):
    row_index, base = scalars[0], scalars[1]
    peers, cap = send_ref.shape[:2]
    per_peer = strips_ref.shape[0] // peers
    band = 8
    blocks = peers * band
    groups = peers * SLOT_PITCH // LANES
    peers_per_group = LANES // SLOT_PITCH
    f32, bf16 = jnp.float32, jnp.bfloat16

    tall = lax.broadcasted_iota(jnp.int32, (blocks, LANES), 0).astype(f32) + 1.0
    short = lax.broadcasted_iota(jnp.int32, (band, LANES), 0).astype(f32) + 1.0
    names = lax.broadcasted_iota(jnp.int32, (band, LANES), 1).astype(f32) + 1.0
    targets = []
    for peer in range(peers):
        meta = strips_ref[peer * per_peer + per_peer - 1]
        row_hot = jnp.where(tall == meta[0:1, :], 1.0, 0.0).astype(bf16)
        col_hot = jnp.where(short + float(peer * band) == meta[1:2, :], names, 0.0).astype(bf16)
        table[peer * band:(peer + 1) * band, :] = lax.dot_general(
            col_hot, row_hot, (((1,), (1,)), ((), ())), preferred_element_type=f32
        )
        if peer % peers_per_group == 0:
            targets.append(meta)
        else:
            targets[-1] = targets[-1] + meta
    by_col = table[...]
    by_row = by_col.T.astype(bf16)
    by_col = by_col.astype(bf16)

    inner = lax.broadcasted_iota(jnp.int32, (blocks, LANES), 0)
    lane = lax.broadcasted_iota(jnp.int32, (blocks, LANES), 1)
    below = jnp.where(
        lax.broadcasted_iota(jnp.int32, (blocks, blocks), 0) >= lax.broadcasted_iota(jnp.int32, (blocks, blocks), 1),
        1.0, 0.0,
    ).astype(bf16)
    lane_from = lax.broadcasted_iota(jnp.int32, (LANES, LANES), 0)
    lane_to = lax.broadcasted_iota(jnp.int32, (LANES, LANES), 1)
    same_peer = lane_from // SLOT_PITCH == lane_to // SLOT_PITCH
    earlier = jnp.where(same_peer & (lane_from < lane_to), 1.0, 0.0).astype(bf16)
    together = jnp.where(same_peer, 1.0, 0.0)
    fixed_code = (inner // band) * per_peer - SLOT_PITCH * row_index - 1 - 512 + ((lane % SLOT_PITCH) << 16)

    counts = []
    for group in range(groups):
        left_hot = jnp.where(tall == targets[group][2:3, :], 1.0, 0.0).astype(bf16)
        right_hot = jnp.where(tall == targets[group][3:4, :], 1.0, 0.0).astype(bf16)
        left = jnp.dot(by_col, left_hot, preferred_element_type=f32)
        right = jnp.dot(by_row, right_hot, preferred_element_type=f32)
        hit = left * right > 0.0
        ranks = jnp.dot(below, jnp.where(hit, 1.0, 0.0).astype(bf16), preferred_element_type=f32)
        found = jnp.broadcast_to(ranks[blocks - 1:blocks, :], (band, LANES))
        ahead = jnp.dot(found.astype(bf16), earlier, preferred_element_type=f32)
        counts.append(jnp.dot(found.astype(bf16), together.astype(bf16), preferred_element_type=f32)[0:1, :])
        place = (ranks + ahead[0:1, :]).astype(jnp.int32) - 1 - base
        place = jnp.where(hit, place, -1)
        code = (fixed_code + left.astype(jnp.int32) + (right.astype(jnp.int32) << 9)).astype(f32)
        for at in range(cap):
            picks[group * cap + at:group * cap + at + 1, :] = jnp.sum(
                jnp.where(place == at, code, 0.0), axis=0, keepdims=True
            )
    spread = jnp.dot(picks[...], together, precision=lax.Precision.HIGHEST, preferred_element_type=f32).astype(jnp.int32)
    slot = lax.broadcasted_iota(jnp.int32, (1, LANES), 1) % SLOT_PITCH
    halves = pl.cdiv(cap, SLOT_PITCH)
    rows = []
    for group in range(groups):
        for half in range(halves):
            merged = jnp.zeros((1, LANES), jnp.int32)
            for at in range(half * SLOT_PITCH, min(cap, (half + 1) * SLOT_PITCH)):
                here = spread[group * cap + at:group * cap + at + 1, :]
                merged = jnp.where(slot == at % SLOT_PITCH, here, merged)
            rows.append(merged)
    codes_ref[...] = jnp.concatenate(rows, axis=0)
    counts_ref[...] = jnp.concatenate(counts + counts, axis=0)[0:8, :].astype(jnp.int32)
    copy = pltpu.make_async_copy(codes_ref, codes_smem, sem)
    copy.start()
    copy.wait()

    def one_peer(peer, carry):
        line = (peer // peers_per_group) * halves
        first = (peer % peers_per_group) * SLOT_PITCH
        for at in range(cap):
            found_at = codes_smem[line + at // SLOT_PITCH, first + at % SLOT_PITCH] & 511
            send_ref[peer, at] = strips_ref[found_at]
        return carry

    lax.fori_loop(0, peers, one_peer, 0)


def product_body(first, scalars, codes, counts, *refs):
    strips_ref = refs[0]
    panels = refs[1:9]
    if first:
        out_ref, right, left, sems = refs[9:]
    else:
        running_ref, out_ref, right, left, sems = refs[9:]
    row_index, base, own = scalars[0], scalars[1], scalars[2]
    peers, cap, strip, _ = strips_ref.shape
    halves = pl.cdiv(cap, SLOT_PITCH)
    peers_per_group = LANES // SLOT_PITCH
    line = (own // peers_per_group) * halves
    lane = (own % peers_per_group) * SLOT_PITCH
    todo = jnp.clip(counts[own // peers_per_group, lane] - base, 0, cap)
    bf16 = jnp.bfloat16

    def code_of(at):
        return codes[line + at // SLOT_PITCH, lane + at % SLOT_PITCH]

    def fetch(at, carry):
        name = (code_of(at) >> 9) & 127
        from_row, slot = name // SLOT_PITCH, name % SLOT_PITCH
        away = ((row_index // 2 - from_row // 2) & 3) + ((row_index ^ from_row) & 1) * 4
        for index, panel in enumerate(panels):
            @pl.when(away == index)
            def _():
                pltpu.make_async_copy(panel.at[slot], right.at[at], sems.at[at]).start()
        return carry

    lax.fori_loop(0, todo, fetch, 0)
    if first:
        out_ref[...] = jnp.zeros_like(out_ref)
    else:
        out_ref[...] = running_ref[...]

    def multiply(at, carry):
        for peer in range(peers):
            left[peer * strip:(peer + 1) * strip, :] = strips_ref[peer, at]
        pltpu.make_async_copy(panels[0].at[0], right.at[at], sems.at[at]).wait()
        a, b = left[...], right[at]
        a_high = a.astype(bf16)
        b_high = b.astype(bf16)
        a_low = (a - a_high.astype(jnp.float32)).astype(bf16)
        b_low = (b - b_high.astype(jnp.float32)).astype(bf16)
        product = jnp.dot(a_high, b_low, preferred_element_type=jnp.float32)
        product = product + jnp.dot(a_low, b_high, preferred_element_type=jnp.float32)
        product = product + jnp.dot(a_high, b_high, preferred_element_type=jnp.float32)
        target = code_of(at) >> 16
        out_ref[target] = out_ref[target] + product
        return carry

    lax.fori_loop(0, todo, multiply, 0)


def whole(shape):
    return pl.BlockSpec(shape, lambda i, *_: (0,) * len(shape))


def pack(tiles, meta, peers):
    count, order = tiles.shape[:2]
    shape = (peers, count + 1, order // peers, order)
    return pl.pallas_call(pack_body, out_shape=jax.ShapeDtypeStruct(shape, jnp.float32))(tiles, meta)


def plan(strips, row_index, base, peers, cap):
    strip, order = strips.shape[1:]
    groups = peers * SLOT_PITCH // LANES
    lines = groups * pl.cdiv(cap, SLOT_PITCH)
    send = (peers, cap, strip, order)
    return pl.pallas_call(
        plan_body,
        grid_spec=pltpu.PrefetchScalarGridSpec(
            num_scalar_prefetch=1,
            grid=(1,),
            in_specs=[whole(strips.shape)],
            out_specs=[whole(send), whole((lines, LANES)), whole((8, LANES))],
            scratch_shapes=[
                pltpu.VMEM((peers * 8, peers * 8), jnp.float32),
                pltpu.VMEM((groups * cap, LANES), jnp.float32),
                pltpu.SMEM((lines, LANES), jnp.int32),
                pltpu.SemaphoreType.DMA,
            ],
        ),
        out_shape=[
            jax.ShapeDtypeStruct(send, jnp.float32),
            jax.ShapeDtypeStruct((lines, LANES), jnp.int32),
            jax.ShapeDtypeStruct((8, LANES), jnp.int32),
        ],
    )(jnp.stack([row_index, base]), strips)


def multiply_round(strips, panels, codes, counts, row_index, base, own, running, kept):
    peers, cap, strip, order = strips.shape
    first = running is None
    tiles = (kept, order, order)
    operands = [strips, *panels] + ([] if first else [running])
    in_specs = [whole(strips.shape)] + [pl.BlockSpec(memory_space=pl.ANY)] * len(panels)
    if not first:
        in_specs.append(whole(tiles))
    return pl.pallas_call(
        functools.partial(product_body, first),
        grid_spec=pltpu.PrefetchScalarGridSpec(
            num_scalar_prefetch=3,
            grid=(1,),
            in_specs=in_specs,
            out_specs=whole(tiles),
            scratch_shapes=[
                pltpu.VMEM((cap, order, order), jnp.float32),
                pltpu.VMEM((order, order), jnp.float32),
                pltpu.SemaphoreType.DMA((cap,)),
            ],
        ),
        out_shape=jax.ShapeDtypeStruct(tiles, jnp.float32),
    )(jnp.stack([row_index, base, own]), codes, counts, *operands)


def shift_rows(array, rows, by):
    return lax.ppermute(array, "row", [(i, (i + by) % rows) for i in range(rows)])


def swap_rows(array, rows, by):
    return lax.ppermute(array, "row", [(i, i ^ by) for i in range(rows)])


def local(tile_values, tile_rows, tile_cols, tile_counts, out_rows, out_cols):
    order = tile_values.shape[-1]
    capacity = tile_rows.shape[-1]
    kept = out_rows.shape[-1]
    rows = lax.axis_size("row")
    peers = lax.axis_size(GROUP)
    row_index = lax.axis_index("row")
    own = lax.axis_index(GROUP)
    layer_index = lax.axis_index("layer")
    tiles = tile_values.reshape(-1, order, order)

    live = jnp.arange(capacity, dtype=jnp.int32) < tile_counts.reshape(-1, 1)
    own_rows = jnp.where(live, tile_rows[0, 0] + 1, 0).reshape(-1)
    own_cols = jnp.where(live, tile_cols[0, 0] + 1, 0).reshape(-1)
    lane = jnp.arange(LANES, dtype=jnp.int32)

    def at_lanes(values, group):
        spread = jnp.tile(jnp.pad(values, (0, SLOT_PITCH - values.shape[0])), LANES // SLOT_PITCH)
        return jnp.where(lane // SLOT_PITCH == group, spread, 0)

    listed = jnp.stack([at_lanes(own_rows, row_index), at_lanes(own_cols, row_index)]).astype(jnp.float32)
    in_group = own % (LANES // SLOT_PITCH)
    target_rows = lax.dynamic_index_in_dim(out_rows[0, 0], layer_index, 0, keepdims=False) + 1
    target_cols = lax.dynamic_index_in_dim(out_cols[0, 0], layer_index, 0, keepdims=False) + 1
    wanted = jnp.stack([at_lanes(target_rows, in_group), at_lanes(target_cols, in_group)]).astype(jnp.float32)
    for by in (1, 2, 4):
        listed = listed + swap_rows(listed, rows, by)
    meta = jnp.concatenate([listed, wanted])

    strips = pack(tiles, meta, peers)
    strips = lax.all_to_all(strips, GROUP, 0, 0, tiled=True)
    near = [tiles] + [shift_rows(tiles, rows, by) for by in (2, 4, 6)]
    strips = strips.reshape(-1, order // peers, order)

    zero = jnp.zeros((), jnp.int32)
    send, codes, counts = plan(strips, row_index, zero, peers, ROUND_CAP)
    send, near = lax.optimization_barrier((send, near))
    panels = near + [swap_rows(piece, rows, 1) for piece in near]
    most = jnp.max(counts)
    for by in (1, 2, 4):
        most = jnp.maximum(most, swap_rows(most, rows, by))
    received = lax.all_to_all(send, GROUP, 0, 0, tiled=True)
    summed = multiply_round(received, panels, codes, counts, row_index, zero, own, None, kept)

    def unfinished(state):
        return state[0] < most

    def further(state):
        base, running = state
        send, codes, counts = plan(strips, row_index, base, peers, ROUND_CAP)
        received = lax.all_to_all(send, GROUP, 0, 0, tiled=True)
        running = multiply_round(received, panels, codes, counts, row_index, base, own, running, kept)
        return base + ROUND_CAP, running

    unused, summed = lax.while_loop(unfinished, further, (jnp.int32(ROUND_CAP), summed))
    return summed.reshape(1, 1, kept, order, order)


def solution(mesh):
    in_specs = (
        P("row", GROUP, None, None, None, None),
        P("row", GROUP, None, None),
        P("row", GROUP, None, None),
        P("row", GROUP, None),
        P("row", "col", None, None),
        P("row", "col", None, None),
    )
    out_specs = P("row", GROUP, None, None, None)
    return jax.shard_map(local, mesh=mesh, in_specs=in_specs, out_specs=out_specs, check_vma=False)
```

```python
import functools

import jax
import jax.numpy as jnp
from jax import lax
from jax.experimental import pallas as pl
from jax.experimental.pallas import tpu as pltpu
from jax.sharding import PartitionSpec as P

GROUP = ("col", "layer")
LANES = 128
SLOT_PITCH = 16
ROUND_CAP = 20
LIMIT = pltpu.CompilerParams(vmem_limit_bytes=20 * 2**20)


def label_body(tile_rows, tile_cols, counts, out_rows, out_cols, listed_ref, wanted_ref):
    lists, capacity = tile_rows.shape[2:]
    row_index, layer_index = lax.axis_index("row"), lax.axis_index("layer")
    in_group = lax.axis_index(GROUP) % (LANES // SLOT_PITCH)
    lane = lax.broadcasted_iota(jnp.int32, (1, LANES), 1)
    nothing = jnp.zeros((1, LANES), jnp.int32)
    rows, cols, kept_rows, kept_cols = nothing, nothing, nothing, nothing
    mate_rows, mate_cols = nothing, nothing
    for at in range(lists):
        for slot in range(capacity):
            live = slot < counts[0, 0, at]
            here = lane == jnp.where(live, row_index * SLOT_PITCH + at * capacity + slot, -1)
            rows = jnp.where(here, tile_rows[0, 0, at, slot] + 1, rows)
            cols = jnp.where(here, tile_cols[0, 0, at, slot] + 1, cols)
    for at in range(out_rows.shape[3]):
        here = lane == in_group * SLOT_PITCH + at
        kept_rows = jnp.where(here, out_rows[0, 0, layer_index, at] + 1, kept_rows)
        kept_cols = jnp.where(here, out_cols[0, 0, layer_index, at] + 1, kept_cols)
        here = lane == row_index * SLOT_PITCH + at
        mate_rows = jnp.where(here, out_rows[0, 0, layer_index, at] + 1, mate_rows)
        mate_cols = jnp.where(here, out_cols[0, 0, layer_index, at] + 1, mate_cols)
    listed_ref[...] = jnp.concatenate([rows, cols, mate_rows, mate_cols]).astype(jnp.float32)
    wanted_ref[...] = jnp.concatenate([kept_rows, kept_cols]).astype(jnp.float32)


def pack_body(tiles_ref, listed_ref, wanted_ref, out_ref):
    peers, per_peer, strip, _ = out_ref.shape

    def one_tile(tile, carry):
        for peer in range(peers):
            out_ref[peer, tile] = tiles_ref[tile, peer * strip:(peer + 1) * strip, :]
        return carry

    lax.fori_loop(0, per_peer - 1, one_tile, 0)
    for peer in range(peers):
        out_ref[peer, per_peer - 1, 0:2, :] = listed_ref[0:2, :]
        out_ref[peer, per_peer - 1, 2:4, :] = wanted_ref[...]


def pack_right_body(tiles_ref, *out_refs):
    count, strip, _ = out_refs[0].shape
    row_index = lax.axis_index("row")
    for away, out_ref in enumerate(out_refs):
        start = pl.multiple_of((row_index + away) % len(out_refs) * strip, strip)
        for tile in range(count):
            out_ref[tile] = tiles_ref[tile, pl.ds(start, strip), :]


def plan_body(rows, scalars, strips_ref, mates_ref, *refs):
    piece_refs, send_ref, right_refs = refs[:rows], refs[rows], refs[rows + 1:2 * rows + 1]
    codes_ref, counts_ref, table, picks, panel, codes_smem, sem = refs[2 * rows + 1:]
    row_index, base = scalars[0], scalars[1]
    peers, cap = send_ref.shape[:2]
    per_peer = strips_ref.shape[0] // peers
    band = 8
    blocks = peers * band
    groups = peers * SLOT_PITCH // LANES
    peers_per_group = LANES // SLOT_PITCH
    f32, bf16 = jnp.float32, jnp.bfloat16

    tall = lax.broadcasted_iota(jnp.int32, (blocks, LANES), 0).astype(f32) + 1.0
    short = lax.broadcasted_iota(jnp.int32, (band, LANES), 0).astype(f32) + 1.0
    names = lax.broadcasted_iota(jnp.int32, (band, LANES), 1).astype(f32) + 1.0
    targets = []
    for peer in range(peers):
        meta = strips_ref[peer * per_peer + per_peer - 1]
        row_hot = jnp.where(tall == meta[0:1, :], 1.0, 0.0).astype(bf16)
        col_hot = jnp.where(short + float(peer * band) == meta[1:2, :], names, 0.0).astype(bf16)
        table[peer * band:(peer + 1) * band, :] = lax.dot_general(
            col_hot, row_hot, (((1,), (1,)), ((), ())), preferred_element_type=f32
        )
        if peer % peers_per_group == 0:
            targets.append(meta)
        else:
            targets[-1] = targets[-1] + meta
    by_col = table[...]
    by_row = by_col.T.astype(bf16)
    by_col = by_col.astype(bf16)

    inner = lax.broadcasted_iota(jnp.int32, (blocks, LANES), 0)
    lane = lax.broadcasted_iota(jnp.int32, (blocks, LANES), 1)
    below = jnp.where(
        lax.broadcasted_iota(jnp.int32, (blocks, blocks), 0) >= lax.broadcasted_iota(jnp.int32, (blocks, blocks), 1),
        1.0, 0.0,
    ).astype(bf16)
    lane_from = lax.broadcasted_iota(jnp.int32, (LANES, LANES), 0)
    lane_to = lax.broadcasted_iota(jnp.int32, (LANES, LANES), 1)
    same_peer = lane_from // SLOT_PITCH == lane_to // SLOT_PITCH
    earlier = jnp.where(same_peer & (lane_from < lane_to), 1.0, 0.0).astype(bf16)
    together = jnp.where(same_peer, 1.0, 0.0)
    fixed_code = (inner // band) * per_peer - SLOT_PITCH * row_index - 1 - 512 + ((lane % SLOT_PITCH) << 16)

    targets = [(meta[2:3, :], meta[3:4, :]) for meta in targets]
    targets.append((mates_ref[2:3, :], mates_ref[3:4, :]))
    counts = []
    for group, (target_rows, target_cols) in enumerate(targets):
        left_hot = jnp.where(tall == target_rows, 1.0, 0.0).astype(bf16)
        right_hot = jnp.where(tall == target_cols, 1.0, 0.0).astype(bf16)
        left = jnp.dot(by_col, left_hot, preferred_element_type=f32)
        right = jnp.dot(by_row, right_hot, preferred_element_type=f32)
        hit = left * right > 0.0
        ranks = jnp.dot(below, jnp.where(hit, 1.0, 0.0).astype(bf16), preferred_element_type=f32)
        found = jnp.broadcast_to(ranks[blocks - 1:blocks, :], (band, LANES))
        ahead = jnp.dot(found.astype(bf16), earlier, preferred_element_type=f32)
        counts.append(jnp.dot(found.astype(bf16), together.astype(bf16), preferred_element_type=f32)[0:1, :])
        place = (ranks + ahead[0:1, :]).astype(jnp.int32) - 1 - base
        place = jnp.where(hit, place, -1)
        if group < groups:
            code = (fixed_code + left.astype(jnp.int32) + (right.astype(jnp.int32) << 9)).astype(f32)
        else:
            code = right - 1.0
        for at in range(cap):
            picks[group * cap + at:group * cap + at + 1, :] = jnp.sum(
                jnp.where(place == at, code, 0.0), axis=0, keepdims=True
            )
    spread = jnp.dot(picks[...], together, precision=lax.Precision.HIGHEST, preferred_element_type=f32).astype(jnp.int32)
    slot = lax.broadcasted_iota(jnp.int32, (1, LANES), 1) % SLOT_PITCH
    halves = pl.cdiv(cap, SLOT_PITCH)
    lines = []
    for group in range(groups + 1):
        for half in range(halves):
            merged = jnp.zeros((1, LANES), jnp.int32)
            for at in range(half * SLOT_PITCH, min(cap, (half + 1) * SLOT_PITCH)):
                here = spread[group * cap + at:group * cap + at + 1, :]
                merged = jnp.where(slot == at % SLOT_PITCH, here, merged)
            lines.append(merged)
    lines += lines[-1:] * (codes_ref.shape[0] - len(lines))
    codes_ref[...] = jnp.concatenate(lines, axis=0)
    counts += counts[-1:] * (counts_ref.shape[0] - len(counts))
    counts_ref[...] = jnp.concatenate(counts, axis=0).astype(jnp.int32)
    copy = pltpu.make_async_copy(codes_ref, codes_smem, sem)
    copy.start()
    for away, piece_ref in enumerate(piece_refs):
        panel[(row_index + rows - away) % rows] = piece_ref[...]
    copy.wait()

    def one_peer(peer, carry):
        line = (peer // peers_per_group) * halves
        first = (peer % peers_per_group) * SLOT_PITCH
        for at in range(cap):
            found_at = codes_smem[line + at // SLOT_PITCH, first + at % SLOT_PITCH] & 511
            send_ref[peer, at] = strips_ref[found_at]
        return carry

    lax.fori_loop(0, peers, one_peer, 0)

    for away, right_ref in enumerate(right_refs):
        lane_at = (row_index + away) % rows * SLOT_PITCH
        for at in range(cap):
            name = codes_smem[groups * halves + at // SLOT_PITCH, lane_at + at % SLOT_PITCH]
            right_ref[at] = panel[name // SLOT_PITCH, name % SLOT_PITCH]


def product_body(first, rows, scalars, codes, counts, left_ref, *refs):
    right_refs, refs = refs[:rows], refs[rows:]
    if first:
        out_ref, left, right = refs
        out_ref[...] = jnp.zeros_like(out_ref)
    else:
        running_ref, out_ref, left, right = refs
        out_ref[...] = running_ref[...]
    base, own = scalars[0], scalars[1]
    row_index = lax.axis_index("row")
    peers, cap, strip, _ = left_ref.shape
    tall_strip = right_refs[0].shape[1]
    halves = pl.cdiv(cap, SLOT_PITCH)
    peers_per_group = LANES // SLOT_PITCH
    line = (own // peers_per_group) * halves
    lane = (own % peers_per_group) * SLOT_PITCH
    todo = jnp.clip(counts[own // peers_per_group, lane] - base, 0, cap)
    bf16 = jnp.bfloat16

    def multiply(at, carry):
        for peer in range(peers):
            left[peer * strip:(peer + 1) * strip, :] = left_ref[peer, at]
        for away, right_ref in enumerate(right_refs):
            start = pl.multiple_of((row_index + rows - away) % rows * tall_strip, tall_strip)
            right[pl.ds(start, tall_strip), :] = right_ref[at]
        a, b = left[...], right[...]
        a_high = a.astype(bf16)
        b_high = b.astype(bf16)
        a_low = (a - a_high.astype(jnp.float32)).astype(bf16)
        b_low = (b - b_high.astype(jnp.float32)).astype(bf16)
        product = jnp.dot(a_high, b_low, preferred_element_type=jnp.float32)
        product = product + jnp.dot(a_low, b_high, preferred_element_type=jnp.float32)
        product = product + jnp.dot(a_high, b_high, preferred_element_type=jnp.float32)
        target = codes[line + at // SLOT_PITCH, lane + at % SLOT_PITCH] >> 16
        out_ref[target] = out_ref[target] + product
        return carry

    lax.fori_loop(0, todo, multiply, 0)


def whole(shape):
    return pl.BlockSpec(shape, lambda i, *_: (0,) * len(shape))


def pack(tiles, listed, wanted, peers):
    count, order = tiles.shape[:2]
    shape = (peers, count + 1, order // peers, order)
    return pl.pallas_call(
        pack_body, out_shape=jax.ShapeDtypeStruct(shape, jnp.float32), compiler_params=LIMIT
    )(tiles, listed, wanted)


def pack_right(tiles, rows):
    count, order = tiles.shape[:2]
    shape = (count, order // rows, order)
    return pl.pallas_call(
        pack_right_body, out_shape=[jax.ShapeDtypeStruct(shape, jnp.float32)] * rows, compiler_params=LIMIT
    )(tiles)


def plan(strips, mates, pieces, row_index, base, peers, cap):
    strip, order = strips.shape[1:]
    rows = len(pieces)
    count, tall_strip, _ = pieces[0].shape
    groups = peers * SLOT_PITCH // LANES
    lines = 8 * pl.cdiv((groups + 1) * pl.cdiv(cap, SLOT_PITCH), 8)
    send, right = (peers, cap, strip, order), (cap, tall_strip, order)
    return pl.pallas_call(
        functools.partial(plan_body, rows),
        grid_spec=pltpu.PrefetchScalarGridSpec(
            num_scalar_prefetch=1,
            grid=(1,),
            in_specs=[whole(operand.shape) for operand in (strips, mates, *pieces)],
            out_specs=[whole(send)] + [whole(right)] * rows + [whole((lines, LANES)), whole((8, LANES))],
            scratch_shapes=[
                pltpu.VMEM((peers * 8, peers * 8), jnp.float32),
                pltpu.VMEM(((groups + 1) * cap, LANES), jnp.float32),
                pltpu.VMEM((rows, count, tall_strip, order), jnp.float32),
                pltpu.SMEM((lines, LANES), jnp.int32),
                pltpu.SemaphoreType.DMA,
            ],
        ),
        out_shape=[
            jax.ShapeDtypeStruct(send, jnp.float32),
            *[jax.ShapeDtypeStruct(right, jnp.float32)] * rows,
            jax.ShapeDtypeStruct((lines, LANES), jnp.int32),
            jax.ShapeDtypeStruct((8, LANES), jnp.int32),
        ],
        compiler_params=LIMIT,
    )(jnp.stack([row_index, base]), strips, mates, *pieces)


def multiply_round(left, right, codes, counts, base, own, running, kept):
    order = left.shape[-1]
    first = running is None
    tiles = (kept, order, order)
    operands = [left, *right] + ([] if first else [running])
    return pl.pallas_call(
        functools.partial(product_body, first, len(right)),
        grid_spec=pltpu.PrefetchScalarGridSpec(
            num_scalar_prefetch=3,
            grid=(1,),
            in_specs=[whole(operand.shape) for operand in operands],
            out_specs=whole(tiles),
            scratch_shapes=[pltpu.VMEM((order, order), jnp.float32)] * 2,
        ),
        out_shape=jax.ShapeDtypeStruct(tiles, jnp.float32),
        compiler_params=LIMIT,
    )(jnp.stack([base, own]), codes, counts, *operands)


def shift_all(pieces):
    rows = len(pieces)
    return [pieces[0]] + [
        lax.ppermute(pieces[by], "row", [(i, (i + by) % rows) for i in range(rows)]) for by in range(1, rows)
    ]


def swap_rows(array, rows, by):
    return lax.ppermute(array, "row", [(i, i ^ by) for i in range(rows)])


def local(tile_values, tile_rows, tile_cols, tile_counts, out_rows, out_cols):
    order = tile_values.shape[-1]
    kept = out_rows.shape[-1]
    rows = lax.axis_size("row")
    peers = lax.axis_size(GROUP)
    row_index = lax.axis_index("row")
    own = lax.axis_index(GROUP)
    tiles = tile_values.reshape(-1, order, order)

    listed, wanted = pl.pallas_call(
        label_body,
        in_specs=[pl.BlockSpec(memory_space=pltpu.SMEM)] * 5,
        out_shape=[jax.ShapeDtypeStruct((n, LANES), jnp.float32) for n in (4, 2)],
        compiler_params=LIMIT,
    )(tile_rows, tile_cols, tile_counts, out_rows, out_cols)
    for by in (1, 2, 4):
        listed = listed + swap_rows(listed, rows, by)
    pieces = shift_all(pack_right(tiles, rows))
    strips = pack(tiles, listed, wanted, peers)
    strips = lax.all_to_all(strips, GROUP, 0, 0, tiled=True)
    strips = strips.reshape(-1, order // peers, order)

    zero = jnp.zeros((), jnp.int32)
    send, *right, codes, counts = plan(strips, listed, pieces, row_index, zero, peers, ROUND_CAP)
    most = jnp.max(counts)
    for by in (1, 2, 4):
        most = jnp.maximum(most, swap_rows(most, rows, by))
    left = lax.all_to_all(send, GROUP, 0, 0, tiled=True)
    right = shift_all(right)
    summed = multiply_round(left, right, codes, counts, zero, own, None, kept)

    def unfinished(state):
        return state[0] < most

    def further(state):
        base, running = state
        send, *right, codes, counts = plan(strips, listed, pieces, row_index, base, peers, ROUND_CAP)
        left = lax.all_to_all(send, GROUP, 0, 0, tiled=True)
        right = shift_all(right)
        running = multiply_round(left, right, codes, counts, base, own, running, kept)
        return base + ROUND_CAP, running

    unused, summed = lax.while_loop(unfinished, further, (jnp.int32(ROUND_CAP), summed))
    return summed.reshape(1, 1, kept, order, order)


def solution(mesh):
    in_specs = (
        P("row", GROUP, None, None, None, None),
        P("row", GROUP, None, None),
        P("row", GROUP, None, None),
        P("row", GROUP, None),
        P("row", "col", None, None),
        P("row", "col", None, None),
    )
    out_specs = P("row", GROUP, None, None, None)
    return jax.shard_map(local, mesh=mesh, in_specs=in_specs, out_specs=out_specs, check_vma=False)
```

```python
import functools

import jax
import jax.numpy as jnp
from jax import lax
from jax.experimental import pallas as pl
from jax.experimental.pallas import tpu as pltpu
from jax.sharding import PartitionSpec as P

GROUP = ("col", "layer")
LANES = 128
SLOT_PITCH = 16
PER_GROUP = LANES // SLOT_PITCH
ROUND_CAP = 20
LIMIT = pltpu.CompilerParams(vmem_limit_bytes=20 * 2**20)
HBM = pl.BlockSpec(memory_space=pltpu.HBM)


def in_hbm(*arrays):
    return [pltpu.with_memory_space_constraint(array, pltpu.HBM) for array in arrays]


def padded(size, unit):
    return unit * pl.cdiv(size, unit)


def label_body(*refs):
    sources, listed_ref, wanted_ref, sems, copies = refs[:5], refs[5], refs[6], refs[7], refs[8:]
    moves = [pltpu.make_async_copy(a, b, sems.at[n]) for n, (a, b) in enumerate(zip(sources, copies))]
    for move in moves:
        move.start()
    for move in moves:
        move.wait()
    tile_rows, tile_cols, counts, out_rows, out_cols = copies
    lists, capacity = tile_rows.shape[2:]
    row_index, layer_index = lax.axis_index("row"), lax.axis_index("layer")
    in_group = lax.axis_index(GROUP) % PER_GROUP
    lane = lax.broadcasted_iota(jnp.int32, (1, LANES), 1)
    nothing = jnp.zeros((1, LANES), jnp.int32)
    rows, cols, kept_rows, kept_cols = nothing, nothing, nothing, nothing
    mate_rows, mate_cols = nothing, nothing
    for at in range(lists):
        for slot in range(capacity):
            live = slot < counts[0, 0, at]
            here = lane == jnp.where(live, row_index * SLOT_PITCH + at * capacity + slot, -1)
            rows = jnp.where(here, tile_rows[0, 0, at, slot] + 1, rows)
            cols = jnp.where(here, tile_cols[0, 0, at, slot] + 1, cols)
    for at in range(out_rows.shape[3]):
        target_row, target_col = out_rows[0, 0, layer_index, at] + 1, out_cols[0, 0, layer_index, at] + 1
        here = lane == in_group * SLOT_PITCH + at
        kept_rows = jnp.where(here, target_row, kept_rows)
        kept_cols = jnp.where(here, target_col, kept_cols)
        here = lane == row_index * SLOT_PITCH + at
        mate_rows = jnp.where(here, target_row, mate_rows)
        mate_cols = jnp.where(here, target_col, mate_cols)
    listed_ref[...] = jnp.concatenate([rows, cols, mate_rows, mate_cols]).astype(jnp.float32)
    wanted_ref[...] = jnp.concatenate([kept_rows, kept_cols]).astype(jnp.float32)


def label(tile_rows, tile_cols, tile_counts, out_rows, out_cols):
    operands = (tile_rows, tile_cols, tile_counts, out_rows, out_cols)
    return pl.pallas_call(
        label_body,
        in_specs=[HBM] * 5,
        out_shape=[jax.ShapeDtypeStruct((n, LANES), jnp.float32) for n in (4, 2)],
        scratch_shapes=[pltpu.SemaphoreType.DMA((5,))] + [pltpu.SMEM(x.shape, jnp.int32) for x in operands],
        compiler_params=LIMIT,
    )(*in_hbm(*operands))


def pack_body(tiles_hbm, out_ref, tiles, sems):
    peers, per_peer, strip, _ = out_ref.shape
    for tile in range(per_peer - 1):
        pltpu.make_async_copy(tiles_hbm.at[tile], tiles.at[tile], sems.at[tile]).start()

    def one_tile(tile, carry):
        pltpu.make_async_copy(tiles_hbm.at[tile], tiles.at[tile], sems.at[tile]).wait()
        for peer in range(peers):
            out_ref[peer, tile] = tiles[tile, peer * strip:(peer + 1) * strip, :]
        return carry

    lax.fori_loop(0, per_peer - 1, one_tile, 0)


def pack(tiles, peers):
    count, order = tiles.shape[:2]
    shape = (peers, count + 1, order // peers, order)
    return pl.pallas_call(
        pack_body,
        in_specs=[HBM],
        out_shape=pltpu.HBM(shape, jnp.float32),
        scratch_shapes=[pltpu.VMEM(tiles.shape, jnp.float32), pltpu.SemaphoreType.DMA((count,))],
        compiler_params=LIMIT,
    )(*in_hbm(tiles))


def stamp_body(one_ref, other_ref, wanted_ref, strips_in, strips_out, total_ref, meta, sem):
    peers, per_peer = strips_out.shape[:2]
    total = one_ref[...] + other_ref[...]
    total_ref[...] = total
    full = jnp.concatenate([total[0:2, :], wanted_ref[...]])
    for peer in range(peers):
        meta[peer] = full
    copy = pltpu.make_async_copy(meta, strips_out.at[:, per_peer - 1], sem)
    copy.start()
    copy.wait()


def stamp(one, other, wanted, strips):
    peers, _, strip, order = strips.shape
    vmem = pl.BlockSpec(memory_space=pltpu.VMEM)
    return pl.pallas_call(
        stamp_body,
        in_specs=[vmem, vmem, vmem, HBM],
        out_specs=[HBM, vmem],
        out_shape=[pltpu.HBM(strips.shape, jnp.float32), jax.ShapeDtypeStruct(one.shape, jnp.float32)],
        input_output_aliases={3: 0},
        scratch_shapes=[pltpu.VMEM((peers, strip, order), jnp.float32), pltpu.SemaphoreType.DMA],
        compiler_params=LIMIT,
    )(one, other, wanted, *in_hbm(strips))


def pack_right_body(tiles_ref, *out_refs):
    count, strip, _ = out_refs[0].shape
    row_index = lax.axis_index("row")
    for away, out_ref in enumerate(out_refs):
        start = pl.multiple_of((row_index + away) % len(out_refs) * strip, strip)
        for tile in range(count):
            out_ref[tile] = tiles_ref[tile, pl.ds(start, strip), :]


def pack_right(tiles, rows):
    count, order = tiles.shape[:2]
    shape = (count, order // rows, order)
    return pl.pallas_call(
        pack_right_body, out_shape=[jax.ShapeDtypeStruct(shape, jnp.float32)] * rows, compiler_params=LIMIT
    )(*in_hbm(tiles))


def plan_body(
    rows, base_ref, strips_ref, mates_ref,
    send_ref, codes_ref, counts_ref, peak_ref,
    table, values, keys, picks, places_vmem, send, places, sem, send_sems,
):
    row_index, base = lax.axis_index("row"), base_ref[0]
    peers, cap = send_ref.shape[:2]
    per_peer = strips_ref.shape[0] // peers
    band = 8
    blocks = peers * band
    band_rows = blocks // rows
    groups = peers // PER_GROUP
    deep = picks.shape[0] // (groups + 1)
    halves = pl.cdiv(cap, SLOT_PITCH)
    f32, bf16 = jnp.float32, jnp.bfloat16
    iota = functools.partial(lax.broadcasted_iota, jnp.int32)

    one, zero = jnp.ones((blocks, LANES), bf16), jnp.zeros((blocks, LANES), bf16)
    tall = (iota((blocks, LANES), 0) + 1).astype(f32).astype(bf16)
    in_band = iota((band_rows, LANES), 0).astype(f32)
    band_start = (iota((1, LANES), 1) // SLOT_PITCH * band_rows + 1).astype(f32)
    band_mask = jnp.where(iota((blocks, LANES), 0) // band_rows == iota((blocks, LANES), 1) // SLOT_PITCH, 1.0, 0.0)
    band_mask = band_mask.astype(bf16)
    short = iota((band, LANES), 0).astype(f32) + 1.0
    names = iota((band, LANES), 1).astype(f32) + 1.0
    targets = []
    for peer in range(peers):
        meta = strips_ref[peer * per_peer + per_peer - 1]
        row_hot = jnp.where(in_band == meta[0:1, :] - band_start, 1.0, 0.0).astype(bf16)
        row_hot = jnp.concatenate([row_hot] * rows, axis=0) * band_mask
        col_hot = jnp.where(short + float(peer * band) == meta[1:2, :], names, 0.0).astype(bf16)
        table[peer * band:(peer + 1) * band, :] = lax.dot_general(
            col_hot, row_hot, (((1,), (1,)), ((), ())), preferred_element_type=f32
        )
        if peer % PER_GROUP == 0:
            targets.append(meta)
        else:
            targets[-1] = targets[-1] + meta
    by_col = table[...]
    by_row = by_col.T.astype(bf16)
    by_col = by_col.astype(bf16)

    below = jnp.where(iota((blocks, blocks), 0) >= iota((blocks, blocks), 1), 1.0, 0.0).astype(bf16)
    lane_from, lane_to = iota((LANES, LANES), 0), iota((LANES, LANES), 1)
    same_peer = lane_from // SLOT_PITCH == lane_to // SLOT_PITCH
    earlier = jnp.where(same_peer & (lane_from < lane_to), 1.0, 0.0).astype(bf16)
    together = jnp.where(same_peer, 1.0, 0.0)
    fixed = iota((blocks, LANES), 0) // band * per_peer + ((iota((blocks, LANES), 1) % SLOT_PITCH) << 16)
    fixed = (fixed - (SLOT_PITCH * row_index + 1 + 512)).astype(f32)

    targets = [(meta[2:3, :], meta[3:4, :]) for meta in targets]
    targets.append((mates_ref[2:3, :], mates_ref[3:4, :]))
    everything = []
    for group, (target_rows, target_cols) in enumerate(targets):
        def hot(target):
            few = jnp.broadcast_to(target, (16, LANES)).astype(bf16)
            return jnp.where(tall == jnp.concatenate([few] * (blocks // 16), axis=0), one, zero)

        left = jnp.dot(by_col, hot(target_rows), preferred_element_type=f32)
        right = jnp.dot(by_row, hot(target_cols), preferred_element_type=f32)
        hit = left * right > 0.0
        ranks = jnp.dot(below, jnp.where(hit, 1.0, 0.0).astype(bf16), preferred_element_type=f32)
        everything.append(ranks[blocks - 1:blocks, :])
        keys[group * blocks:(group + 1) * blocks, :] = jnp.where(hit, ranks, 0.0)
        if group < groups:
            value = fixed + left + right * 512.0
        else:
            name = right.astype(jnp.int32) - 1
            value = (name - (SLOT_PITCH - per_peer + 1) * (name >> 4)).astype(f32)
        values[group * blocks:(group + 1) * blocks, :] = value
    found = jnp.concatenate(everything + everything[-1:] * (8 - len(everything)), axis=0)
    ahead = jnp.dot(found.astype(bf16), earlier, preferred_element_type=f32) - base.astype(f32)
    counts = jnp.dot(found.astype(bf16), together.astype(bf16), preferred_element_type=f32)
    counts_ref[...] = counts.astype(jnp.int32)
    peak_ref[...] = jnp.broadcast_to(jnp.max(jnp.max(counts[0:groups, :], axis=0, keepdims=True), axis=1, keepdims=True), (8, LANES))
    picks[...] = jnp.zeros_like(picks)
    depth = jnp.max(found).astype(jnp.int32)
    slot_at = iota((deep, LANES), 0).astype(f32)

    def one_depth(level, carry):
        level_f = level.astype(f32)
        for group in range(groups + 1):
            span = slice(group * blocks, (group + 1) * blocks)
            value = jnp.sum(jnp.where(keys[span, :] == level_f + 1.0, values[span, :], 0.0), axis=0, keepdims=True)
            place = jnp.where(found[group:group + 1, :] > level_f, ahead[group:group + 1, :] + level_f, -1.0)
            span = slice(group * deep, (group + 1) * deep)
            picks[span, :] = picks[span, :] + jnp.where(slot_at == place, value, 0.0)
        return carry

    lax.fori_loop(0, depth, one_depth, 0)
    spread = jnp.dot(picks[...], together, precision=lax.Precision.HIGHEST, preferred_element_type=f32)
    mine = iota((deep, LANES), 0) % SLOT_PITCH == iota((deep, LANES), 1) % SLOT_PITCH
    lines = []
    for group in range(groups + 1):
        chosen = jnp.where(mine, spread[group * deep:(group + 1) * deep, :], 0.0)
        for half in range(halves):
            lines.append(jnp.sum(chosen[half * SLOT_PITCH:(half + 1) * SLOT_PITCH, :], axis=0, keepdims=True))
    lines += lines[-1:] * (codes_ref.shape[0] - len(lines))
    codes = jnp.concatenate(lines, axis=0).astype(jnp.int32)
    codes_ref[...] = codes
    places_vmem[...] = codes & 511
    copy = pltpu.make_async_copy(places_vmem, places, sem)
    copy.start()
    copy.wait()

    def one_group(group):
        part = pl.ds(group * PER_GROUP, PER_GROUP)
        return pltpu.make_async_copy(send.at[part], send_ref.at[part], send_sems.at[group])

    def one_peer(peer, carry):
        line = (peer >> 3) * halves
        first = (peer & (PER_GROUP - 1)) * SLOT_PITCH
        for at in range(cap):
            send[peer, at] = strips_ref[places[line + at // SLOT_PITCH, first + at % SLOT_PITCH]]
        return carry

    for group in range(groups):
        lax.fori_loop(group * PER_GROUP, (group + 1) * PER_GROUP, one_peer, 0)
        one_group(group).start()
    for group in range(groups):
        one_group(group).wait()


def whole(shape):
    return pl.BlockSpec(shape, lambda i, *_: (0,) * len(shape))


def plan(strips, mates, base, rows, peers, cap):
    strip, order = strips.shape[1:]
    groups = peers // PER_GROUP
    lines = padded((groups + 1) * pl.cdiv(cap, SLOT_PITCH), 8)
    send = (peers, cap, strip, order)
    blocks = peers * 8
    shapes = [(send, jnp.float32), ((lines, LANES), jnp.int32), ((8, LANES), jnp.int32), ((8, LANES), jnp.float32)]
    return pl.pallas_call(
        functools.partial(plan_body, rows),
        grid_spec=pltpu.PrefetchScalarGridSpec(
            num_scalar_prefetch=1,
            grid=(1,),
            in_specs=[whole(strips.shape), whole(mates.shape)],
            out_specs=[HBM] + [whole(shape) for shape, _ in shapes[1:]],
            scratch_shapes=[
                pltpu.VMEM((blocks, blocks), jnp.float32),
                pltpu.VMEM(((groups + 1) * blocks, LANES), jnp.float32),
                pltpu.VMEM(((groups + 1) * blocks, LANES), jnp.float32),
                pltpu.VMEM(((groups + 1) * padded(cap, 8), LANES), jnp.float32),
                pltpu.VMEM((lines, LANES), jnp.int32),
                pltpu.VMEM(send, jnp.float32),
                pltpu.SMEM((lines, LANES), jnp.int32),
                pltpu.SemaphoreType.DMA,
                pltpu.SemaphoreType.DMA((groups,)),
            ],
        ),
        out_shape=[pltpu.HBM(*shapes[0])] + [jax.ShapeDtypeStruct(*shape) for shape in shapes[1:]],
        compiler_params=LIMIT,
    )(base.reshape(1), pltpu.with_memory_space_constraint(strips, pltpu.VMEM), mates)


def collect_body(rows, first_line, codes, peak_ref, *refs):
    piece_refs, right_refs, panel = refs[:rows], refs[rows:2 * rows], refs[2 * rows]
    row_index = lax.axis_index("row")
    count, strip, _ = piece_refs[0].shape
    cap = right_refs[0].shape[0] - 1
    for away, piece_ref in enumerate(piece_refs):
        start = (row_index + rows - away) % rows * count
        for tile in range(count):
            panel[start + tile] = piece_ref[tile]
    for away, right_ref in enumerate(right_refs):
        lane = (row_index + away) % rows * SLOT_PITCH
        for at in range(cap):
            right_ref[at] = panel[codes[first_line + at // SLOT_PITCH, lane + at % SLOT_PITCH]]
        right_ref[cap, 0:8, :] = peak_ref[...]
        right_ref[cap, 8:16, :] = peak_ref[...]


def collect(codes, peak, pieces, peers, cap):
    rows = len(pieces)
    count, strip, order = pieces[0].shape
    right = (cap + 1, strip, order)
    return pl.pallas_call(
        functools.partial(collect_body, rows, peers // PER_GROUP * pl.cdiv(cap, SLOT_PITCH)),
        grid_spec=pltpu.PrefetchScalarGridSpec(
            num_scalar_prefetch=1,
            grid=(1,),
            in_specs=[whole(operand.shape) for operand in (peak, *pieces)],
            out_specs=[whole(right)] * rows,
            scratch_shapes=[pltpu.VMEM((rows * count, strip, order), jnp.float32)],
        ),
        out_shape=[jax.ShapeDtypeStruct(right, jnp.float32)] * rows,
        compiler_params=LIMIT,
    )(codes, peak, *in_hbm(*pieces))


def product_body(first, rows, base_ref, codes, counts, left_ref, *refs):
    right_refs, refs = refs[:rows], refs[rows:]
    if first:
        out_ref, most_ref, left, right = refs
        out_ref[...] = jnp.zeros_like(out_ref)
    else:
        running_ref, out_ref, most_ref, left, right = refs
        out_ref[...] = running_ref[...]
    row_index, own, base = lax.axis_index("row"), lax.axis_index(GROUP), base_ref[0]
    peers, cap, strip, order = left_ref.shape
    tall_strip = right_refs[0].shape[1]
    line = (own >> 3) * pl.cdiv(cap, SLOT_PITCH)
    lane = (own & (PER_GROUP - 1)) * SLOT_PITCH
    todo = jnp.clip(counts[own >> 3, lane] - base, 0, cap)
    most = right_refs[0][cap, 0:8, :]
    for right_ref in right_refs[1:]:
        most = jnp.maximum(most, right_ref[cap, 0:8, :])
    most_ref[...] = most.astype(jnp.int32)
    bf16 = jnp.bfloat16

    def product(at, half):
        for peer in range(peers):
            left[half, peer * strip:(peer + 1) * strip, :] = left_ref[peer, at]
        for away, right_ref in enumerate(right_refs):
            start = pl.multiple_of((row_index + rows - away) % rows * tall_strip, tall_strip)
            right[half, pl.ds(start, tall_strip), :] = right_ref[at]
        a, b = left[half], right[half]
        a_high, b_high = a.astype(bf16), b.astype(bf16)
        a_low = (a - a_high.astype(jnp.float32)).astype(bf16)
        b_low = (b - b_high.astype(jnp.float32)).astype(bf16)
        both = jnp.concatenate([b_high, b_low], axis=1)
        sums = jnp.dot(
            jnp.concatenate([a_high, a_low], axis=1),
            jnp.concatenate([both, both], axis=0),
            preferred_element_type=jnp.float32,
        )
        return sums[:, :order] + sums[:, order:]

    def target(at):
        return codes[line + (at >> 4), lane + (at & (SLOT_PITCH - 1))] >> 16

    def two(pair, carry):
        at = 2 * pair
        one, other = product(at, 0), product(at + 1, 1)
        out_ref[target(at)] += one

        @pl.when(at + 1 < todo)
        def _():
            out_ref[target(at + 1)] += other

        return carry

    lax.fori_loop(0, (todo + 1) >> 1, two, 0)


def multiply_round(left, right, codes, counts, base, running, kept):
    order = left.shape[-1]
    first = running is None
    tiles = (kept, order, order)
    operands = [pltpu.with_memory_space_constraint(left, pltpu.VMEM), *right] + ([] if first else [running])
    return pl.pallas_call(
        functools.partial(product_body, first, len(right)),
        grid_spec=pltpu.PrefetchScalarGridSpec(
            num_scalar_prefetch=3,
            grid=(1,),
            in_specs=[whole(operand.shape) for operand in operands],
            out_specs=[whole(tiles), whole((8, LANES))],
            scratch_shapes=[pltpu.VMEM((2, order, order), jnp.float32)] * 2,
        ),
        out_shape=[jax.ShapeDtypeStruct(tiles, jnp.float32), jax.ShapeDtypeStruct((8, LANES), jnp.int32)],
        compiler_params=LIMIT,
    )(base.reshape(1), codes, counts, *operands)


def shift_all(pieces):
    rows = len(pieces)
    return [pieces[0]] + [
        lax.ppermute(pieces[by], "row", [(i, (i + by) % rows) for i in range(rows)]) for by in range(1, rows)
    ]


def swap_rows(array, rows, by):
    return lax.ppermute(array, "row", [(i, i ^ by) for i in range(rows)])


def local(tile_values, tile_rows, tile_cols, tile_counts, out_rows, out_cols):
    order = tile_values.shape[-1]
    kept = out_rows.shape[-1]
    rows = lax.axis_size("row")
    peers = lax.axis_size(GROUP)
    tiles = tile_values.reshape(-1, order, order)

    listed, wanted = label(tile_rows, tile_cols, tile_counts, out_rows, out_cols)
    for by in (1, 2):
        listed = listed + swap_rows(listed, rows, by)
    strips, mates = stamp(listed, swap_rows(listed, rows, 4), wanted, pack(tiles, peers))
    pieces = shift_all(pack_right(tiles, rows))
    strips = lax.all_to_all(strips, GROUP, 0, 0, tiled=True)
    strips, pieces = lax.optimization_barrier((strips, pieces))
    strips = strips.reshape(-1, order // peers, order)

    def one_round(base, running):
        send, codes, counts, peak = plan(strips, mates, base, rows, peers, ROUND_CAP)
        left = lax.all_to_all(send, GROUP, 0, 0, tiled=True)
        right = shift_all(collect(codes, peak, pieces, peers, ROUND_CAP))
        return multiply_round(left, right, codes, counts, base, running, kept)

    summed, most = one_round(jnp.zeros((), jnp.int32), None)

    def unfinished(state):
        return state[0] < most[0, 0]

    def further(state):
        return state[0] + ROUND_CAP, one_round(*state)[0]

    unused, summed = lax.while_loop(unfinished, further, (jnp.int32(ROUND_CAP), summed))
    return summed.reshape(1, 1, kept, order, order)


def solution(mesh):
    in_specs = (
        P("row", GROUP, None, None, None, None),
        P("row", GROUP, None, None),
        P("row", GROUP, None, None),
        P("row", GROUP, None),
        P("row", "col", None, None),
        P("row", "col", None, None),
    )
    out_specs = P("row", GROUP, None, None, None)
    return jax.shard_map(local, mesh=mesh, in_specs=in_specs, out_specs=out_specs, check_vma=False)
```

```python
import functools

import jax
import jax.numpy as jnp
from jax import lax
from jax.experimental import pallas as pl
from jax.experimental.pallas import tpu as pltpu
from jax.sharding import PartitionSpec as P

GROUP = ("col", "layer")
LANES = 128
SLOT_PITCH = 16
PER_GROUP = LANES // SLOT_PITCH
ROUND_CAP = 20
LIMIT = pltpu.CompilerParams(vmem_limit_bytes=20 * 2**20)
HBM = pl.BlockSpec(memory_space=pltpu.HBM)


NEAR, FAR = 4, 8


def away_from(peer, near, far):
    x = (((peer >> 1) & 3) + NEAR - near) & 3
    z = (((peer >> 3) * 2 + (peer & 1)) + FAR - far) & 7
    return ((z >> 1) << 3) + (x << 1) + (z & 1)


def in_hbm(*arrays):
    return [pltpu.with_memory_space_constraint(array, pltpu.HBM) for array in arrays]


def padded(size, unit):
    return unit * pl.cdiv(size, unit)


def label_body(*refs):
    sources, listed_ref, wanted_ref, sems, copies = refs[:5], refs[5], refs[6], refs[7], refs[8:]
    moves = [pltpu.make_async_copy(a, b, sems.at[n]) for n, (a, b) in enumerate(zip(sources, copies))]
    for move in moves:
        move.start()
    for move in moves:
        move.wait()
    tile_rows, tile_cols, counts, out_rows, out_cols = copies
    lists, capacity = tile_rows.shape[2:]
    row_index, layer_index = lax.axis_index("row"), lax.axis_index("layer")
    in_group = lax.axis_index(GROUP) % PER_GROUP
    lane = lax.broadcasted_iota(jnp.int32, (1, LANES), 1)
    nothing = jnp.zeros((1, LANES), jnp.int32)
    rows, cols, kept_rows, kept_cols = nothing, nothing, nothing, nothing
    mate_rows, mate_cols = nothing, nothing
    for at in range(lists):
        for slot in range(capacity):
            live = slot < counts[0, 0, at]
            here = lane == jnp.where(live, row_index * SLOT_PITCH + at * capacity + slot, -1)
            rows = jnp.where(here, tile_rows[0, 0, at, slot] + 1, rows)
            cols = jnp.where(here, tile_cols[0, 0, at, slot] + 1, cols)
    for at in range(out_rows.shape[3]):
        target_row, target_col = out_rows[0, 0, layer_index, at] + 1, out_cols[0, 0, layer_index, at] + 1
        here = lane == in_group * SLOT_PITCH + at
        kept_rows = jnp.where(here, target_row, kept_rows)
        kept_cols = jnp.where(here, target_col, kept_cols)
        here = lane == row_index * SLOT_PITCH + at
        mate_rows = jnp.where(here, target_row, mate_rows)
        mate_cols = jnp.where(here, target_col, mate_cols)
    listed_ref[...] = jnp.concatenate([rows, cols, mate_rows, mate_cols]).astype(jnp.float32)
    wanted_ref[...] = jnp.concatenate([kept_rows, kept_cols]).astype(jnp.float32)


def label(tile_rows, tile_cols, tile_counts, out_rows, out_cols):
    operands = (tile_rows, tile_cols, tile_counts, out_rows, out_cols)
    return pl.pallas_call(
        label_body,
        in_specs=[HBM] * 5,
        out_shape=[jax.ShapeDtypeStruct((n, LANES), jnp.float32) for n in (4, 2)],
        scratch_shapes=[pltpu.SemaphoreType.DMA((5,))] + [pltpu.SMEM(x.shape, jnp.int32) for x in operands],
        compiler_params=LIMIT,
    )(*in_hbm(*operands))


def pack_body(tiles_hbm, out_ref, tiles, sems):
    peers, per_peer, strip, _ = out_ref.shape
    for tile in range(per_peer):
        pltpu.make_async_copy(tiles_hbm.at[tile], tiles.at[tile], sems.at[tile]).start()

    def one_tile(tile, carry):
        pltpu.make_async_copy(tiles_hbm.at[tile], tiles.at[tile], sems.at[tile]).wait()
        for peer in range(peers):
            out_ref[peer, tile] = tiles[tile, peer * strip:(peer + 1) * strip, :]
        return carry

    lax.fori_loop(0, per_peer, one_tile, 0)


def pack(tiles, peers):
    count, order = tiles.shape[:2]
    shape = (peers, count, order // peers, order)
    return pl.pallas_call(
        pack_body,
        in_specs=[HBM],
        out_shape=pltpu.HBM(shape, jnp.float32),
        scratch_shapes=[pltpu.VMEM(tiles.shape, jnp.float32), pltpu.SemaphoreType.DMA((count,))],
        compiler_params=LIMIT,
    )(*in_hbm(tiles))


def merge_body(*refs):
    listed_refs, wanted_ref, meta_ref, mates_ref = refs[:-3], *refs[-3:]
    total = listed_refs[0][...]
    for listed_ref in listed_refs[1:]:
        total = total + listed_ref[...]
    meta_ref[0:2, :] = total[0:2, :]
    meta_ref[2:4, :] = wanted_ref[...]
    mates_ref[...] = total[2:4, :]


def merge(listed, wanted):
    return pl.pallas_call(
        merge_body,
        out_shape=[jax.ShapeDtypeStruct((n, LANES), jnp.float32) for n in (4, 2)],
        compiler_params=LIMIT,
    )(*listed, wanted)


def pack_right_body(tiles_ref, *out_refs):
    count, strip, _ = out_refs[0].shape
    row_index = lax.axis_index("row")
    for away, out_ref in enumerate(out_refs):
        start = pl.multiple_of((row_index + away) % len(out_refs) * strip, strip)
        for tile in range(count):
            out_ref[tile] = tiles_ref[tile, pl.ds(start, strip), :]


def pack_right(tiles, rows):
    count, order = tiles.shape[:2]
    shape = (count, order // rows, order)
    return pl.pallas_call(
        pack_right_body, out_shape=[jax.ShapeDtypeStruct(shape, jnp.float32)] * rows, compiler_params=LIMIT
    )(*in_hbm(tiles))


def plan_body(rows, peers, per_peer, cap, base_ref, *refs):
    meta_refs, mates_ref = refs[:FAR], refs[FAR]
    codes_ref, places_ref, counts_ref, peak_ref, table, wanted, values, keys, picks = refs[FAR + 1:]
    row_index, own, base = lax.axis_index("row"), lax.axis_index(GROUP), base_ref[0]
    band = 8
    blocks = peers * band
    band_rows = blocks // rows
    groups = peers // PER_GROUP
    deep = picks.shape[0] // (groups + 1)
    halves = pl.cdiv(cap, SLOT_PITCH)
    f32, bf16 = jnp.float32, jnp.bfloat16
    iota = functools.partial(lax.broadcasted_iota, jnp.int32)

    one, zero = jnp.ones((blocks, LANES), bf16), jnp.zeros((blocks, LANES), bf16)
    tall = (iota((blocks, LANES), 0) + 1).astype(f32).astype(bf16)
    in_band = iota((band_rows, LANES), 0).astype(f32)
    band_start = (iota((1, LANES), 1) // SLOT_PITCH * band_rows + 1).astype(f32)
    band_mask = jnp.where(iota((blocks, LANES), 0) // band_rows == iota((blocks, LANES), 1) // SLOT_PITCH, 1.0, 0.0)
    band_mask = band_mask.astype(bf16)
    short = iota((band, LANES), 0).astype(f32) + 1.0
    names = iota((band, LANES), 1).astype(f32) + 1.0
    wanted[...] = jnp.zeros_like(wanted)
    for far in range(FAR):
        for near in range(NEAR):
            peer = away_from(own, near, far)
            meta = meta_refs[far][near]
            row_hot = jnp.where(in_band == meta[0:1, :] - band_start, 1.0, 0.0).astype(bf16)
            row_hot = jnp.concatenate([row_hot] * rows, axis=0) * band_mask
            col_hot = jnp.where(short + (peer * band).astype(f32) == meta[1:2, :], names, 0.0).astype(bf16)
            table[pl.ds(pl.multiple_of(peer * band, band), band), :] = lax.dot_general(
                col_hot, row_hot, (((1,), (1,)), ((), ())), preferred_element_type=f32
            )
            wanted[peer >> 3] = wanted[peer >> 3] + meta
    by_col = table[...]
    by_row = by_col.T.astype(bf16)
    by_col = by_col.astype(bf16)

    below = jnp.where(iota((blocks, blocks), 0) >= iota((blocks, blocks), 1), 1.0, 0.0).astype(bf16)
    lane_from, lane_to = iota((LANES, LANES), 0), iota((LANES, LANES), 1)
    same_peer = lane_from // SLOT_PITCH == lane_to // SLOT_PITCH
    earlier = jnp.where(same_peer & (lane_from < lane_to), 1.0, 0.0).astype(bf16)
    together = jnp.where(same_peer, 1.0, 0.0)
    fixed = iota((blocks, LANES), 0) // band * per_peer + ((iota((blocks, LANES), 1) % SLOT_PITCH) << 16)
    fixed = (fixed - (SLOT_PITCH * row_index + 1 + 512)).astype(f32)

    targets = [(wanted[group, 2:3, :], wanted[group, 3:4, :]) for group in range(groups)]
    targets.append((mates_ref[0:1, :], mates_ref[1:2, :]))
    everything = []
    for group, (target_rows, target_cols) in enumerate(targets):
        def hot(target):
            few = jnp.broadcast_to(target, (16, LANES)).astype(bf16)
            return jnp.where(tall == jnp.concatenate([few] * (blocks // 16), axis=0), one, zero)

        left = jnp.dot(by_col, hot(target_rows), preferred_element_type=f32)
        right = jnp.dot(by_row, hot(target_cols), preferred_element_type=f32)
        hit = left * right > 0.0
        ranks = jnp.dot(below, jnp.where(hit, 1.0, 0.0).astype(bf16), preferred_element_type=f32)
        everything.append(ranks[blocks - 1:blocks, :])
        keys[group * blocks:(group + 1) * blocks, :] = jnp.where(hit, ranks, 0.0)
        if group < groups:
            value = fixed + left + right * 512.0
        else:
            name = right.astype(jnp.int32) - 1
            value = (name - (SLOT_PITCH - per_peer) * (name >> 4)).astype(f32)
        values[group * blocks:(group + 1) * blocks, :] = value
    found = jnp.concatenate(everything + everything[-1:] * (8 - len(everything)), axis=0)
    ahead = jnp.dot(found.astype(bf16), earlier, preferred_element_type=f32) - base.astype(f32)
    counts = jnp.dot(found.astype(bf16), together.astype(bf16), preferred_element_type=f32)
    counts_ref[...] = counts.astype(jnp.int32)
    peak_ref[...] = jnp.broadcast_to(jnp.max(jnp.max(counts[0:groups, :], axis=0, keepdims=True), axis=1, keepdims=True), (8, LANES))
    picks[...] = jnp.zeros_like(picks)
    depth = jnp.max(found).astype(jnp.int32)
    slot_at = iota((deep, LANES), 0).astype(f32)

    def one_depth(level, carry):
        level_f = level.astype(f32)
        for group in range(groups + 1):
            span = slice(group * blocks, (group + 1) * blocks)
            value = jnp.sum(jnp.where(keys[span, :] == level_f + 1.0, values[span, :], 0.0), axis=0, keepdims=True)
            place = jnp.where(found[group:group + 1, :] > level_f, ahead[group:group + 1, :] + level_f, -1.0)
            span = slice(group * deep, (group + 1) * deep)
            picks[span, :] = picks[span, :] + jnp.where(slot_at == place, value, 0.0)
        return carry

    lax.fori_loop(0, depth, one_depth, 0)
    spread = jnp.dot(picks[...], together, precision=lax.Precision.HIGHEST, preferred_element_type=f32)
    mine = iota((deep, LANES), 0) % SLOT_PITCH == iota((deep, LANES), 1) % SLOT_PITCH
    lines = []
    for group in range(groups + 1):
        chosen = jnp.where(mine, spread[group * deep:(group + 1) * deep, :], 0.0)
        for half in range(halves):
            lines.append(jnp.sum(chosen[half * SLOT_PITCH:(half + 1) * SLOT_PITCH, :], axis=0, keepdims=True))
    lines += lines[-1:] * (codes_ref.shape[0] - len(lines))
    codes = jnp.concatenate(lines, axis=0).astype(jnp.int32)
    codes_ref[...] = codes
    places_ref[...] = codes & 511


def send_body(places, strips_ref, send_ref, send, sems):
    peers, cap = send.shape[:2]
    groups = peers // PER_GROUP
    halves = pl.cdiv(cap, SLOT_PITCH)

    def one_group(group):
        part = pl.ds(group * PER_GROUP, PER_GROUP)
        return pltpu.make_async_copy(send.at[part], send_ref.at[part], sems.at[group])

    def one_peer(peer, carry):
        line = (peer >> 3) * halves
        first = (peer & (PER_GROUP - 1)) * SLOT_PITCH
        for at in range(cap):
            send[peer, at] = strips_ref[places[line + at // SLOT_PITCH, first + at % SLOT_PITCH]]
        return carry

    for group in range(groups):
        lax.fori_loop(group * PER_GROUP, (group + 1) * PER_GROUP, one_peer, 0)
        one_group(group).start()
    for group in range(groups):
        one_group(group).wait()


def whole(shape):
    return pl.BlockSpec(shape, lambda i, *_: (0,) * len(shape))


def plan(metas, mates, base, rows, peers, per_peer, cap):
    groups = peers // PER_GROUP
    lines = padded((groups + 1) * pl.cdiv(cap, SLOT_PITCH), 8)
    blocks = peers * 8
    shapes = [((lines, LANES), jnp.int32)] * 2 + [((8, LANES), jnp.int32), ((8, LANES), jnp.float32)]
    return pl.pallas_call(
        functools.partial(plan_body, rows, peers, per_peer, cap),
        grid_spec=pltpu.PrefetchScalarGridSpec(
            num_scalar_prefetch=1,
            grid=(1,),
            in_specs=[whole(operand.shape) for operand in (*metas, mates)],
            out_specs=[whole(shape) for shape, _ in shapes],
            scratch_shapes=[
                pltpu.VMEM((blocks, blocks), jnp.float32),
                pltpu.VMEM((groups, 4, LANES), jnp.float32),
                pltpu.VMEM(((groups + 1) * blocks, LANES), jnp.float32),
                pltpu.VMEM(((groups + 1) * blocks, LANES), jnp.float32),
                pltpu.VMEM(((groups + 1) * padded(cap, 8), LANES), jnp.float32),
            ],
        ),
        out_shape=[jax.ShapeDtypeStruct(*shape) for shape in shapes],
        compiler_params=LIMIT,
    )(base.reshape(1), *metas, mates)


def send_strips(places, strips, peers, cap):
    strip, order = strips.shape[1:]
    send = (peers, cap, strip, order)
    return pl.pallas_call(
        send_body,
        grid_spec=pltpu.PrefetchScalarGridSpec(
            num_scalar_prefetch=1,
            grid=(1,),
            in_specs=[whole(strips.shape)],
            out_specs=HBM,
            scratch_shapes=[pltpu.VMEM(send, jnp.float32), pltpu.SemaphoreType.DMA((peers // PER_GROUP,))],
        ),
        out_shape=pltpu.HBM(send, jnp.float32),
        compiler_params=LIMIT,
    )(places, pltpu.with_memory_space_constraint(strips, pltpu.VMEM))


def collect_body(rows, first_line, codes, peak_ref, *refs):
    piece_refs, right_refs, panel = refs[:rows], refs[rows:2 * rows], refs[2 * rows]
    row_index = lax.axis_index("row")
    count, strip, _ = piece_refs[0].shape
    cap = right_refs[0].shape[0] - 1
    for away, piece_ref in enumerate(piece_refs):
        start = (row_index + rows - away) % rows * count
        for tile in range(count):
            panel[start + tile] = piece_ref[tile]
    for away, right_ref in enumerate(right_refs):
        lane = (row_index + away) % rows * SLOT_PITCH
        for at in range(cap):
            right_ref[at] = panel[codes[first_line + at // SLOT_PITCH, lane + at % SLOT_PITCH]]
        right_ref[cap, 0:8, :] = peak_ref[...]
        right_ref[cap, 8:16, :] = peak_ref[...]


def collect(codes, peak, pieces, peers, cap):
    rows = len(pieces)
    count, strip, order = pieces[0].shape
    right = (cap + 1, strip, order)
    return pl.pallas_call(
        functools.partial(collect_body, rows, peers // PER_GROUP * pl.cdiv(cap, SLOT_PITCH)),
        grid_spec=pltpu.PrefetchScalarGridSpec(
            num_scalar_prefetch=1,
            grid=(1,),
            in_specs=[whole(operand.shape) for operand in (peak, *pieces)],
            out_specs=[whole(right)] * rows,
            scratch_shapes=[pltpu.VMEM((rows * count, strip, order), jnp.float32)],
        ),
        out_shape=[jax.ShapeDtypeStruct(right, jnp.float32)] * rows,
        compiler_params=LIMIT,
    )(codes, peak, *in_hbm(*pieces))


def product_body(first, rows, base_ref, codes, counts, left_ref, *refs):
    right_refs, refs = refs[:rows], refs[rows:]
    if first:
        out_ref, most_ref, left, right = refs
        out_ref[...] = jnp.zeros_like(out_ref)
    else:
        running_ref, out_ref, most_ref, left, right = refs
        out_ref[...] = running_ref[...]
    row_index, own, base = lax.axis_index("row"), lax.axis_index(GROUP), base_ref[0]
    peers, cap, strip, order = left_ref.shape
    tall_strip = right_refs[0].shape[1]
    line = (own >> 3) * pl.cdiv(cap, SLOT_PITCH)
    lane = (own & (PER_GROUP - 1)) * SLOT_PITCH
    todo = jnp.clip(counts[own >> 3, lane] - base, 0, cap)
    most = right_refs[0][cap, 0:8, :]
    for right_ref in right_refs[1:]:
        most = jnp.maximum(most, right_ref[cap, 0:8, :])
    most_ref[...] = most.astype(jnp.int32)
    bf16 = jnp.bfloat16

    def product(at, half):
        for peer in range(peers):
            left[half, peer * strip:(peer + 1) * strip, :] = left_ref[peer, at]
        for away, right_ref in enumerate(right_refs):
            start = pl.multiple_of((row_index + rows - away) % rows * tall_strip, tall_strip)
            right[half, pl.ds(start, tall_strip), :] = right_ref[at]
        a, b = left[half], right[half]
        a_high, b_high = a.astype(bf16), b.astype(bf16)
        a_low = (a - a_high.astype(jnp.float32)).astype(bf16)
        b_low = (b - b_high.astype(jnp.float32)).astype(bf16)
        both = jnp.concatenate([b_high, b_low], axis=1)
        sums = jnp.dot(
            jnp.concatenate([a_high, a_low], axis=1),
            jnp.concatenate([both, both], axis=0),
            preferred_element_type=jnp.float32,
        )
        return sums[:, :order] + sums[:, order:]

    def target(at):
        return codes[line + (at >> 4), lane + (at & (SLOT_PITCH - 1))] >> 16

    def two(pair, carry):
        at = 2 * pair
        one, other = product(at, 0), product(at + 1, 1)
        out_ref[target(at)] += one

        @pl.when(at + 1 < todo)
        def _():
            out_ref[target(at + 1)] += other

        return carry

    lax.fori_loop(0, (todo + 1) >> 1, two, 0)


def multiply_round(left, right, codes, counts, base, running, kept):
    order = left.shape[-1]
    first = running is None
    tiles = (kept, order, order)
    operands = [pltpu.with_memory_space_constraint(left, pltpu.VMEM), *right] + ([] if first else [running])
    return pl.pallas_call(
        functools.partial(product_body, first, len(right)),
        grid_spec=pltpu.PrefetchScalarGridSpec(
            num_scalar_prefetch=3,
            grid=(1,),
            in_specs=[whole(operand.shape) for operand in operands],
            out_specs=[whole(tiles), whole((8, LANES))],
            scratch_shapes=[pltpu.VMEM((2, order, order), jnp.float32)] * 2,
        ),
        out_shape=[jax.ShapeDtypeStruct(tiles, jnp.float32), jax.ShapeDtypeStruct((8, LANES), jnp.int32)],
        compiler_params=LIMIT,
    )(base.reshape(1), codes, counts, *operands)


def shift_all(pieces):
    rows = len(pieces)
    return [pieces[0]] + [
        lax.ppermute(pieces[by], "row", [(i, (i + by) % rows) for i in range(rows)]) for by in range(1, rows)
    ]


def from_peers(array, near, far, peers):
    pairs = [(away_from(peer, near, far), peer) for peer in range(peers)]
    return array if near + far == 0 else lax.ppermute(array, GROUP, pairs)


def swap_rows(array, rows, by):
    return lax.ppermute(array, "row", [(i, i ^ by) for i in range(rows)])


def local(tile_values, tile_rows, tile_cols, tile_counts, out_rows, out_cols):
    order = tile_values.shape[-1]
    kept = out_rows.shape[-1]
    rows = lax.axis_size("row")
    peers = lax.axis_size(GROUP)
    tiles = tile_values.reshape(-1, order, order)

    listed, wanted = label(tile_rows, tile_cols, tile_counts, out_rows, out_cols)
    listed = listed + swap_rows(listed, rows, 1)
    listed = [listed] + [lax.ppermute(listed, "row", [(i, (i + by) % rows) for i in range(rows)]) for by in (2, 4, 6)]
    meta, mates = merge(listed, wanted)
    metas = jnp.stack([from_peers(meta, near, 0, peers) for near in range(NEAR)])
    metas = [from_peers(metas, 0, far, peers) for far in range(FAR)]
    strips = lax.all_to_all(pack(tiles, peers), GROUP, 0, 0, tiled=True)
    per_peer = strips.shape[1]
    strips = strips.reshape(-1, order // peers, order)
    pieces = shift_all(pack_right(tiles, rows))

    def one_round(base, running):
        codes, places, counts, peak = plan(metas, mates, base, rows, peers, per_peer, ROUND_CAP)
        send = send_strips(places, strips, peers, ROUND_CAP)
        left = lax.all_to_all(send, GROUP, 0, 0, tiled=True)
        right = shift_all(collect(codes, peak, pieces, peers, ROUND_CAP))
        return multiply_round(left, right, codes, counts, base, running, kept)

    summed, most = one_round(jnp.zeros((), jnp.int32), None)

    def unfinished(state):
        return state[0] < most[0, 0]

    def further(state):
        return state[0] + ROUND_CAP, one_round(*state)[0]

    unused, summed = lax.while_loop(unfinished, further, (jnp.int32(ROUND_CAP), summed))
    return summed.reshape(1, 1, kept, order, order)


def solution(mesh):
    in_specs = (
        P("row", GROUP, None, None, None, None),
        P("row", GROUP, None, None),
        P("row", GROUP, None, None),
        P("row", GROUP, None),
        P("row", "col", None, None),
        P("row", "col", None, None),
    )
    out_specs = P("row", GROUP, None, None, None)
    return jax.shard_map(local, mesh=mesh, in_specs=in_specs, out_specs=out_specs, check_vma=False)
```

```python
import functools

import jax
import jax.numpy as jnp
from jax import lax
from jax.experimental import pallas as pl
from jax.experimental.pallas import tpu as pltpu
from jax.sharding import PartitionSpec as P

GROUP = ("col", "layer")
LANES = 128
SLOT_PITCH = 16
PER_GROUP = LANES // SLOT_PITCH
ROUND_CAP = 20
TOGETHER = 2
LIMIT = pltpu.CompilerParams(vmem_limit_bytes=20 * 2**20)
HBM = pl.BlockSpec(memory_space=pltpu.HBM)


def in_hbm(*arrays):
    return [pltpu.with_memory_space_constraint(array, pltpu.HBM) for array in arrays]


def padded(size, unit):
    return unit * pl.cdiv(size, unit)


def label_body(*refs):
    sources, listed_ref, wanted_ref, sems, copies = refs[:5], refs[5], refs[6], refs[7], refs[8:]
    moves = [pltpu.make_async_copy(a, b, sems.at[n]) for n, (a, b) in enumerate(zip(sources, copies))]
    for move in moves:
        move.start()
    for move in moves:
        move.wait()
    tile_rows, tile_cols, counts, out_rows, out_cols = copies
    lists, capacity = tile_rows.shape[2:]
    row_index, layer_index = lax.axis_index("row"), lax.axis_index("layer")
    in_group = lax.axis_index(GROUP) % PER_GROUP
    lane = lax.broadcasted_iota(jnp.int32, (1, LANES), 1)
    nothing = jnp.zeros((1, LANES), jnp.int32)
    rows, cols, kept_rows, kept_cols = nothing, nothing, nothing, nothing
    mate_rows, mate_cols = nothing, nothing
    for at in range(lists):
        for slot in range(capacity):
            live = slot < counts[0, 0, at]
            here = lane == jnp.where(live, row_index * SLOT_PITCH + at * capacity + slot, -1)
            rows = jnp.where(here, tile_rows[0, 0, at, slot] + 1, rows)
            cols = jnp.where(here, tile_cols[0, 0, at, slot] + 1, cols)
    for at in range(out_rows.shape[3]):
        target_row, target_col = out_rows[0, 0, layer_index, at] + 1, out_cols[0, 0, layer_index, at] + 1
        here = lane == in_group * SLOT_PITCH + at
        kept_rows = jnp.where(here, target_row, kept_rows)
        kept_cols = jnp.where(here, target_col, kept_cols)
        here = lane == row_index * SLOT_PITCH + at
        mate_rows = jnp.where(here, target_row, mate_rows)
        mate_cols = jnp.where(here, target_col, mate_cols)
    listed_ref[...] = jnp.concatenate([rows, cols, mate_rows, mate_cols]).astype(jnp.float32)
    wanted_ref[...] = jnp.concatenate([kept_rows, kept_cols]).astype(jnp.float32)


def label(tile_rows, tile_cols, tile_counts, out_rows, out_cols):
    operands = (tile_rows, tile_cols, tile_counts, out_rows, out_cols)
    return pl.pallas_call(
        label_body,
        in_specs=[HBM] * 5,
        out_shape=[jax.ShapeDtypeStruct((n, LANES), jnp.float32) for n in (4, 2)],
        scratch_shapes=[pltpu.SemaphoreType.DMA((5,))] + [pltpu.SMEM(x.shape, jnp.int32) for x in operands],
        compiler_params=LIMIT,
    )(*in_hbm(*operands))


def pack_body(tiles_hbm, out_ref, tiles, sems):
    peers, per_peer, strip, _ = out_ref.shape
    for tile in range(per_peer - 1):
        pltpu.make_async_copy(tiles_hbm.at[tile], tiles.at[tile], sems.at[tile]).start()

    def one_tile(tile, carry):
        pltpu.make_async_copy(tiles_hbm.at[tile], tiles.at[tile], sems.at[tile]).wait()
        for peer in range(peers):
            out_ref[peer, tile] = tiles[tile, peer * strip:(peer + 1) * strip, :]
        return carry

    lax.fori_loop(0, per_peer - 1, one_tile, 0)


def pack(tiles, peers):
    count, order = tiles.shape[:2]
    shape = (peers, count + 1, order // peers, order)
    return pl.pallas_call(
        pack_body,
        in_specs=[HBM],
        out_shape=pltpu.HBM(shape, jnp.float32),
        scratch_shapes=[pltpu.VMEM(tiles.shape, jnp.float32), pltpu.SemaphoreType.DMA((count,))],
        compiler_params=LIMIT,
    )(*in_hbm(tiles))


def stamp_body(one_ref, other_ref, wanted_ref, strips_in, strips_out, total_ref, meta, sem):
    peers, per_peer = strips_out.shape[:2]
    total = one_ref[...] + other_ref[...]
    total_ref[...] = total
    full = jnp.concatenate([total[0:2, :], wanted_ref[...]])
    for peer in range(peers):
        meta[peer] = full
    copy = pltpu.make_async_copy(meta, strips_out.at[:, per_peer - 1], sem)
    copy.start()
    copy.wait()


def stamp(one, other, wanted, strips):
    peers, _, strip, order = strips.shape
    vmem = pl.BlockSpec(memory_space=pltpu.VMEM)
    return pl.pallas_call(
        stamp_body,
        in_specs=[vmem, vmem, vmem, HBM],
        out_specs=[HBM, vmem],
        out_shape=[pltpu.HBM(strips.shape, jnp.float32), jax.ShapeDtypeStruct(one.shape, jnp.float32)],
        input_output_aliases={3: 0},
        scratch_shapes=[pltpu.VMEM((peers, strip, order), jnp.float32), pltpu.SemaphoreType.DMA],
        compiler_params=LIMIT,
    )(one, other, wanted, *in_hbm(strips))


def pack_right_body(tiles_ref, *out_refs):
    count, strip, _ = out_refs[0].shape
    row_index = lax.axis_index("row")
    for away, out_ref in enumerate(out_refs):
        start = pl.multiple_of((row_index + away) % len(out_refs) * strip, strip)
        for tile in range(count):
            out_ref[tile] = tiles_ref[tile, pl.ds(start, strip), :]


def pack_right(tiles, rows):
    count, order = tiles.shape[:2]
    shape = (count, order // rows, order)
    return pl.pallas_call(
        pack_right_body, out_shape=[jax.ShapeDtypeStruct(shape, jnp.float32)] * rows, compiler_params=LIMIT
    )(*in_hbm(tiles))


def plan_body(
    rows, base_ref, strips_ref, mates_ref,
    send_ref, codes_ref, counts_ref, peak_ref,
    table, values, keys, picks, places_vmem, send, places, sem, send_sems,
):
    row_index, base = lax.axis_index("row"), base_ref[0]
    peers, cap = send_ref.shape[:2]
    per_peer = strips_ref.shape[0] // peers
    band = 8
    blocks = peers * band
    band_rows = blocks // rows
    groups = peers // PER_GROUP
    deep = picks.shape[0] // (groups + 1)
    halves = pl.cdiv(cap, SLOT_PITCH)
    f32, bf16 = jnp.float32, jnp.bfloat16
    iota = functools.partial(lax.broadcasted_iota, jnp.int32)

    one, zero = jnp.ones((blocks, LANES), bf16), jnp.zeros((blocks, LANES), bf16)
    tall = (iota((blocks, LANES), 0) + 1).astype(f32).astype(bf16)
    in_band = iota((band_rows, LANES), 0).astype(f32)
    band_start = (iota((1, LANES), 1) // SLOT_PITCH * band_rows + 1).astype(f32)
    band_mask = jnp.where(iota((blocks, LANES), 0) // band_rows == iota((blocks, LANES), 1) // SLOT_PITCH, 1.0, 0.0)
    band_mask = band_mask.astype(bf16)
    short = iota((band, LANES), 0).astype(f32) + 1.0
    names = iota((band, LANES), 1).astype(f32) + 1.0
    targets = []
    for peer in range(peers):
        meta = strips_ref[peer * per_peer + per_peer - 1]
        row_hot = jnp.where(in_band == meta[0:1, :] - band_start, 1.0, 0.0).astype(bf16)
        row_hot = jnp.concatenate([row_hot] * rows, axis=0) * band_mask
        col_hot = jnp.where(short + float(peer * band) == meta[1:2, :], names, 0.0).astype(bf16)
        table[peer * band:(peer + 1) * band, :] = lax.dot_general(
            col_hot, row_hot, (((1,), (1,)), ((), ())), preferred_element_type=f32
        )
        if peer % PER_GROUP == 0:
            targets.append(meta)
        else:
            targets[-1] = targets[-1] + meta
    by_col = table[...]
    by_row = by_col.T.astype(bf16)
    by_col = by_col.astype(bf16)

    below = jnp.where(iota((blocks, blocks), 0) >= iota((blocks, blocks), 1), 1.0, 0.0).astype(bf16)
    lane_from, lane_to = iota((LANES, LANES), 0), iota((LANES, LANES), 1)
    same_peer = lane_from // SLOT_PITCH == lane_to // SLOT_PITCH
    earlier = jnp.where(same_peer & (lane_from < lane_to), 1.0, 0.0).astype(bf16)
    together = jnp.where(same_peer, 1.0, 0.0)
    fixed = iota((blocks, LANES), 0) // band * per_peer + ((iota((blocks, LANES), 1) % SLOT_PITCH) << 16)
    fixed = (fixed - (SLOT_PITCH * row_index + 1 + 512)).astype(f32)

    targets = [(meta[2:3, :], meta[3:4, :]) for meta in targets]
    targets.append((mates_ref[2:3, :], mates_ref[3:4, :]))
    everything = []
    for group, (target_rows, target_cols) in enumerate(targets):
        def hot(target):
            few = jnp.broadcast_to(target, (16, LANES)).astype(bf16)
            return jnp.where(tall == jnp.concatenate([few] * (blocks // 16), axis=0), one, zero)

        left = jnp.dot(by_col, hot(target_rows), preferred_element_type=f32)
        right = jnp.dot(by_row, hot(target_cols), preferred_element_type=f32)
        hit = left * right > 0.0
        ranks = jnp.dot(below, jnp.where(hit, 1.0, 0.0).astype(bf16), preferred_element_type=f32)
        everything.append(ranks[blocks - 1:blocks, :])
        keys[group * blocks:(group + 1) * blocks, :] = jnp.where(hit, ranks, 0.0)
        if group < groups:
            value = fixed + left + right * 512.0
        else:
            name = right.astype(jnp.int32) - 1
            value = (name - (SLOT_PITCH - per_peer + 1) * (name >> 4)).astype(f32)
        values[group * blocks:(group + 1) * blocks, :] = value
    found = jnp.concatenate(everything + everything[-1:] * (8 - len(everything)), axis=0)
    ahead = jnp.dot(found.astype(bf16), earlier, preferred_element_type=f32) - base.astype(f32)
    counts = jnp.dot(found.astype(bf16), together.astype(bf16), preferred_element_type=f32)
    counts_ref[...] = counts.astype(jnp.int32)
    peak_ref[...] = jnp.broadcast_to(jnp.max(jnp.max(counts[0:groups, :], axis=0, keepdims=True), axis=1, keepdims=True), (8, LANES))
    picks[...] = jnp.zeros_like(picks)
    depth = jnp.max(found).astype(jnp.int32)
    slot_at = iota((deep, LANES), 0).astype(f32)

    def one_depth(level, carry):
        level_f = level.astype(f32)
        for group in range(groups + 1):
            span = slice(group * blocks, (group + 1) * blocks)
            value = jnp.sum(jnp.where(keys[span, :] == level_f + 1.0, values[span, :], 0.0), axis=0, keepdims=True)
            place = jnp.where(found[group:group + 1, :] > level_f, ahead[group:group + 1, :] + level_f, -1.0)
            span = slice(group * deep, (group + 1) * deep)
            picks[span, :] = picks[span, :] + jnp.where(slot_at == place, value, 0.0)
        return carry

    lax.fori_loop(0, depth, one_depth, 0)
    spread = jnp.dot(picks[...], together, precision=lax.Precision.HIGHEST, preferred_element_type=f32)
    mine = iota((deep, LANES), 0) % SLOT_PITCH == iota((deep, LANES), 1) % SLOT_PITCH
    lines = []
    for group in range(groups + 1):
        chosen = jnp.where(mine, spread[group * deep:(group + 1) * deep, :], 0.0)
        for half in range(halves):
            lines.append(jnp.sum(chosen[half * SLOT_PITCH:(half + 1) * SLOT_PITCH, :], axis=0, keepdims=True))
    lines += lines[-1:] * (codes_ref.shape[0] - len(lines))
    codes = jnp.concatenate(lines, axis=0).astype(jnp.int32)
    codes_ref[...] = codes
    places_vmem[...] = codes & 511
    copy = pltpu.make_async_copy(places_vmem, places, sem)
    copy.start()
    copy.wait()

    def one_group(group):
        part = pl.ds(group * PER_GROUP, PER_GROUP)
        return pltpu.make_async_copy(send.at[part], send_ref.at[part], send_sems.at[group])

    for group in range(groups):
        for peer in range(group * PER_GROUP, (group + 1) * PER_GROUP):
            line, first = group * halves, peer % PER_GROUP * SLOT_PITCH
            for at in range(cap):
                send[peer, at] = strips_ref[places[line + at // SLOT_PITCH, first + at % SLOT_PITCH]]
        one_group(group).start()
    for group in range(groups):
        one_group(group).wait()


def whole(shape):
    return pl.BlockSpec(shape, lambda i, *_: (0,) * len(shape))


def plan(strips, mates, base, rows, peers, cap):
    strip, order = strips.shape[1:]
    groups = peers // PER_GROUP
    lines = padded((groups + 1) * pl.cdiv(cap, SLOT_PITCH), 8)
    send = (peers, cap, strip, order)
    blocks = peers * 8
    shapes = [(send, jnp.float32), ((lines, LANES), jnp.int32), ((8, LANES), jnp.int32), ((8, LANES), jnp.float32)]
    return pl.pallas_call(
        functools.partial(plan_body, rows),
        grid_spec=pltpu.PrefetchScalarGridSpec(
            num_scalar_prefetch=1,
            grid=(1,),
            in_specs=[whole(strips.shape), whole(mates.shape)],
            out_specs=[HBM] + [whole(shape) for shape, _ in shapes[1:]],
            scratch_shapes=[
                pltpu.VMEM((blocks, blocks), jnp.float32),
                pltpu.VMEM(((groups + 1) * blocks, LANES), jnp.float32),
                pltpu.VMEM(((groups + 1) * blocks, LANES), jnp.float32),
                pltpu.VMEM(((groups + 1) * padded(cap, 8), LANES), jnp.float32),
                pltpu.VMEM((lines, LANES), jnp.int32),
                pltpu.VMEM(send, jnp.float32),
                pltpu.SMEM((lines, LANES), jnp.int32),
                pltpu.SemaphoreType.DMA,
                pltpu.SemaphoreType.DMA((groups,)),
            ],
        ),
        out_shape=[pltpu.HBM(*shapes[0])] + [jax.ShapeDtypeStruct(*shape) for shape in shapes[1:]],
        compiler_params=LIMIT,
    )(base.reshape(1), pltpu.with_memory_space_constraint(strips, pltpu.VMEM), mates)


def collect_body(rows, first_line, codes, peak_ref, *refs):
    piece_refs, right_refs, panel = refs[:rows], refs[rows:2 * rows], refs[2 * rows]
    row_index = lax.axis_index("row")
    count, strip, _ = piece_refs[0].shape
    cap = right_refs[0].shape[0] - 1
    for away, piece_ref in enumerate(piece_refs):
        start = (row_index + rows - away) % rows * count
        for tile in range(count):
            panel[start + tile] = piece_ref[tile]
    for away, right_ref in enumerate(right_refs):
        lane = (row_index + away) % rows * SLOT_PITCH
        for at in range(cap):
            right_ref[at] = panel[codes[first_line + at // SLOT_PITCH, lane + at % SLOT_PITCH]]
        right_ref[cap, 0:8, :] = peak_ref[...]
        right_ref[cap, 8:16, :] = peak_ref[...]


def collect(codes, peak, pieces, peers, cap):
    rows = len(pieces)
    count, strip, order = pieces[0].shape
    right = (cap + 1, strip, order)
    return pl.pallas_call(
        functools.partial(collect_body, rows, peers // PER_GROUP * pl.cdiv(cap, SLOT_PITCH)),
        grid_spec=pltpu.PrefetchScalarGridSpec(
            num_scalar_prefetch=1,
            grid=(1,),
            in_specs=[whole(operand.shape) for operand in (peak, *pieces)],
            out_specs=[whole(right)] * rows,
            scratch_shapes=[pltpu.VMEM((rows * count, strip, order), jnp.float32)],
        ),
        out_shape=[jax.ShapeDtypeStruct(right, jnp.float32)] * rows,
        compiler_params=LIMIT,
    )(codes, peak, *in_hbm(*pieces))


def ready_body(*refs):
    right_refs, out_hbm, most_ref, right, out_ref, sem = refs[:-5], *refs[-5:]
    rows, cap, order = len(right_refs), *out_ref.shape[:2]
    row_index = lax.axis_index("row")
    strip = right_refs[0].shape[1]
    most = right_refs[0][cap, 0:8, :]
    for right_ref in right_refs[1:]:
        most = jnp.maximum(most, right_ref[cap, 0:8, :])
    most_ref[...] = most.astype(jnp.int32)

    def one_tile(at, carry):
        for away, right_ref in enumerate(right_refs):
            start = pl.multiple_of((row_index + rows - away) % rows * strip, strip)
            right[pl.ds(start, strip), :] = right_ref[at]
        b = right[...]
        b_high = b.astype(jnp.bfloat16)
        out_ref[at, :, :order] = b_high
        out_ref[at, :, order:] = (b - b_high.astype(jnp.float32)).astype(jnp.bfloat16)
        return carry

    lax.fori_loop(0, cap, one_tile, 0)
    copy = pltpu.make_async_copy(out_ref, out_hbm, sem)
    copy.start()
    copy.wait()


def ready(right):
    cap, order = right[0].shape[0] - 1, right[0].shape[2]
    vmem = pl.BlockSpec(memory_space=pltpu.VMEM)
    rights, most = pl.pallas_call(
        ready_body,
        in_specs=[vmem] * len(right),
        out_specs=[HBM, vmem],
        out_shape=[pltpu.HBM((cap, order, 2 * order), jnp.bfloat16), jax.ShapeDtypeStruct((8, LANES), jnp.int32)],
        scratch_shapes=[
            pltpu.VMEM((order, order), jnp.float32),
            pltpu.VMEM((cap, order, 2 * order), jnp.bfloat16),
            pltpu.SemaphoreType.DMA,
        ],
        compiler_params=LIMIT,
    )(*right)
    return rights, most[0, 0]


def product_body(first, scalars, codes, counts, left_ref, rights_ref, *refs):
    out_ref, left, rights, sems = refs[-4:]
    own, base = lax.axis_index(GROUP), scalars[0]
    peers, cap, strip, order = left_ref.shape
    line = (own >> 3) * pl.cdiv(cap, SLOT_PITCH)
    lane = (own & (PER_GROUP - 1)) * SLOT_PITCH
    todo = jnp.clip(counts[own >> 3, lane] - base, 0, cap)

    def fetch(at):
        return pltpu.make_async_copy(rights_ref.at[at], rights.at[at], sems.at[at])

    for at in range(cap):
        fetch(at).start()
    if first:
        out_ref[...] = jnp.zeros_like(out_ref)
    else:
        out_ref[...] = refs[0][...]

    def product(at, half):
        fetch(at).wait()
        for peer in range(peers):
            left[half, peer * strip:(peer + 1) * strip, :] = left_ref[peer, at]
        a = left[half]
        a_high = a.astype(jnp.bfloat16)
        a_low = (a - a_high.astype(jnp.float32)).astype(jnp.bfloat16)
        both = rights[at]
        sums = jnp.dot(
            jnp.concatenate([a_high, a_low], axis=1),
            jnp.concatenate([both, both], axis=0),
            preferred_element_type=jnp.float32,
        )
        return sums[:, :order] + sums[:, order:]

    def target(at):
        return codes[line + (at >> 4), lane + (at & (SLOT_PITCH - 1))] >> 16

    def several(step, carry):
        at = TOGETHER * step
        sums = [product(at + n, n) for n in range(TOGETHER)]
        out_ref[target(at)] += sums[0]
        for n in range(1, TOGETHER):
            @pl.when(at + n < todo)
            def _():
                out_ref[target(at + n)] += sums[n]

        return carry

    def unused(at, carry):
        fetch(at).wait()
        return carry

    steps = (todo + TOGETHER - 1) // TOGETHER
    lax.fori_loop(0, steps, several, 0)
    lax.fori_loop(TOGETHER * steps, cap, unused, 0)


def multiply_round(left, right, codes, counts, base, running, kept):
    order = left.shape[-1]
    first = running is None
    tiles = (kept, order, order)
    rights, most = ready(right)
    scalars = jnp.stack([base, most])
    operands = [pltpu.with_memory_space_constraint(left, pltpu.VMEM), *in_hbm(rights)] + ([] if first else [running])
    summed = pl.pallas_call(
        functools.partial(product_body, first),
        grid_spec=pltpu.PrefetchScalarGridSpec(
            num_scalar_prefetch=3,
            grid=(1,),
            in_specs=[whole(left.shape), HBM] + ([] if first else [whole(tiles)]),
            out_specs=whole(tiles),
            scratch_shapes=[
                pltpu.VMEM((TOGETHER, order, order), jnp.float32),
                pltpu.VMEM(rights.shape, rights.dtype),
                pltpu.SemaphoreType.DMA((rights.shape[0],)),
            ],
        ),
        out_shape=jax.ShapeDtypeStruct(tiles, jnp.float32),
        compiler_params=LIMIT,
    )(scalars, codes, counts, *operands)
    return summed, most


def shift_all(pieces):
    rows = len(pieces)
    return [pieces[0]] + [
        lax.ppermute(pieces[by], "row", [(i, (i + by) % rows) for i in range(rows)]) for by in range(1, rows)
    ]


def swap_rows(array, rows, by):
    return lax.ppermute(array, "row", [(i, i ^ by) for i in range(rows)])


def local(tile_values, tile_rows, tile_cols, tile_counts, out_rows, out_cols):
    order = tile_values.shape[-1]
    kept = out_rows.shape[-1]
    rows = lax.axis_size("row")
    peers = lax.axis_size(GROUP)
    tiles = tile_values.reshape(-1, order, order)

    listed, wanted = label(tile_rows, tile_cols, tile_counts, out_rows, out_cols)
    for by in (1, 2):
        listed = listed + swap_rows(listed, rows, by)
    strips, mates = stamp(listed, swap_rows(listed, rows, rows - 2), wanted, pack(tiles, peers))
    pieces = shift_all(pack_right(tiles, rows))
    strips = lax.all_to_all(strips, GROUP, 0, 0, tiled=True)
    strips, pieces = lax.optimization_barrier((strips, pieces))
    strips = strips.reshape(-1, order // peers, order)

    def one_round(base, running):
        send, codes, counts, peak = plan(strips, mates, base, rows, peers, ROUND_CAP)
        left = lax.all_to_all(send, GROUP, 0, 0, tiled=True)
        right = shift_all(collect(codes, peak, pieces, peers, ROUND_CAP))
        return multiply_round(left, right, codes, counts, base, running, kept)

    summed, most = one_round(jnp.zeros((), jnp.int32), None)

    def unfinished(state):
        return state[0] < most

    def further(state):
        return state[0] + ROUND_CAP, one_round(*state)[0]

    unused, summed = lax.while_loop(unfinished, further, (jnp.int32(ROUND_CAP), summed))
    return summed.reshape(1, 1, kept, order, order)


def solution(mesh):
    in_specs = (
        P("row", GROUP, None, None, None, None),
        P("row", GROUP, None, None),
        P("row", GROUP, None, None),
        P("row", GROUP, None),
        P("row", "col", None, None),
        P("row", "col", None, None),
    )
    out_specs = P("row", GROUP, None, None, None)
    return jax.shard_map(local, mesh=mesh, in_specs=in_specs, out_specs=out_specs, check_vma=False)
```

```python
import functools

import jax
import jax.numpy as jnp
from jax import lax
from jax.experimental import pallas as pl
from jax.experimental.pallas import tpu as pltpu
from jax.sharding import PartitionSpec as P

GROUP = ("col", "layer")
LANES = 128
SLOT_PITCH = 16
PER_GROUP = LANES // SLOT_PITCH
ROUND_CAP = 20
TOGETHER = 2
LIMIT = pltpu.CompilerParams(vmem_limit_bytes=20 * 2**20)
HBM = pl.BlockSpec(memory_space=pltpu.HBM)


def in_hbm(*arrays):
    return [pltpu.with_memory_space_constraint(array, pltpu.HBM) for array in arrays]


def padded(size, unit):
    return unit * pl.cdiv(size, unit)


def label_body(*refs):
    sources, listed_ref, wanted_ref, sems, copies = refs[:5], refs[5], refs[6], refs[7], refs[8:]
    moves = [pltpu.make_async_copy(a, b, sems.at[n]) for n, (a, b) in enumerate(zip(sources, copies))]
    for move in moves:
        move.start()
    for move in moves:
        move.wait()
    tile_rows, tile_cols, counts, out_rows, out_cols = copies
    lists, capacity = tile_rows.shape[2:]
    row_index, layer_index = lax.axis_index("row"), lax.axis_index("layer")
    in_group = lax.axis_index(GROUP) % PER_GROUP
    lane = lax.broadcasted_iota(jnp.int32, (1, LANES), 1)
    nothing = jnp.zeros((1, LANES), jnp.int32)
    rows, cols, kept_rows, kept_cols = nothing, nothing, nothing, nothing
    mate_rows, mate_cols = nothing, nothing
    for at in range(lists):
        for slot in range(capacity):
            live = slot < counts[0, 0, at]
            here = lane == jnp.where(live, row_index * SLOT_PITCH + at * capacity + slot, -1)
            rows = jnp.where(here, tile_rows[0, 0, at, slot] + 1, rows)
            cols = jnp.where(here, tile_cols[0, 0, at, slot] + 1, cols)
    for at in range(out_rows.shape[3]):
        target_row, target_col = out_rows[0, 0, layer_index, at] + 1, out_cols[0, 0, layer_index, at] + 1
        here = lane == in_group * SLOT_PITCH + at
        kept_rows = jnp.where(here, target_row, kept_rows)
        kept_cols = jnp.where(here, target_col, kept_cols)
        here = lane == row_index * SLOT_PITCH + at
        mate_rows = jnp.where(here, target_row, mate_rows)
        mate_cols = jnp.where(here, target_col, mate_cols)
    listed_ref[...] = jnp.concatenate([rows, cols, mate_rows, mate_cols]).astype(jnp.float32)
    wanted_ref[...] = jnp.concatenate([kept_rows, kept_cols]).astype(jnp.float32)


def label(tile_rows, tile_cols, tile_counts, out_rows, out_cols):
    operands = (tile_rows, tile_cols, tile_counts, out_rows, out_cols)
    return pl.pallas_call(
        label_body,
        in_specs=[HBM] * 5,
        out_shape=[jax.ShapeDtypeStruct((n, LANES), jnp.float32) for n in (4, 2)],
        scratch_shapes=[pltpu.SemaphoreType.DMA((5,))] + [pltpu.SMEM(x.shape, jnp.int32) for x in operands],
        compiler_params=LIMIT,
    )(*in_hbm(*operands))


def pack_body(tiles_hbm, out_ref, tiles, sems):
    peers, per_peer, strip, _ = out_ref.shape
    for tile in range(per_peer - 1):
        pltpu.make_async_copy(tiles_hbm.at[tile], tiles.at[tile], sems.at[tile]).start()

    def one_tile(tile, carry):
        pltpu.make_async_copy(tiles_hbm.at[tile], tiles.at[tile], sems.at[tile]).wait()
        for peer in range(peers):
            out_ref[peer, tile] = tiles[tile, peer * strip:(peer + 1) * strip, :]
        return carry

    lax.fori_loop(0, per_peer - 1, one_tile, 0)


def pack(tiles, peers):
    count, order = tiles.shape[:2]
    shape = (peers, count + 1, order // peers, order)
    return pl.pallas_call(
        pack_body,
        in_specs=[HBM],
        out_shape=pltpu.HBM(shape, jnp.float32),
        scratch_shapes=[pltpu.VMEM(tiles.shape, jnp.float32), pltpu.SemaphoreType.DMA((count,))],
        compiler_params=LIMIT,
    )(*in_hbm(tiles))


def stamp_body(one_ref, other_ref, wanted_ref, strips_in, strips_out, total_ref, meta, sem):
    peers, per_peer = strips_out.shape[:2]
    total = one_ref[...] + other_ref[...]
    total_ref[...] = total
    full = jnp.concatenate([total[0:2, :], wanted_ref[...]])
    for peer in range(peers):
        meta[peer] = full
    copy = pltpu.make_async_copy(meta, strips_out.at[:, per_peer - 1], sem)
    copy.start()
    copy.wait()


def stamp(one, other, wanted, strips):
    peers, _, strip, order = strips.shape
    vmem = pl.BlockSpec(memory_space=pltpu.VMEM)
    return pl.pallas_call(
        stamp_body,
        in_specs=[vmem, vmem, vmem, HBM],
        out_specs=[HBM, vmem],
        out_shape=[pltpu.HBM(strips.shape, jnp.float32), jax.ShapeDtypeStruct(one.shape, jnp.float32)],
        input_output_aliases={3: 0},
        scratch_shapes=[pltpu.VMEM((peers, strip, order), jnp.float32), pltpu.SemaphoreType.DMA],
        compiler_params=LIMIT,
    )(one, other, wanted, *in_hbm(strips))


def pack_right_body(tiles_ref, *out_refs):
    count, strip, _ = out_refs[0].shape
    row_index = lax.axis_index("row")
    for away, out_ref in enumerate(out_refs):
        start = pl.multiple_of((row_index + away) % len(out_refs) * strip, strip)
        for tile in range(count):
            out_ref[tile] = tiles_ref[tile, pl.ds(start, strip), :]


def pack_right(tiles, rows):
    count, order = tiles.shape[:2]
    shape = (count, order // rows, order)
    return pl.pallas_call(
        pack_right_body, out_shape=[jax.ShapeDtypeStruct(shape, jnp.float32)] * rows, compiler_params=LIMIT
    )(*in_hbm(tiles))


def list_products(by_col, by_row, targets, value_of, base, cap, values, keys, picks):
    blocks = by_col.shape[0]
    groups = len(targets)
    deep = picks.shape[0] // groups
    f32, bf16 = jnp.float32, jnp.bfloat16
    iota = functools.partial(lax.broadcasted_iota, jnp.int32)
    one, zero = jnp.ones((blocks, LANES), bf16), jnp.zeros((blocks, LANES), bf16)
    tall = (iota((blocks, LANES), 0) + 1).astype(f32).astype(bf16)
    below = jnp.where(iota((blocks, blocks), 0) >= iota((blocks, blocks), 1), 1.0, 0.0).astype(bf16)
    lane_from, lane_to = iota((LANES, LANES), 0), iota((LANES, LANES), 1)
    same_peer = lane_from // SLOT_PITCH == lane_to // SLOT_PITCH
    earlier = jnp.where(same_peer & (lane_from < lane_to), 1.0, 0.0).astype(bf16)
    together = jnp.where(same_peer, 1.0, 0.0)

    everything = []
    for group, (target_rows, target_cols) in enumerate(targets):
        def hot(target):
            few = jnp.broadcast_to(target, (16, LANES)).astype(bf16)
            return jnp.where(tall == jnp.concatenate([few] * (blocks // 16), axis=0), one, zero)

        left = jnp.dot(by_col, hot(target_rows), preferred_element_type=f32)
        right = jnp.dot(by_row, hot(target_cols), preferred_element_type=f32)
        hit = left * right > 0.0
        ranks = jnp.dot(below, jnp.where(hit, 1.0, 0.0).astype(bf16), preferred_element_type=f32)
        everything.append(ranks[blocks - 1:blocks, :])
        keys[group * blocks:(group + 1) * blocks, :] = jnp.where(hit, ranks, 0.0)
        values[group * blocks:(group + 1) * blocks, :] = value_of(left, right)
    found = jnp.concatenate(everything + everything[-1:] * (8 - len(everything)), axis=0)
    ahead = jnp.dot(found.astype(bf16), earlier, preferred_element_type=f32) - base.astype(f32)
    counts = jnp.dot(found.astype(bf16), together.astype(bf16), preferred_element_type=f32)
    picks[...] = jnp.zeros_like(picks)
    depth = jnp.max(found).astype(jnp.int32)
    slot_at = iota((deep, LANES), 0).astype(f32)

    def one_depth(level, carry):
        level_f = level.astype(f32)
        for group in range(groups):
            span = slice(group * blocks, (group + 1) * blocks)
            value = jnp.sum(jnp.where(keys[span, :] == level_f + 1.0, values[span, :], 0.0), axis=0, keepdims=True)
            place = jnp.where(found[group:group + 1, :] > level_f, ahead[group:group + 1, :] + level_f, -1.0)
            span = slice(group * deep, (group + 1) * deep)
            picks[span, :] = picks[span, :] + jnp.where(slot_at == place, value, 0.0)
        return carry

    lax.fori_loop(0, depth, one_depth, 0)
    spread = jnp.dot(picks[...], together, precision=lax.Precision.HIGHEST, preferred_element_type=f32)
    mine = iota((deep, LANES), 0) % SLOT_PITCH == iota((deep, LANES), 1) % SLOT_PITCH
    lines = []
    for group in range(groups):
        chosen = jnp.where(mine, spread[group * deep:(group + 1) * deep, :], 0.0)
        for half in range(pl.cdiv(cap, SLOT_PITCH)):
            lines.append(jnp.sum(chosen[half * SLOT_PITCH:(half + 1) * SLOT_PITCH, :], axis=0, keepdims=True))
    return lines, counts


def plan_body(
    rows, base_ref, strips_ref,
    send_ref, codes_ref, counts_ref, peak_ref, by_col_ref, by_row_ref,
    table, values, keys, picks, places_vmem, send, places, sem, send_sems,
):
    row_index, base = lax.axis_index("row"), base_ref[0]
    peers, cap = send_ref.shape[:2]
    per_peer = strips_ref.shape[0] // peers
    band = 8
    blocks = peers * band
    band_rows = blocks // rows
    groups = peers // PER_GROUP
    halves = pl.cdiv(cap, SLOT_PITCH)
    f32, bf16 = jnp.float32, jnp.bfloat16
    iota = functools.partial(lax.broadcasted_iota, jnp.int32)

    in_band = iota((band_rows, LANES), 0).astype(f32)
    band_start = (iota((1, LANES), 1) // SLOT_PITCH * band_rows + 1).astype(f32)
    band_mask = jnp.where(iota((blocks, LANES), 0) // band_rows == iota((blocks, LANES), 1) // SLOT_PITCH, 1.0, 0.0)
    band_mask = band_mask.astype(bf16)
    short = iota((band, LANES), 0).astype(f32) + 1.0
    names = iota((band, LANES), 1).astype(f32) + 1.0
    targets = []
    for peer in range(peers):
        meta = strips_ref[peer * per_peer + per_peer - 1]
        row_hot = jnp.where(in_band == meta[0:1, :] - band_start, 1.0, 0.0).astype(bf16)
        row_hot = jnp.concatenate([row_hot] * rows, axis=0) * band_mask
        col_hot = jnp.where(short + float(peer * band) == meta[1:2, :], names, 0.0).astype(bf16)
        table[peer * band:(peer + 1) * band, :] = lax.dot_general(
            col_hot, row_hot, (((1,), (1,)), ((), ())), preferred_element_type=f32
        )
        if peer % PER_GROUP == 0:
            targets.append(meta)
        else:
            targets[-1] = targets[-1] + meta
    by_col = table[...]
    by_row = by_col.T.astype(bf16)
    by_col = by_col.astype(bf16)
    by_col_ref[...] = by_col
    by_row_ref[...] = by_row

    fixed = iota((blocks, LANES), 0) // band * per_peer + ((iota((blocks, LANES), 1) % SLOT_PITCH) << 16)
    fixed = (fixed - (SLOT_PITCH * row_index + 1 + 512)).astype(f32)
    lines, counts = list_products(
        by_col, by_row, [(meta[2:3, :], meta[3:4, :]) for meta in targets],
        lambda left, right: fixed + left + right * 512.0, base, cap, values, keys, picks,
    )
    codes = jnp.concatenate(lines, axis=0).astype(jnp.int32)
    places_vmem[...] = codes & 511
    copy = pltpu.make_async_copy(places_vmem, places, sem)
    copy.start()
    codes_ref[...] = codes
    counts_ref[...] = counts.astype(jnp.int32)
    longest = jnp.max(jnp.max(counts[0:groups, :], axis=0, keepdims=True), axis=1, keepdims=True)
    peak_ref[...] = jnp.broadcast_to(longest, (8, LANES))
    copy.wait()

    def one_group(group):
        part = pl.ds(group * PER_GROUP, PER_GROUP)
        return pltpu.make_async_copy(send.at[part], send_ref.at[part], send_sems.at[group])

    for group in range(groups):
        for peer in range(group * PER_GROUP, (group + 1) * PER_GROUP):
            line, first = group * halves, peer % PER_GROUP * SLOT_PITCH
            for at in range(cap):
                send[peer, at] = strips_ref[places[line + at // SLOT_PITCH, first + at % SLOT_PITCH]]
        one_group(group).start()
    for group in range(groups):
        one_group(group).wait()


def whole(shape):
    return pl.BlockSpec(shape, lambda i, *_: (0,) * len(shape))


def list_scratch(groups, blocks, cap):
    lists = pltpu.VMEM((groups * blocks, LANES), jnp.float32)
    return [lists, lists, pltpu.VMEM((groups * padded(cap, 8), LANES), jnp.float32)]


def plan(strips, base, rows, peers, cap):
    strip, order = strips.shape[1:]
    groups = peers // PER_GROUP
    lines = groups * pl.cdiv(cap, SLOT_PITCH)
    send = (peers, cap, strip, order)
    blocks = peers * 8
    shapes = [
        (send, jnp.float32), ((lines, LANES), jnp.int32), ((8, LANES), jnp.int32), ((8, LANES), jnp.float32),
        ((blocks, blocks), jnp.bfloat16), ((blocks, blocks), jnp.bfloat16),
    ]
    return pl.pallas_call(
        functools.partial(plan_body, rows),
        grid_spec=pltpu.PrefetchScalarGridSpec(
            num_scalar_prefetch=1,
            grid=(1,),
            in_specs=[whole(strips.shape)],
            out_specs=[HBM] + [whole(shape) for shape, _ in shapes[1:]],
            scratch_shapes=[
                pltpu.VMEM((blocks, blocks), jnp.float32),
                *list_scratch(groups, blocks, cap),
                pltpu.VMEM((lines, LANES), jnp.int32),
                pltpu.VMEM(send, jnp.float32),
                pltpu.SMEM((lines, LANES), jnp.int32),
                pltpu.SemaphoreType.DMA,
                pltpu.SemaphoreType.DMA((groups,)),
            ],
        ),
        out_shape=[pltpu.HBM(*shapes[0])] + [jax.ShapeDtypeStruct(*shape) for shape in shapes[1:]],
        compiler_params=LIMIT,
    )(base.reshape(1), pltpu.with_memory_space_constraint(strips, pltpu.VMEM))


def collect_body(rows, base_ref, by_col_ref, by_row_ref, mates_ref, peak_ref, *refs):
    piece_refs, right_refs = refs[:rows], refs[rows:2 * rows]
    values, keys, picks, places_vmem, panel, places, sem = refs[2 * rows:]
    row_index = lax.axis_index("row")
    count, strip, _ = piece_refs[0].shape
    cap = right_refs[0].shape[0] - 1

    def place_of(left, right):
        name = right.astype(jnp.int32) - 1
        return (name - (SLOT_PITCH - count) * (name >> 4)).astype(jnp.float32)

    lines, _ = list_products(
        by_col_ref[...], by_row_ref[...], [(mates_ref[2:3, :], mates_ref[3:4, :])],
        place_of, base_ref[0], cap, values, keys, picks,
    )
    lines += lines[-1:] * (places_vmem.shape[0] - len(lines))
    places_vmem[...] = jnp.concatenate(lines, axis=0).astype(jnp.int32)
    copy = pltpu.make_async_copy(places_vmem, places, sem)
    copy.start()
    for away, piece_ref in enumerate(piece_refs):
        start = (row_index + rows - away) % rows * count
        for tile in range(count):
            panel[start + tile] = piece_ref[tile]
    copy.wait()
    for away, right_ref in enumerate(right_refs):
        lane = (row_index + away) % rows * SLOT_PITCH
        for at in range(cap):
            right_ref[at] = panel[places[at // SLOT_PITCH, lane + at % SLOT_PITCH]]
        right_ref[cap, 0:8, :] = peak_ref[...]
        right_ref[cap, 8:16, :] = peak_ref[...]


def collect(tables, mates, peak, pieces, base, cap):
    rows = len(pieces)
    count, strip, order = pieces[0].shape
    right = (cap + 1, strip, order)
    operands = (*tables, mates, peak, *pieces)
    return pl.pallas_call(
        functools.partial(collect_body, rows),
        grid_spec=pltpu.PrefetchScalarGridSpec(
            num_scalar_prefetch=1,
            grid=(1,),
            in_specs=[whole(operand.shape) for operand in operands],
            out_specs=[whole(right)] * rows,
            scratch_shapes=[
                *list_scratch(1, tables[0].shape[0], cap),
                pltpu.VMEM((8, LANES), jnp.int32),
                pltpu.VMEM((rows * count, strip, order), jnp.float32),
                pltpu.SMEM((8, LANES), jnp.int32),
                pltpu.SemaphoreType.DMA,
            ],
        ),
        out_shape=[jax.ShapeDtypeStruct(right, jnp.float32)] * rows,
        compiler_params=LIMIT,
    )(base.reshape(1), *tables, mates, peak, *in_hbm(*pieces))


def peak_body(*refs):
    *right_refs, most_ref = refs
    cap = right_refs[0].shape[0] - 1
    most = right_refs[0][cap, 0:8, :]
    for right_ref in right_refs[1:]:
        most = jnp.maximum(most, right_ref[cap, 0:8, :])
    most_ref[...] = most.astype(jnp.int32)


def product_body(first, rows, scalars, codes, counts, left_ref, *refs):
    right_refs, refs = refs[:rows], refs[rows:]
    out_ref, right = refs[-2:]
    out_ref[...] = jnp.zeros_like(out_ref) if first else refs[0][...]
    row_index, own, base = lax.axis_index("row"), lax.axis_index(GROUP), scalars[0]
    peers, cap, strip, order = left_ref.shape
    tall_strip = right_refs[0].shape[1]
    line = (own >> 3) * pl.cdiv(cap, SLOT_PITCH)
    lane = (own & (PER_GROUP - 1)) * SLOT_PITCH
    todo = jnp.clip(counts[own >> 3, lane] - base, 0, cap)
    bf16 = jnp.bfloat16

    def product(at, half):
        for away, right_ref in enumerate(right_refs):
            start = pl.multiple_of((row_index + rows - away) % rows * tall_strip, tall_strip)
            right[half, pl.ds(start, tall_strip), :] = right_ref[at]
        a, b = jnp.concatenate([left_ref[peer, at] for peer in range(peers)], axis=0), right[half]
        a_high, b_high = a.astype(bf16), b.astype(bf16)
        a_low = (a - a_high.astype(jnp.float32)).astype(bf16)
        b_low = (b - b_high.astype(jnp.float32)).astype(bf16)
        both = jnp.concatenate([b_high, b_low], axis=1)
        sums = jnp.dot(
            jnp.concatenate([a_high, a_low], axis=1),
            jnp.concatenate([both, both], axis=0),
            preferred_element_type=jnp.float32,
        )
        return sums[:, :order] + sums[:, order:]

    def target(at):
        return codes[line + (at >> 4), lane + (at & (SLOT_PITCH - 1))] >> 16

    def several(step, carry):
        at = TOGETHER * step
        sums = [product(at + n, n) for n in range(TOGETHER)]
        out_ref[target(at)] += sums[0]
        for n in range(1, TOGETHER):
            @pl.when(at + n < todo)
            def _():
                out_ref[target(at + n)] += sums[n]

        return carry

    lax.fori_loop(0, (todo + TOGETHER - 1) // TOGETHER, several, 0)


def multiply_round(left, right, codes, counts, base, running, kept):
    order = left.shape[-1]
    first = running is None
    tiles = (kept, order, order)
    most = pl.pallas_call(
        peak_body, out_shape=jax.ShapeDtypeStruct((8, LANES), jnp.int32), compiler_params=LIMIT
    )(*right)[0, 0]
    operands = [pltpu.with_memory_space_constraint(x, pltpu.VMEM) for x in (left, *right)] + ([] if first else [running])
    summed = pl.pallas_call(
        functools.partial(product_body, first, len(right)),
        grid_spec=pltpu.PrefetchScalarGridSpec(
            num_scalar_prefetch=3,
            grid=(1,),
            in_specs=[whole(operand.shape) for operand in operands],
            out_specs=whole(tiles),
            scratch_shapes=[pltpu.VMEM((TOGETHER, order, order), jnp.float32)],
        ),
        out_shape=jax.ShapeDtypeStruct(tiles, jnp.float32),
        compiler_params=LIMIT,
    )(jnp.stack([base, most]), codes, counts, *operands)
    return summed, most


def shift_all(pieces):
    rows = len(pieces)
    return [pieces[0]] + [
        lax.ppermute(pieces[by], "row", [(i, (i + by) % rows) for i in range(rows)]) for by in range(1, rows)
    ]


def swap_rows(array, rows, by):
    return lax.ppermute(array, "row", [(i, i ^ by) for i in range(rows)])


def local(tile_values, tile_rows, tile_cols, tile_counts, out_rows, out_cols):
    order = tile_values.shape[-1]
    kept = out_rows.shape[-1]
    rows = lax.axis_size("row")
    peers = lax.axis_size(GROUP)
    tiles = tile_values.reshape(-1, order, order)

    listed, wanted = label(tile_rows, tile_cols, tile_counts, out_rows, out_cols)
    for by in (1, 2):
        listed = listed + swap_rows(listed, rows, by)
    strips, mates = stamp(listed, swap_rows(listed, rows, rows - 2), wanted, pack(tiles, peers))
    pieces = shift_all(pack_right(tiles, rows))
    strips = lax.all_to_all(strips, GROUP, 0, 0, tiled=True)
    strips, pieces = lax.optimization_barrier((strips, pieces))
    strips = strips.reshape(-1, order // peers, order)

    def one_round(base, running):
        send, codes, counts, peak, *tables = plan(strips, base, rows, peers, ROUND_CAP)
        left = lax.all_to_all(send, GROUP, 0, 0, tiled=True)
        right = shift_all(collect(tables, mates, peak, pieces, base, ROUND_CAP))
        return multiply_round(left, right, codes, counts, base, running, kept)

    summed, most = one_round(jnp.zeros((), jnp.int32), None)

    def unfinished(state):
        return state[0] < most

    def further(state):
        return state[0] + ROUND_CAP, one_round(*state)[0]

    unused, summed = lax.while_loop(unfinished, further, (jnp.int32(ROUND_CAP), summed))
    return summed.reshape(1, 1, kept, order, order)


def solution(mesh):
    in_specs = (
        P("row", GROUP, None, None, None, None),
        P("row", GROUP, None, None),
        P("row", GROUP, None, None),
        P("row", GROUP, None),
        P("row", "col", None, None),
        P("row", "col", None, None),
    )
    out_specs = P("row", GROUP, None, None, None)
    return jax.shard_map(local, mesh=mesh, in_specs=in_specs, out_specs=out_specs, check_vma=False)
```

```python
import functools

import jax
import jax.numpy as jnp
from jax import lax
from jax.experimental import pallas as pl
from jax.experimental.pallas import tpu as pltpu
from jax.sharding import PartitionSpec as P

GROUP = ("col", "layer")
LANES = 128
SLOT_PITCH = 16
PER_GROUP = LANES // SLOT_PITCH
ROUND_CAP = 20
TOGETHER = 2
LIMIT = pltpu.CompilerParams(vmem_limit_bytes=20 * 2**20)
HBM = pl.BlockSpec(memory_space=pltpu.HBM)


def in_hbm(*arrays):
    return [pltpu.with_memory_space_constraint(array, pltpu.HBM) for array in arrays]


def padded(size, unit):
    return unit * pl.cdiv(size, unit)


def label_body(*refs):
    sources, listed_ref, wanted_ref, sems, copies = refs[:5], refs[5], refs[6], refs[7], refs[8:]
    moves = [pltpu.make_async_copy(a, b, sems.at[n]) for n, (a, b) in enumerate(zip(sources, copies))]
    for move in moves:
        move.start()
    for move in moves:
        move.wait()
    tile_rows, tile_cols, counts, out_rows, out_cols = copies
    lists, capacity = tile_rows.shape[2:]
    row_index, layer_index = lax.axis_index("row"), lax.axis_index("layer")
    in_group = lax.axis_index(GROUP) % PER_GROUP
    lane = lax.broadcasted_iota(jnp.int32, (1, LANES), 1)
    nothing = jnp.zeros((1, LANES), jnp.int32)
    rows, cols, kept_rows, kept_cols = nothing, nothing, nothing, nothing
    mate_rows, mate_cols = nothing, nothing
    for at in range(lists):
        for slot in range(capacity):
            live = slot < counts[0, 0, at]
            here = lane == jnp.where(live, row_index * SLOT_PITCH + at * capacity + slot, -1)
            rows = jnp.where(here, tile_rows[0, 0, at, slot] + 1, rows)
            cols = jnp.where(here, tile_cols[0, 0, at, slot] + 1, cols)
    for at in range(out_rows.shape[3]):
        target_row, target_col = out_rows[0, 0, layer_index, at] + 1, out_cols[0, 0, layer_index, at] + 1
        here = lane == in_group * SLOT_PITCH + at
        kept_rows = jnp.where(here, target_row, kept_rows)
        kept_cols = jnp.where(here, target_col, kept_cols)
        here = lane == row_index * SLOT_PITCH + at
        mate_rows = jnp.where(here, target_row, mate_rows)
        mate_cols = jnp.where(here, target_col, mate_cols)
    listed_ref[...] = jnp.concatenate([rows, cols, mate_rows, mate_cols]).astype(jnp.float32)
    wanted_ref[...] = jnp.concatenate([kept_rows, kept_cols]).astype(jnp.float32)


def label(tile_rows, tile_cols, tile_counts, out_rows, out_cols):
    operands = (tile_rows, tile_cols, tile_counts, out_rows, out_cols)
    return pl.pallas_call(
        label_body,
        in_specs=[HBM] * 5,
        out_shape=[jax.ShapeDtypeStruct((n, LANES), jnp.float32) for n in (4, 2)],
        scratch_shapes=[pltpu.SemaphoreType.DMA((5,))] + [pltpu.SMEM(x.shape, jnp.int32) for x in operands],
        compiler_params=LIMIT,
    )(*in_hbm(*operands))


def pack_body(tiles_hbm, out_ref, tiles, sems):
    peers, per_peer, strip, _ = out_ref.shape
    for tile in range(per_peer - 1):
        pltpu.make_async_copy(tiles_hbm.at[tile], tiles.at[tile], sems.at[tile]).start()

    def one_tile(tile, carry):
        pltpu.make_async_copy(tiles_hbm.at[tile], tiles.at[tile], sems.at[tile]).wait()
        for peer in range(peers):
            out_ref[peer, tile] = tiles[tile, peer * strip:(peer + 1) * strip, :]
        return carry

    lax.fori_loop(0, per_peer - 1, one_tile, 0)


def pack(tiles, peers):
    count, order = tiles.shape[:2]
    shape = (peers, count + 1, order // peers, order)
    return pl.pallas_call(
        pack_body,
        in_specs=[HBM],
        out_shape=pltpu.HBM(shape, jnp.float32),
        scratch_shapes=[pltpu.VMEM(tiles.shape, jnp.float32), pltpu.SemaphoreType.DMA((count,))],
        compiler_params=LIMIT,
    )(*in_hbm(tiles))


def stamp_body(one_ref, other_ref, wanted_ref, strips_in, strips_out, total_ref, meta, sem):
    peers, per_peer = strips_out.shape[:2]
    total = one_ref[...] + other_ref[...]
    total_ref[...] = total
    full = jnp.concatenate([total[0:2, :], wanted_ref[...]])
    for peer in range(peers):
        meta[peer] = full
    copy = pltpu.make_async_copy(meta, strips_out.at[:, per_peer - 1], sem)
    copy.start()
    copy.wait()


def stamp(one, other, wanted, strips):
    peers, _, strip, order = strips.shape
    vmem = pl.BlockSpec(memory_space=pltpu.VMEM)
    return pl.pallas_call(
        stamp_body,
        in_specs=[vmem, vmem, vmem, HBM],
        out_specs=[HBM, vmem],
        out_shape=[pltpu.HBM(strips.shape, jnp.float32), jax.ShapeDtypeStruct(one.shape, jnp.float32)],
        input_output_aliases={3: 0},
        scratch_shapes=[pltpu.VMEM((peers, strip, order), jnp.float32), pltpu.SemaphoreType.DMA],
        compiler_params=LIMIT,
    )(one, other, wanted, *in_hbm(strips))


def pack_right_body(tiles_ref, *out_refs):
    count, strip, _ = out_refs[0].shape
    row_index = lax.axis_index("row")
    for away, out_ref in enumerate(out_refs):
        start = pl.multiple_of((row_index + away) % len(out_refs) * strip, strip)
        for tile in range(count):
            out_ref[tile] = tiles_ref[tile, pl.ds(start, strip), :]


def pack_right(tiles, rows):
    count, order = tiles.shape[:2]
    shape = (count, order // rows, order)
    return pl.pallas_call(
        pack_right_body, out_shape=[jax.ShapeDtypeStruct(shape, jnp.float32)] * rows, compiler_params=LIMIT
    )(*in_hbm(tiles))


def list_products(by_col, by_row, targets, value_of, base, cap, values, keys, picks):
    blocks = by_col.shape[0]
    groups = len(targets)
    deep = picks.shape[0] // groups
    f32, bf16 = jnp.float32, jnp.bfloat16
    iota = functools.partial(lax.broadcasted_iota, jnp.int32)
    one, zero = jnp.ones((blocks, LANES), bf16), jnp.zeros((blocks, LANES), bf16)
    tall = (iota((blocks, LANES), 0) + 1).astype(f32).astype(bf16)
    below = jnp.where(iota((blocks, blocks), 0) >= iota((blocks, blocks), 1), 1.0, 0.0).astype(bf16)
    lane_from, lane_to = iota((LANES, LANES), 0), iota((LANES, LANES), 1)
    same_peer = lane_from // SLOT_PITCH == lane_to // SLOT_PITCH
    earlier = jnp.where(same_peer & (lane_from < lane_to), 1.0, 0.0).astype(bf16)
    together = jnp.where(same_peer, 1.0, 0.0)

    everything = []
    for group, (target_rows, target_cols) in enumerate(targets):
        def hot(target):
            few = jnp.broadcast_to(target, (16, LANES)).astype(bf16)
            return jnp.where(tall == jnp.concatenate([few] * (blocks // 16), axis=0), one, zero)

        left = jnp.dot(by_col, hot(target_rows), preferred_element_type=f32)
        right = jnp.dot(by_row, hot(target_cols), preferred_element_type=f32)
        hit = left * right > 0.0
        ranks = jnp.dot(below, jnp.where(hit, 1.0, 0.0).astype(bf16), preferred_element_type=f32)
        everything.append(ranks[blocks - 1:blocks, :])
        keys[group * blocks:(group + 1) * blocks, :] = jnp.where(hit, ranks, 0.0)
        values[group * blocks:(group + 1) * blocks, :] = value_of(left, right)
    found = jnp.concatenate(everything + everything[-1:] * (8 - len(everything)), axis=0)
    ahead = jnp.dot(found.astype(bf16), earlier, preferred_element_type=f32) - base.astype(f32)
    counts = jnp.dot(found.astype(bf16), together.astype(bf16), preferred_element_type=f32)
    picks[...] = jnp.zeros_like(picks)
    depth = jnp.max(found).astype(jnp.int32)
    slot_at = iota((deep, LANES), 0).astype(f32)

    def one_depth(level, carry):
        level_f = level.astype(f32)
        for group in range(groups):
            span = slice(group * blocks, (group + 1) * blocks)
            value = jnp.sum(jnp.where(keys[span, :] == level_f + 1.0, values[span, :], 0.0), axis=0, keepdims=True)
            place = jnp.where(found[group:group + 1, :] > level_f, ahead[group:group + 1, :] + level_f, -1.0)
            span = slice(group * deep, (group + 1) * deep)
            picks[span, :] = picks[span, :] + jnp.where(slot_at == place, value, 0.0)
        return carry

    lax.fori_loop(0, depth, one_depth, 0)
    spread = jnp.dot(picks[...], together, precision=lax.Precision.HIGHEST, preferred_element_type=f32)
    mine = iota((deep, LANES), 0) % SLOT_PITCH == iota((deep, LANES), 1) % SLOT_PITCH
    lines = []
    for group in range(groups):
        chosen = jnp.where(mine, spread[group * deep:(group + 1) * deep, :], 0.0)
        for half in range(pl.cdiv(cap, SLOT_PITCH)):
            lines.append(jnp.sum(chosen[half * SLOT_PITCH:(half + 1) * SLOT_PITCH, :], axis=0, keepdims=True))
    return lines, counts


def plan_body(
    rows, base_ref, strips_ref,
    send_ref, codes_ref, counts_ref, peak_ref, by_col_ref, by_row_ref,
    table, values, keys, picks, places_vmem, send, places, sem, send_sems,
):
    row_index, base = lax.axis_index("row"), base_ref[0]
    peers, cap = send_ref.shape[:2]
    per_peer = strips_ref.shape[0] // peers
    band = 8
    blocks = peers * band
    band_rows = blocks // rows
    groups = peers // PER_GROUP
    halves = pl.cdiv(cap, SLOT_PITCH)
    f32, bf16 = jnp.float32, jnp.bfloat16
    iota = functools.partial(lax.broadcasted_iota, jnp.int32)

    in_band = iota((band_rows, LANES), 0).astype(f32)
    band_start = (iota((1, LANES), 1) // SLOT_PITCH * band_rows + 1).astype(f32)
    band_mask = jnp.where(iota((blocks, LANES), 0) // band_rows == iota((blocks, LANES), 1) // SLOT_PITCH, 1.0, 0.0)
    band_mask = band_mask.astype(bf16)
    short = iota((band, LANES), 0).astype(f32) + 1.0
    names = iota((band, LANES), 1).astype(f32) + 1.0
    targets = []
    for peer in range(peers):
        meta = strips_ref[peer * per_peer + per_peer - 1]
        row_hot = jnp.where(in_band == meta[0:1, :] - band_start, 1.0, 0.0).astype(bf16)
        row_hot = jnp.concatenate([row_hot] * rows, axis=0) * band_mask
        col_hot = jnp.where(short + float(peer * band) == meta[1:2, :], names, 0.0).astype(bf16)
        table[peer * band:(peer + 1) * band, :] = lax.dot_general(
            col_hot, row_hot, (((1,), (1,)), ((), ())), preferred_element_type=f32
        )
        if peer % PER_GROUP == 0:
            targets.append(meta)
        else:
            targets[-1] = targets[-1] + meta
    by_col = table[...]
    by_row = by_col.T.astype(bf16)
    by_col = by_col.astype(bf16)
    by_col_ref[...] = by_col
    by_row_ref[...] = by_row

    fixed = iota((blocks, LANES), 0) // band * per_peer + ((iota((blocks, LANES), 1) % SLOT_PITCH) << 16)
    fixed = (fixed - (SLOT_PITCH * row_index + 1 + 512)).astype(f32)
    lines, counts = list_products(
        by_col, by_row, [(meta[2:3, :], meta[3:4, :]) for meta in targets],
        lambda left, right: fixed + left + right * 512.0, base, cap, values, keys, picks,
    )
    codes = jnp.concatenate(lines, axis=0).astype(jnp.int32)
    places_vmem[...] = codes & 511
    copy = pltpu.make_async_copy(places_vmem, places, sem)
    copy.start()
    codes_ref[...] = codes
    counts_ref[...] = counts.astype(jnp.int32)
    longest = jnp.max(jnp.max(counts[0:groups, :], axis=0, keepdims=True), axis=1, keepdims=True)
    peak_ref[...] = jnp.broadcast_to(longest, (8, LANES))
    copy.wait()

    def one_group(group):
        part = pl.ds(group * PER_GROUP, PER_GROUP)
        return pltpu.make_async_copy(send.at[part], send_ref.at[part], send_sems.at[group])

    for group in range(groups):
        for peer in range(group * PER_GROUP, (group + 1) * PER_GROUP):
            line, first = group * halves, peer % PER_GROUP * SLOT_PITCH
            for at in range(cap):
                send[peer, at] = strips_ref[places[line + at // SLOT_PITCH, first + at % SLOT_PITCH]]
        one_group(group).start()
    for group in range(groups):
        one_group(group).wait()


def whole(shape):
    return pl.BlockSpec(shape, lambda i, *_: (0,) * len(shape))


def list_scratch(groups, blocks, cap):
    lists = pltpu.VMEM((groups * blocks, LANES), jnp.float32)
    return [lists, lists, pltpu.VMEM((groups * padded(cap, 8), LANES), jnp.float32)]


def plan(strips, base, rows, peers, cap):
    strip, order = strips.shape[1:]
    groups = peers // PER_GROUP
    lines = groups * pl.cdiv(cap, SLOT_PITCH)
    send = (peers, cap, strip, order)
    blocks = peers * 8
    shapes = [
        (send, jnp.float32), ((lines, LANES), jnp.int32), ((8, LANES), jnp.int32), ((8, LANES), jnp.float32),
        ((blocks, blocks), jnp.bfloat16), ((blocks, blocks), jnp.bfloat16),
    ]
    return pl.pallas_call(
        functools.partial(plan_body, rows),
        grid_spec=pltpu.PrefetchScalarGridSpec(
            num_scalar_prefetch=1,
            grid=(1,),
            in_specs=[whole(strips.shape)],
            out_specs=[HBM] + [whole(shape) for shape, _ in shapes[1:]],
            scratch_shapes=[
                pltpu.VMEM((blocks, blocks), jnp.float32),
                *list_scratch(groups, blocks, cap),
                pltpu.VMEM((lines, LANES), jnp.int32),
                pltpu.VMEM(send, jnp.float32),
                pltpu.SMEM((lines, LANES), jnp.int32),
                pltpu.SemaphoreType.DMA,
                pltpu.SemaphoreType.DMA((groups,)),
            ],
        ),
        out_shape=[pltpu.HBM(*shapes[0])] + [jax.ShapeDtypeStruct(*shape) for shape in shapes[1:]],
        compiler_params=LIMIT,
    )(base.reshape(1), pltpu.with_memory_space_constraint(strips, pltpu.VMEM))


def collect_body(rows, base_ref, by_col_ref, by_row_ref, mates_ref, peak_ref, *refs):
    piece_refs, right_refs = refs[:rows], refs[rows:2 * rows]
    values, keys, picks, places_vmem, panel, places, sem = refs[2 * rows:]
    row_index = lax.axis_index("row")
    count, strip, _ = piece_refs[0].shape
    cap = right_refs[0].shape[0] - 1

    def place_of(left, right):
        name = right.astype(jnp.int32) - 1
        return (name - (SLOT_PITCH - count) * (name >> 4)).astype(jnp.float32)

    lines, _ = list_products(
        by_col_ref[...], by_row_ref[...], [(mates_ref[2:3, :], mates_ref[3:4, :])],
        place_of, base_ref[0], cap, values, keys, picks,
    )
    lines += lines[-1:] * (places_vmem.shape[0] - len(lines))
    places_vmem[...] = jnp.concatenate(lines, axis=0).astype(jnp.int32)
    copy = pltpu.make_async_copy(places_vmem, places, sem)
    copy.start()
    for away, piece_ref in enumerate(piece_refs):
        start = (row_index + rows - away) % rows * count
        for tile in range(count):
            panel[start + tile] = piece_ref[tile]
    copy.wait()
    for away, right_ref in enumerate(right_refs):
        lane = (row_index + away) % rows * SLOT_PITCH
        for at in range(cap):
            right_ref[at] = panel[places[at // SLOT_PITCH, lane + at % SLOT_PITCH]]
        right_ref[cap, 0:8, :] = peak_ref[...]
        right_ref[cap, 8:16, :] = peak_ref[...]


def collect(tables, mates, peak, pieces, base, cap):
    rows = len(pieces)
    count, strip, order = pieces[0].shape
    right = (cap + 1, strip, order)
    operands = (*tables, mates, peak, *pieces)
    return pl.pallas_call(
        functools.partial(collect_body, rows),
        grid_spec=pltpu.PrefetchScalarGridSpec(
            num_scalar_prefetch=1,
            grid=(1,),
            in_specs=[whole(operand.shape) for operand in operands],
            out_specs=[whole(right)] * rows,
            scratch_shapes=[
                *list_scratch(1, tables[0].shape[0], cap),
                pltpu.VMEM((8, LANES), jnp.int32),
                pltpu.VMEM((rows * count, strip, order), jnp.float32),
                pltpu.SMEM((8, LANES), jnp.int32),
                pltpu.SemaphoreType.DMA,
            ],
        ),
        out_shape=[jax.ShapeDtypeStruct(right, jnp.float32)] * rows,
        compiler_params=LIMIT,
    )(base.reshape(1), *tables, mates, peak, *in_hbm(*pieces))


def peak_body(*refs):
    *right_refs, most_ref = refs
    cap = right_refs[0].shape[0] - 1
    most = right_refs[0][cap, 0:8, :]
    for right_ref in right_refs[1:]:
        most = jnp.maximum(most, right_ref[cap, 0:8, :])
    most_ref[...] = most.astype(jnp.int32)


def product_body(first, rows, scalars, codes, counts, left_ref, *refs):
    right_refs, refs = refs[:rows], refs[rows:]
    out_ref, right = refs[-2:]
    out_ref[...] = jnp.zeros_like(out_ref) if first else refs[0][...]
    row_index, own, base = lax.axis_index("row"), lax.axis_index(GROUP), scalars[0]
    peers, cap = left_ref.shape[:2]
    tall_strip = right_refs[0].shape[1]
    line = (own >> 3) * pl.cdiv(cap, SLOT_PITCH)
    lane = (own & (PER_GROUP - 1)) * SLOT_PITCH
    todo = jnp.clip(counts[own >> 3, lane] - base, 0, cap)
    bf16 = jnp.bfloat16

    def product(at, half):
        for away, right_ref in enumerate(right_refs):
            start = pl.multiple_of((row_index + rows - away) % rows * tall_strip, tall_strip)
            right[half, pl.ds(start, tall_strip), :] = right_ref[at]
        a, b = jnp.concatenate([left_ref[peer, at] for peer in range(peers)], axis=0), right[half]
        a_high, b_high = a.astype(bf16), b.astype(bf16)
        a_low = (a - a_high.astype(jnp.float32)).astype(bf16)
        b_low = (b - b_high.astype(jnp.float32)).astype(bf16)
        return jnp.dot(
            jnp.concatenate([a_high, a_low, a_high], axis=1),
            jnp.concatenate([b_high, b_high, b_low], axis=0),
            preferred_element_type=jnp.float32,
        )

    def target(at):
        return codes[line + (at >> 4), lane + (at & (SLOT_PITCH - 1))] >> 16

    def several(step, carry):
        at = TOGETHER * step
        sums = [product(at + n, n) for n in range(TOGETHER)]
        out_ref[target(at)] += sums[0]
        for n in range(1, TOGETHER):
            @pl.when(at + n < todo)
            def _():
                out_ref[target(at + n)] += sums[n]

        return carry

    lax.fori_loop(0, (todo + TOGETHER - 1) // TOGETHER, several, 0)


def multiply_round(left, right, codes, counts, base, running, kept):
    order = left.shape[-1]
    first = running is None
    tiles = (kept, order, order)
    most = pl.pallas_call(
        peak_body, out_shape=jax.ShapeDtypeStruct((8, LANES), jnp.int32), compiler_params=LIMIT
    )(*right)[0, 0]
    operands = [pltpu.with_memory_space_constraint(x, pltpu.VMEM) for x in (left, *right)] + ([] if first else [running])
    summed = pl.pallas_call(
        functools.partial(product_body, first, len(right)),
        grid_spec=pltpu.PrefetchScalarGridSpec(
            num_scalar_prefetch=3,
            grid=(1,),
            in_specs=[whole(operand.shape) for operand in operands],
            out_specs=whole(tiles),
            scratch_shapes=[pltpu.VMEM((TOGETHER, order, order), jnp.float32)],
        ),
        out_shape=jax.ShapeDtypeStruct(tiles, jnp.float32),
        compiler_params=LIMIT,
    )(jnp.stack([base, most]), codes, counts, *operands)
    return summed, most


def shift_all(pieces):
    rows = len(pieces)
    return [pieces[0]] + [
        lax.ppermute(pieces[by], "row", [(i, (i + by) % rows) for i in range(rows)]) for by in range(1, rows)
    ]


def swap_rows(array, rows, by):
    return lax.ppermute(array, "row", [(i, i ^ by) for i in range(rows)])


def local(tile_values, tile_rows, tile_cols, tile_counts, out_rows, out_cols):
    order = tile_values.shape[-1]
    kept = out_rows.shape[-1]
    rows = lax.axis_size("row")
    peers = lax.axis_size(GROUP)
    tiles = tile_values.reshape(-1, order, order)

    listed, wanted = label(tile_rows, tile_cols, tile_counts, out_rows, out_cols)
    for by in (1, 2):
        listed = listed + swap_rows(listed, rows, by)
    listed, strips = lax.optimization_barrier((listed, pack(tiles, peers)))
    strips, mates = stamp(listed, swap_rows(listed, rows, rows - 2), wanted, strips)
    pieces = shift_all(pack_right(tiles, rows))
    strips = lax.all_to_all(strips, GROUP, 0, 0, tiled=True)
    strips, pieces = lax.optimization_barrier((strips, pieces))
    strips = strips.reshape(-1, order // peers, order)

    def one_round(base, running):
        send, codes, counts, peak, *tables = plan(strips, base, rows, peers, ROUND_CAP)
        left = lax.all_to_all(send, GROUP, 0, 0, tiled=True)
        right = shift_all(collect(tables, mates, peak, pieces, base, ROUND_CAP))
        return multiply_round(left, right, codes, counts, base, running, kept)

    summed, most = one_round(jnp.zeros((), jnp.int32), None)

    def unfinished(state):
        return state[0] < most

    def further(state):
        return state[0] + ROUND_CAP, one_round(*state)[0]

    unused, summed = lax.while_loop(unfinished, further, (jnp.int32(ROUND_CAP), summed))
    return summed.reshape(1, 1, kept, order, order)


def solution(mesh):
    in_specs = (
        P("row", GROUP, None, None, None, None),
        P("row", GROUP, None, None),
        P("row", GROUP, None, None),
        P("row", GROUP, None),
        P("row", "col", None, None),
        P("row", "col", None, None),
    )
    out_specs = P("row", GROUP, None, None, None)
    return jax.shard_map(local, mesh=mesh, in_specs=in_specs, out_specs=out_specs, check_vma=False)
```

```python
import functools

import jax
import jax.numpy as jnp
from jax import lax
from jax.experimental import pallas as pl
from jax.experimental.pallas import tpu as pltpu
from jax.sharding import PartitionSpec as P

GROUP = ("col", "layer")
LANES = 128
SLOT_PITCH = 16
PER_GROUP = LANES // SLOT_PITCH
ROUND_CAP = 20
TOGETHER = 2
LIMIT = pltpu.CompilerParams(vmem_limit_bytes=20 * 2**20)
HBM = pl.BlockSpec(memory_space=pltpu.HBM)


def in_hbm(*arrays):
    return [pltpu.with_memory_space_constraint(array, pltpu.HBM) for array in arrays]


def padded(size, unit):
    return unit * pl.cdiv(size, unit)


def label_body(*refs):
    sources, listed_ref, wanted_ref, sems, copies = refs[:5], refs[5], refs[6], refs[7], refs[8:]
    moves = [pltpu.make_async_copy(a, b, sems.at[n]) for n, (a, b) in enumerate(zip(sources, copies))]
    for move in moves:
        move.start()
    for move in moves:
        move.wait()
    tile_rows, tile_cols, counts, out_rows, out_cols = copies
    lists, capacity = tile_rows.shape[2:]
    row_index, layer_index = lax.axis_index("row"), lax.axis_index("layer")
    in_group = lax.axis_index(GROUP) % PER_GROUP
    lane = lax.broadcasted_iota(jnp.int32, (1, LANES), 1)
    nothing = jnp.zeros((1, LANES), jnp.int32)
    rows, cols, kept_rows, kept_cols = nothing, nothing, nothing, nothing
    mate_rows, mate_cols = nothing, nothing
    for at in range(lists):
        for slot in range(capacity):
            live = slot < counts[0, 0, at]
            here = lane == jnp.where(live, row_index * SLOT_PITCH + at * capacity + slot, -1)
            rows = jnp.where(here, tile_rows[0, 0, at, slot] + 1, rows)
            cols = jnp.where(here, tile_cols[0, 0, at, slot] + 1, cols)
    for at in range(out_rows.shape[3]):
        target_row, target_col = out_rows[0, 0, layer_index, at] + 1, out_cols[0, 0, layer_index, at] + 1
        here = lane == in_group * SLOT_PITCH + at
        kept_rows = jnp.where(here, target_row, kept_rows)
        kept_cols = jnp.where(here, target_col, kept_cols)
        here = lane == row_index * SLOT_PITCH + at
        mate_rows = jnp.where(here, target_row, mate_rows)
        mate_cols = jnp.where(here, target_col, mate_cols)
    listed_ref[...] = jnp.concatenate([rows, cols, mate_rows, mate_cols]).astype(jnp.float32)
    wanted_ref[...] = jnp.concatenate([kept_rows, kept_cols]).astype(jnp.float32)


def label(tile_rows, tile_cols, tile_counts, out_rows, out_cols):
    operands = (tile_rows, tile_cols, tile_counts, out_rows, out_cols)
    return pl.pallas_call(
        label_body,
        in_specs=[HBM] * 5,
        out_shape=[jax.ShapeDtypeStruct((n, LANES), jnp.float32) for n in (4, 2)],
        scratch_shapes=[pltpu.SemaphoreType.DMA((5,))] + [pltpu.SMEM(x.shape, jnp.int32) for x in operands],
        compiler_params=LIMIT,
    )(*in_hbm(*operands))


def pack_body(tiles_hbm, out_ref, tiles, sems):
    peers, per_peer, strip, _ = out_ref.shape
    for tile in range(per_peer - 1):
        pltpu.make_async_copy(tiles_hbm.at[tile], tiles.at[tile], sems.at[tile]).start()

    def one_tile(tile, carry):
        pltpu.make_async_copy(tiles_hbm.at[tile], tiles.at[tile], sems.at[tile]).wait()
        for peer in range(peers):
            out_ref[peer, tile] = tiles[tile, peer * strip:(peer + 1) * strip, :]
        return carry

    lax.fori_loop(0, per_peer - 1, one_tile, 0)


def pack(tiles, peers):
    count, order = tiles.shape[:2]
    shape = (peers, count + 1, order // peers, order)
    return pl.pallas_call(
        pack_body,
        in_specs=[HBM],
        out_shape=pltpu.HBM(shape, jnp.float32),
        scratch_shapes=[pltpu.VMEM(tiles.shape, jnp.float32), pltpu.SemaphoreType.DMA((count,))],
        compiler_params=LIMIT,
    )(*in_hbm(tiles))


def stamp_body(one_ref, other_ref, wanted_ref, strips_in, strips_out, total_ref, meta, sem):
    peers, per_peer = strips_out.shape[:2]
    total = one_ref[...] + other_ref[...]
    total_ref[...] = total
    full = jnp.concatenate([total[0:2, :], wanted_ref[...]])
    for peer in range(peers):
        meta[peer] = full
    copy = pltpu.make_async_copy(meta, strips_out.at[:, per_peer - 1], sem)
    copy.start()
    copy.wait()


def stamp(one, other, wanted, strips):
    peers, _, strip, order = strips.shape
    vmem = pl.BlockSpec(memory_space=pltpu.VMEM)
    return pl.pallas_call(
        stamp_body,
        in_specs=[vmem, vmem, vmem, HBM],
        out_specs=[HBM, vmem],
        out_shape=[pltpu.HBM(strips.shape, jnp.float32), jax.ShapeDtypeStruct(one.shape, jnp.float32)],
        input_output_aliases={3: 0},
        scratch_shapes=[pltpu.VMEM((peers, strip, order), jnp.float32), pltpu.SemaphoreType.DMA],
        compiler_params=LIMIT,
    )(one, other, wanted, *in_hbm(strips))


def pack_right_body(tiles_ref, *out_refs):
    count, strip, _ = out_refs[0].shape
    row_index = lax.axis_index("row")
    for away, out_ref in enumerate(out_refs):
        start = pl.multiple_of((row_index + away) % len(out_refs) * strip, strip)
        for tile in range(count):
            out_ref[tile] = tiles_ref[tile, pl.ds(start, strip), :]


def pack_right(tiles, rows):
    count, order = tiles.shape[:2]
    shape = (count, order // rows, order)
    return pl.pallas_call(
        pack_right_body, out_shape=[jax.ShapeDtypeStruct(shape, jnp.float32)] * rows, compiler_params=LIMIT
    )(*in_hbm(tiles))


def list_products(by_col, by_row, targets, value_of, base, cap, values, keys, picks):
    blocks = by_col.shape[0]
    groups = len(targets)
    bands = values.shape[0] // groups
    deep = picks.shape[0] // groups
    f32, bf16 = jnp.float32, jnp.bfloat16
    iota = functools.partial(lax.broadcasted_iota, jnp.int32)
    one, zero = jnp.ones((blocks, LANES), bf16), jnp.zeros((blocks, LANES), bf16)
    tall = (iota((blocks, LANES), 0) + 1).astype(f32).astype(bf16)
    below = jnp.where(iota((bands, bands), 0) >= iota((bands, bands), 1), 1.0, 0.0).astype(bf16)
    lane_from, lane_to = iota((LANES, LANES), 0), iota((LANES, LANES), 1)
    same_peer = lane_from // SLOT_PITCH == lane_to // SLOT_PITCH
    earlier = jnp.where(same_peer & (lane_from < lane_to), 1.0, 0.0).astype(bf16)
    together = jnp.where(same_peer, 1.0, 0.0)

    everything = []
    for group, (target_rows, target_cols) in enumerate(targets):
        def hot(target):
            few = jnp.broadcast_to(target, (16, LANES)).astype(bf16)
            return jnp.where(tall == jnp.concatenate([few] * (blocks // 16), axis=0), one, zero)

        left = jnp.dot(by_col, hot(target_rows), preferred_element_type=f32)
        right = jnp.dot(by_row, hot(target_cols), preferred_element_type=f32)
        pair = jnp.where(left * right > 0.0, left + right * 512.0, 0.0)
        name = pair[0:bands, :]
        for place in range(1, blocks // bands):
            name = name + pair[place * bands:(place + 1) * bands, :]
        hit = name > 0.0
        ranks = jnp.dot(below, jnp.where(hit, 1.0, 0.0).astype(bf16), preferred_element_type=f32)
        everything.append(ranks[bands - 1:bands, :])
        keys[group * bands:(group + 1) * bands, :] = jnp.where(hit, ranks, 0.0)
        values[group * bands:(group + 1) * bands, :] = value_of(name)
    found = jnp.concatenate(everything + everything[-1:] * (8 - len(everything)), axis=0)
    ahead = jnp.dot(found.astype(bf16), earlier, preferred_element_type=f32) - base.astype(f32)
    counts = jnp.dot(found.astype(bf16), together.astype(bf16), preferred_element_type=f32)
    picks[...] = jnp.zeros_like(picks)
    depth = jnp.max(found).astype(jnp.int32)
    slot_at = iota((deep, LANES), 0).astype(f32)

    def one_depth(level, carry):
        level_f = level.astype(f32)
        for group in range(groups):
            span = slice(group * bands, (group + 1) * bands)
            value = jnp.sum(jnp.where(keys[span, :] == level_f + 1.0, values[span, :], 0.0), axis=0, keepdims=True)
            place = jnp.where(found[group:group + 1, :] > level_f, ahead[group:group + 1, :] + level_f, -1.0)
            span = slice(group * deep, (group + 1) * deep)
            picks[span, :] = picks[span, :] + jnp.where(slot_at == place, value, 0.0)
        return carry

    lax.fori_loop(0, depth, one_depth, 0)
    spread = jnp.dot(picks[...], together, precision=lax.Precision.HIGHEST, preferred_element_type=f32)
    mine = iota((deep, LANES), 0) % SLOT_PITCH == iota((deep, LANES), 1) % SLOT_PITCH
    lines = []
    for group in range(groups):
        chosen = jnp.where(mine, spread[group * deep:(group + 1) * deep, :], 0.0)
        for half in range(pl.cdiv(cap, SLOT_PITCH)):
            lines.append(jnp.sum(chosen[half * SLOT_PITCH:(half + 1) * SLOT_PITCH, :], axis=0, keepdims=True))
    return lines, counts


def plan_body(
    rows, base_ref, strips_ref,
    send_ref, codes_ref, counts_ref, peak_ref, by_col_ref, by_row_ref,
    table, values, keys, picks, places_vmem, send, places, sem, send_sems,
):
    row_index, base = lax.axis_index("row"), base_ref[0]
    peers, cap = send_ref.shape[:2]
    per_peer = strips_ref.shape[0] // peers
    band = 8
    blocks = peers * band
    band_rows = blocks // rows
    groups = peers // PER_GROUP
    halves = pl.cdiv(cap, SLOT_PITCH)
    f32, bf16 = jnp.float32, jnp.bfloat16
    iota = functools.partial(lax.broadcasted_iota, jnp.int32)

    in_band = iota((band_rows, LANES), 0).astype(f32)
    band_start = (iota((1, LANES), 1) // SLOT_PITCH * band_rows + 1).astype(f32)
    band_mask = jnp.where(iota((blocks, LANES), 0) // band_rows == iota((blocks, LANES), 1) // SLOT_PITCH, 1.0, 0.0)
    band_mask = band_mask.astype(bf16)
    short = iota((band, LANES), 0).astype(f32) + 1.0
    names = iota((band, LANES), 1).astype(f32) + 1.0
    targets = []
    for peer in range(peers):
        meta = strips_ref[peer * per_peer + per_peer - 1]
        row_hot = jnp.where(in_band == meta[0:1, :] - band_start, 1.0, 0.0).astype(bf16)
        row_hot = jnp.concatenate([row_hot] * rows, axis=0) * band_mask
        col_hot = jnp.where(short + float(peer * band) == meta[1:2, :], names, 0.0).astype(bf16)
        table[peer * band:(peer + 1) * band, :] = lax.dot_general(
            col_hot, row_hot, (((1,), (1,)), ((), ())), preferred_element_type=f32
        )
        if peer % PER_GROUP == 0:
            targets.append(meta)
        else:
            targets[-1] = targets[-1] + meta
    by_index = table[...].astype(bf16)
    index = iota((blocks, blocks), 0)
    order = jnp.where(index % peers * band + index // peers == iota((blocks, blocks), 1), 1.0, 0.0).astype(bf16)
    by_col = jnp.dot(order, by_index, preferred_element_type=f32).astype(bf16)
    by_row = lax.dot_general(order, by_index, (((1,), (1,)), ((), ())), preferred_element_type=f32).astype(bf16)
    by_col_ref[...] = by_col
    by_row_ref[...] = by_row

    fixed = iota((peers, LANES), 0) * per_peer + ((iota((peers, LANES), 1) % SLOT_PITCH) << 16)
    fixed = (fixed - (SLOT_PITCH * row_index + 1 + 512)).astype(f32)
    lines, counts = list_products(
        by_col, by_row, [(meta[2:3, :], meta[3:4, :]) for meta in targets],
        lambda name: name + fixed, base, cap, values, keys, picks,
    )
    codes = jnp.concatenate(lines, axis=0).astype(jnp.int32)
    places_vmem[...] = codes & 511
    copy = pltpu.make_async_copy(places_vmem, places, sem)
    copy.start()
    codes_ref[...] = codes
    counts_ref[...] = counts.astype(jnp.int32)
    longest = jnp.max(jnp.max(counts[0:groups, :], axis=0, keepdims=True), axis=1, keepdims=True)
    peak_ref[...] = jnp.broadcast_to(longest, (8, LANES))
    copy.wait()

    def one_group(group):
        part = pl.ds(group * PER_GROUP, PER_GROUP)
        return pltpu.make_async_copy(send.at[part], send_ref.at[part], send_sems.at[group])

    for group in range(groups):
        for peer in range(group * PER_GROUP, (group + 1) * PER_GROUP):
            line, first = group * halves, peer % PER_GROUP * SLOT_PITCH
            for at in range(cap):
                send[peer, at] = strips_ref[places[line + at // SLOT_PITCH, first + at % SLOT_PITCH]]
        one_group(group).start()
    for group in range(groups):
        one_group(group).wait()


def whole(shape):
    return pl.BlockSpec(shape, lambda i, *_: (0,) * len(shape))


def list_scratch(groups, peers, cap):
    lists = pltpu.VMEM((groups * peers, LANES), jnp.float32)
    return [lists, lists, pltpu.VMEM((groups * padded(cap, 8), LANES), jnp.float32)]


def plan(strips, base, rows, peers, cap):
    strip, order = strips.shape[1:]
    groups = peers // PER_GROUP
    lines = groups * pl.cdiv(cap, SLOT_PITCH)
    send = (peers, cap, strip, order)
    blocks = peers * 8
    shapes = [
        (send, jnp.float32), ((lines, LANES), jnp.int32), ((8, LANES), jnp.int32), ((8, LANES), jnp.float32),
        ((blocks, blocks), jnp.bfloat16), ((blocks, blocks), jnp.bfloat16),
    ]
    return pl.pallas_call(
        functools.partial(plan_body, rows),
        grid_spec=pltpu.PrefetchScalarGridSpec(
            num_scalar_prefetch=1,
            grid=(1,),
            in_specs=[whole(strips.shape)],
            out_specs=[HBM] + [whole(shape) for shape, _ in shapes[1:]],
            scratch_shapes=[
                pltpu.VMEM((blocks, blocks), jnp.float32),
                *list_scratch(groups, peers, cap),
                pltpu.VMEM((lines, LANES), jnp.int32),
                pltpu.VMEM(send, jnp.float32),
                pltpu.SMEM((lines, LANES), jnp.int32),
                pltpu.SemaphoreType.DMA,
                pltpu.SemaphoreType.DMA((groups,)),
            ],
        ),
        out_shape=[pltpu.HBM(*shapes[0])] + [jax.ShapeDtypeStruct(*shape) for shape in shapes[1:]],
        compiler_params=LIMIT,
    )(base.reshape(1), pltpu.with_memory_space_constraint(strips, pltpu.VMEM))


def collect_body(rows, base_ref, by_col_ref, by_row_ref, mates_ref, peak_ref, *refs):
    piece_refs, right_refs = refs[:rows], refs[rows:2 * rows]
    values, keys, picks, places_vmem, panel, places, sem = refs[2 * rows:]
    row_index = lax.axis_index("row")
    count, strip, _ = piece_refs[0].shape
    cap = right_refs[0].shape[0] - 1

    def place_of(name):
        name = (name.astype(jnp.int32) >> 9) - 1
        return (name - (SLOT_PITCH - count) * (name >> 4)).astype(jnp.float32)

    lines, _ = list_products(
        by_col_ref[...], by_row_ref[...], [(mates_ref[2:3, :], mates_ref[3:4, :])],
        place_of, base_ref[0], cap, values, keys, picks,
    )
    lines += lines[-1:] * (places_vmem.shape[0] - len(lines))
    places_vmem[...] = jnp.concatenate(lines, axis=0).astype(jnp.int32)
    copy = pltpu.make_async_copy(places_vmem, places, sem)
    copy.start()
    for away, piece_ref in enumerate(piece_refs):
        start = (row_index + rows - away) % rows * count
        for tile in range(count):
            panel[start + tile] = piece_ref[tile]
    copy.wait()
    for away, right_ref in enumerate(right_refs):
        lane = (row_index + away) % rows * SLOT_PITCH
        for at in range(cap):
            right_ref[at] = panel[places[at // SLOT_PITCH, lane + at % SLOT_PITCH]]
        right_ref[cap, 0:8, :] = peak_ref[...]
        right_ref[cap, 8:16, :] = peak_ref[...]


def collect(tables, mates, peak, pieces, base, peers, cap):
    rows = len(pieces)
    count, strip, order = pieces[0].shape
    right = (cap + 1, strip, order)
    operands = (*tables, mates, peak, *pieces)
    return pl.pallas_call(
        functools.partial(collect_body, rows),
        grid_spec=pltpu.PrefetchScalarGridSpec(
            num_scalar_prefetch=1,
            grid=(1,),
            in_specs=[whole(operand.shape) for operand in operands],
            out_specs=[whole(right)] * rows,
            scratch_shapes=[
                *list_scratch(1, peers, cap),
                pltpu.VMEM((8, LANES), jnp.int32),
                pltpu.VMEM((rows * count, strip, order), jnp.float32),
                pltpu.SMEM((8, LANES), jnp.int32),
                pltpu.SemaphoreType.DMA,
            ],
        ),
        out_shape=[jax.ShapeDtypeStruct(right, jnp.float32)] * rows,
        compiler_params=LIMIT,
    )(base.reshape(1), *tables, mates, peak, *in_hbm(*pieces))


def peak_body(*refs):
    *right_refs, most_ref = refs
    cap = right_refs[0].shape[0] - 1
    most = right_refs[0][cap, 0:8, :]
    for right_ref in right_refs[1:]:
        most = jnp.maximum(most, right_ref[cap, 0:8, :])
    most_ref[...] = most.astype(jnp.int32)


def product_body(first, rows, scalars, codes, counts, left_ref, *refs):
    right_refs, refs = refs[:rows], refs[rows:]
    out_ref, right = refs[-2:]
    out_ref[...] = jnp.zeros_like(out_ref) if first else refs[0][...]
    row_index, own, base = lax.axis_index("row"), lax.axis_index(GROUP), scalars[0]
    peers, cap = left_ref.shape[:2]
    tall_strip = right_refs[0].shape[1]
    line = (own >> 3) * pl.cdiv(cap, SLOT_PITCH)
    lane = (own & (PER_GROUP - 1)) * SLOT_PITCH
    todo = jnp.clip(counts[own >> 3, lane] - base, 0, cap)
    bf16 = jnp.bfloat16

    def product(at, half):
        for away, right_ref in enumerate(right_refs):
            start = pl.multiple_of((row_index + rows - away) % rows * tall_strip, tall_strip)
            right[half, pl.ds(start, tall_strip), :] = right_ref[at]
        a, b = jnp.concatenate([left_ref[peer, at] for peer in range(peers)], axis=0), right[half]
        a_high, b_high = a.astype(bf16), b.astype(bf16)
        a_low = (a - a_high.astype(jnp.float32)).astype(bf16)
        b_low = (b - b_high.astype(jnp.float32)).astype(bf16)
        return jnp.dot(
            jnp.concatenate([a_high, a_low, a_high], axis=1),
            jnp.concatenate([b_high, b_high, b_low], axis=0),
            preferred_element_type=jnp.float32,
        )

    def target(at):
        return codes[line + (at >> 4), lane + (at & (SLOT_PITCH - 1))] >> 16

    def several(step, carry):
        at = TOGETHER * step
        sums = [product(at + n, n) for n in range(TOGETHER)]
        out_ref[target(at)] += sums[0]
        for n in range(1, TOGETHER):
            @pl.when(at + n < todo)
            def _():
                out_ref[target(at + n)] += sums[n]

        return carry

    lax.fori_loop(0, (todo + TOGETHER - 1) // TOGETHER, several, 0)


def multiply_round(left, right, codes, counts, base, running, kept):
    order = left.shape[-1]
    first = running is None
    tiles = (kept, order, order)
    most = pl.pallas_call(
        peak_body, out_shape=jax.ShapeDtypeStruct((8, LANES), jnp.int32), compiler_params=LIMIT
    )(*right)[0, 0]
    operands = [pltpu.with_memory_space_constraint(x, pltpu.VMEM) for x in (left, *right)] + ([] if first else [running])
    summed = pl.pallas_call(
        functools.partial(product_body, first, len(right)),
        grid_spec=pltpu.PrefetchScalarGridSpec(
            num_scalar_prefetch=3,
            grid=(1,),
            in_specs=[whole(operand.shape) for operand in operands],
            out_specs=whole(tiles),
            scratch_shapes=[pltpu.VMEM((TOGETHER, order, order), jnp.float32)],
        ),
        out_shape=jax.ShapeDtypeStruct(tiles, jnp.float32),
        compiler_params=LIMIT,
    )(jnp.stack([base, most]), codes, counts, *operands)
    return summed, most


def shift_all(pieces):
    rows = len(pieces)
    return [pieces[0]] + [
        lax.ppermute(pieces[by], "row", [(i, (i + by) % rows) for i in range(rows)]) for by in range(1, rows)
    ]


def swap_rows(array, rows, by):
    return lax.ppermute(array, "row", [(i, i ^ by) for i in range(rows)])


def local(tile_values, tile_rows, tile_cols, tile_counts, out_rows, out_cols):
    order = tile_values.shape[-1]
    kept = out_rows.shape[-1]
    rows = lax.axis_size("row")
    peers = lax.axis_size(GROUP)
    tiles = tile_values.reshape(-1, order, order)

    listed, wanted = label(tile_rows, tile_cols, tile_counts, out_rows, out_cols)
    for by in (1, 2):
        listed = listed + swap_rows(listed, rows, by)
    listed, strips = lax.optimization_barrier((listed, pack(tiles, peers)))
    strips, mates = stamp(listed, swap_rows(listed, rows, rows - 2), wanted, strips)
    pieces = shift_all(pack_right(tiles, rows))
    strips = lax.all_to_all(strips, GROUP, 0, 0, tiled=True)
    strips, pieces = lax.optimization_barrier((strips, pieces))
    strips = strips.reshape(-1, order // peers, order)

    def one_round(base, running):
        send, codes, counts, peak, *tables = plan(strips, base, rows, peers, ROUND_CAP)
        left = lax.all_to_all(send, GROUP, 0, 0, tiled=True)
        right = shift_all(collect(tables, mates, peak, pieces, base, peers, ROUND_CAP))
        return multiply_round(left, right, codes, counts, base, running, kept)

    summed, most = one_round(jnp.zeros((), jnp.int32), None)

    def unfinished(state):
        return state[0] < most

    def further(state):
        return state[0] + ROUND_CAP, one_round(*state)[0]

    unused, summed = lax.while_loop(unfinished, further, (jnp.int32(ROUND_CAP), summed))
    return summed.reshape(1, 1, kept, order, order)


def solution(mesh):
    in_specs = (
        P("row", GROUP, None, None, None, None),
        P("row", GROUP, None, None),
        P("row", GROUP, None, None),
        P("row", GROUP, None),
        P("row", "col", None, None),
        P("row", "col", None, None),
    )
    out_specs = P("row", GROUP, None, None, None)
    return jax.shard_map(local, mesh=mesh, in_specs=in_specs, out_specs=out_specs, check_vma=False)
```

```python
import functools

import jax
import jax.numpy as jnp
from jax import lax
from jax.experimental import pallas as pl
from jax.experimental.pallas import tpu as pltpu
from jax.sharding import PartitionSpec as P

GROUP = ("col", "layer")
LANES = 128
SLOT_PITCH = 16
PER_GROUP = LANES // SLOT_PITCH
ROUND_CAP = 20
TOGETHER = 2
LIMIT = pltpu.CompilerParams(vmem_limit_bytes=20 * 2**20)
HBM = pl.BlockSpec(memory_space=pltpu.HBM)


def in_hbm(*arrays):
    return [pltpu.with_memory_space_constraint(array, pltpu.HBM) for array in arrays]


def padded(size, unit):
    return unit * pl.cdiv(size, unit)


def label_body(*refs):
    sources, listed_ref, wanted_ref, sems, copies = refs[:5], refs[5], refs[6], refs[7], refs[8:]
    moves = [pltpu.make_async_copy(a, b, sems.at[n]) for n, (a, b) in enumerate(zip(sources, copies))]
    for move in moves:
        move.start()
    for move in moves:
        move.wait()
    tile_rows, tile_cols, counts, out_rows, out_cols = copies
    lists, capacity = tile_rows.shape[2:]
    row_index, layer_index = lax.axis_index("row"), lax.axis_index("layer")
    in_group = lax.axis_index(GROUP) % PER_GROUP
    lane = lax.broadcasted_iota(jnp.int32, (1, LANES), 1)
    nothing = jnp.zeros((1, LANES), jnp.int32)
    rows, cols, kept_rows, kept_cols = nothing, nothing, nothing, nothing
    mate_rows, mate_cols = nothing, nothing
    for at in range(lists):
        for slot in range(capacity):
            live = slot < counts[0, 0, at]
            here = lane == jnp.where(live, row_index * SLOT_PITCH + at * capacity + slot, -1)
            rows = jnp.where(here, tile_rows[0, 0, at, slot] + 1, rows)
            cols = jnp.where(here, tile_cols[0, 0, at, slot] + 1, cols)
    for at in range(out_rows.shape[3]):
        target_row, target_col = out_rows[0, 0, layer_index, at] + 1, out_cols[0, 0, layer_index, at] + 1
        here = lane == in_group * SLOT_PITCH + at
        kept_rows = jnp.where(here, target_row, kept_rows)
        kept_cols = jnp.where(here, target_col, kept_cols)
        here = lane == row_index * SLOT_PITCH + at
        mate_rows = jnp.where(here, target_row, mate_rows)
        mate_cols = jnp.where(here, target_col, mate_cols)
    listed_ref[...] = jnp.concatenate([rows, cols, mate_rows, mate_cols]).astype(jnp.float32)
    wanted_ref[...] = jnp.concatenate([kept_rows, kept_cols]).astype(jnp.float32)


def label(tile_rows, tile_cols, tile_counts, out_rows, out_cols):
    operands = (tile_rows, tile_cols, tile_counts, out_rows, out_cols)
    return pl.pallas_call(
        label_body,
        in_specs=[HBM] * 5,
        out_shape=[jax.ShapeDtypeStruct((n, LANES), jnp.float32) for n in (4, 2)],
        scratch_shapes=[pltpu.SemaphoreType.DMA((5,))] + [pltpu.SMEM(x.shape, jnp.int32) for x in operands],
        compiler_params=LIMIT,
    )(*in_hbm(*operands))


def pack_body(tiles_hbm, out_ref, tiles, sems):
    peers, per_peer, strip, _ = out_ref.shape
    for tile in range(per_peer - 1):
        pltpu.make_async_copy(tiles_hbm.at[tile], tiles.at[tile], sems.at[tile]).start()

    def one_tile(tile, carry):
        pltpu.make_async_copy(tiles_hbm.at[tile], tiles.at[tile], sems.at[tile]).wait()
        for peer in range(peers):
            out_ref[peer, tile] = tiles[tile, peer * strip:(peer + 1) * strip, :]
        return carry

    lax.fori_loop(0, per_peer - 1, one_tile, 0)


def pack(tiles, peers):
    count, order = tiles.shape[:2]
    shape = (peers, count + 1, order // peers, order)
    return pl.pallas_call(
        pack_body,
        in_specs=[HBM],
        out_shape=pltpu.HBM(shape, jnp.float32),
        scratch_shapes=[pltpu.VMEM(tiles.shape, jnp.float32), pltpu.SemaphoreType.DMA((count,))],
        compiler_params=LIMIT,
    )(*in_hbm(tiles))


def stamp_body(*refs):
    *listed_refs, wanted_ref, strips_in, strips_out, total_ref, meta, sem = refs
    peers, per_peer = strips_out.shape[:2]
    total = listed_refs[0][...]
    for listed_ref in listed_refs[1:]:
        total = total + listed_ref[...]
    total_ref[...] = total
    full = jnp.concatenate([total[0:2, :], wanted_ref[...]])
    for peer in range(peers):
        meta[peer] = full
    copy = pltpu.make_async_copy(meta, strips_out.at[:, per_peer - 1], sem)
    copy.start()
    copy.wait()


def stamp(listed, wanted, strips):
    peers, _, strip, order = strips.shape
    vmem = pl.BlockSpec(memory_space=pltpu.VMEM)
    small = [*listed, wanted]
    return pl.pallas_call(
        stamp_body,
        in_specs=[vmem] * len(small) + [HBM],
        out_specs=[HBM, vmem],
        out_shape=[pltpu.HBM(strips.shape, jnp.float32), jax.ShapeDtypeStruct(listed[0].shape, jnp.float32)],
        input_output_aliases={len(small): 0},
        scratch_shapes=[pltpu.VMEM((peers, strip, order), jnp.float32), pltpu.SemaphoreType.DMA],
        compiler_params=LIMIT,
    )(*small, *in_hbm(strips))


def pack_right_body(tiles_ref, *out_refs):
    count, strip, _ = out_refs[0].shape
    row_index = lax.axis_index("row")
    for away, out_ref in enumerate(out_refs):
        start = pl.multiple_of((row_index + away) % len(out_refs) * strip, strip)
        for tile in range(count):
            out_ref[tile] = tiles_ref[tile, pl.ds(start, strip), :]


def pack_right(tiles, rows):
    count, order = tiles.shape[:2]
    shape = (count, order // rows, order)
    return pl.pallas_call(
        pack_right_body, out_shape=[jax.ShapeDtypeStruct(shape, jnp.float32)] * rows, compiler_params=LIMIT
    )(*in_hbm(tiles))


def list_products(by_col, by_row, targets, value_of, base, cap, values, keys, picks):
    blocks = by_col.shape[0]
    groups = len(targets)
    bands = values.shape[0] // groups
    deep = picks.shape[0] // groups
    f32, bf16 = jnp.float32, jnp.bfloat16
    iota = functools.partial(lax.broadcasted_iota, jnp.int32)
    one, zero = jnp.ones((blocks, LANES), bf16), jnp.zeros((blocks, LANES), bf16)
    tall = (iota((blocks, LANES), 0) + 1).astype(f32).astype(bf16)
    below = jnp.where(iota((bands, bands), 0) >= iota((bands, bands), 1), 1.0, 0.0).astype(bf16)
    lane_from, lane_to = iota((LANES, LANES), 0), iota((LANES, LANES), 1)
    same_peer = lane_from // SLOT_PITCH == lane_to // SLOT_PITCH
    earlier = jnp.where(same_peer & (lane_from < lane_to), 1.0, 0.0).astype(bf16)
    together = jnp.where(same_peer, 1.0, 0.0)

    everything = []
    for group, (target_rows, target_cols) in enumerate(targets):
        def hot(target):
            few = jnp.broadcast_to(target, (16, LANES)).astype(bf16)
            return jnp.where(tall == jnp.concatenate([few] * (blocks // 16), axis=0), one, zero)

        left = jnp.dot(by_col, hot(target_rows), preferred_element_type=f32)
        right = jnp.dot(by_row, hot(target_cols), preferred_element_type=f32)
        pair = jnp.where(left * right > 0.0, left + right * 512.0, 0.0)
        name = pair[0:bands, :]
        for place in range(1, blocks // bands):
            name = name + pair[place * bands:(place + 1) * bands, :]
        hit = name > 0.0
        ranks = jnp.dot(below, jnp.where(hit, 1.0, 0.0).astype(bf16), preferred_element_type=f32)
        everything.append(ranks[bands - 1:bands, :])
        keys[group * bands:(group + 1) * bands, :] = jnp.where(hit, ranks, 0.0)
        values[group * bands:(group + 1) * bands, :] = value_of(name)
    found = jnp.concatenate(everything + everything[-1:] * (8 - len(everything)), axis=0)
    ahead = jnp.dot(found.astype(bf16), earlier, preferred_element_type=f32) - base.astype(f32)
    counts = jnp.dot(found.astype(bf16), together.astype(bf16), preferred_element_type=f32)
    picks[...] = jnp.zeros_like(picks)
    depth = jnp.max(found).astype(jnp.int32)
    slot_at = iota((deep, LANES), 0).astype(f32)

    def one_depth(level, carry):
        level_f = level.astype(f32)
        for group in range(groups):
            span = slice(group * bands, (group + 1) * bands)
            value = jnp.sum(jnp.where(keys[span, :] == level_f + 1.0, values[span, :], 0.0), axis=0, keepdims=True)
            place = jnp.where(found[group:group + 1, :] > level_f, ahead[group:group + 1, :] + level_f, -1.0)
            span = slice(group * deep, (group + 1) * deep)
            picks[span, :] = picks[span, :] + jnp.where(slot_at == place, value, 0.0)
        return carry

    lax.fori_loop(0, depth, one_depth, 0)
    spread = jnp.dot(picks[...], together, precision=lax.Precision.HIGHEST, preferred_element_type=f32)
    mine = iota((deep, LANES), 0) % SLOT_PITCH == iota((deep, LANES), 1) % SLOT_PITCH
    lines = []
    for group in range(groups):
        chosen = jnp.where(mine, spread[group * deep:(group + 1) * deep, :], 0.0)
        for half in range(pl.cdiv(cap, SLOT_PITCH)):
            lines.append(jnp.sum(chosen[half * SLOT_PITCH:(half + 1) * SLOT_PITCH, :], axis=0, keepdims=True))
    return lines, counts


def plan_body(
    rows, base_ref, strips_ref,
    send_ref, codes_ref, counts_ref, peak_ref, by_col_ref, by_row_ref,
    table, values, keys, picks, places_vmem, send, places, sem, send_sems,
):
    row_index, base = lax.axis_index("row"), base_ref[0]
    peers, cap = send_ref.shape[:2]
    per_peer = strips_ref.shape[0] // peers
    band = 8
    blocks = peers * band
    band_rows = blocks // rows
    groups = peers // PER_GROUP
    halves = pl.cdiv(cap, SLOT_PITCH)
    f32, bf16 = jnp.float32, jnp.bfloat16
    iota = functools.partial(lax.broadcasted_iota, jnp.int32)

    in_band = iota((band_rows, LANES), 0).astype(f32)
    band_start = (iota((1, LANES), 1) // SLOT_PITCH * band_rows + 1).astype(f32)
    band_mask = jnp.where(iota((blocks, LANES), 0) // band_rows == iota((blocks, LANES), 1) // SLOT_PITCH, 1.0, 0.0)
    band_mask = band_mask.astype(bf16)
    short = iota((band, LANES), 0).astype(f32) + 1.0
    names = iota((band, LANES), 1).astype(f32) + 1.0
    targets = []
    for peer in range(peers):
        meta = strips_ref[peer * per_peer + per_peer - 1]
        row_hot = jnp.where(in_band == meta[0:1, :] - band_start, 1.0, 0.0).astype(bf16)
        row_hot = jnp.concatenate([row_hot] * rows, axis=0) * band_mask
        col_hot = jnp.where(short + float(peer * band) == meta[1:2, :], names, 0.0).astype(bf16)
        table[peer * band:(peer + 1) * band, :] = lax.dot_general(
            col_hot, row_hot, (((1,), (1,)), ((), ())), preferred_element_type=f32
        )
        if peer % PER_GROUP == 0:
            targets.append(meta)
        else:
            targets[-1] = targets[-1] + meta
    by_index = table[...].astype(bf16)
    index = iota((blocks, blocks), 0)
    order = jnp.where(index % peers * band + index // peers == iota((blocks, blocks), 1), 1.0, 0.0).astype(bf16)
    by_col = jnp.dot(order, by_index, preferred_element_type=f32).astype(bf16)
    by_row = lax.dot_general(order, by_index, (((1,), (1,)), ((), ())), preferred_element_type=f32).astype(bf16)
    by_col_ref[...] = by_col
    by_row_ref[...] = by_row

    fixed = iota((peers, LANES), 0) * per_peer + ((iota((peers, LANES), 1) % SLOT_PITCH) << 16)
    fixed = (fixed - (SLOT_PITCH * row_index + 1 + 512)).astype(f32)
    lines, counts = list_products(
        by_col, by_row, [(meta[2:3, :], meta[3:4, :]) for meta in targets],
        lambda name: name + fixed, base, cap, values, keys, picks,
    )
    codes = jnp.concatenate(lines, axis=0).astype(jnp.int32)
    places_vmem[...] = codes & 511
    copy = pltpu.make_async_copy(places_vmem, places, sem)
    copy.start()
    codes_ref[...] = codes
    counts_ref[...] = counts.astype(jnp.int32)
    longest = jnp.max(jnp.max(counts[0:groups, :], axis=0, keepdims=True), axis=1, keepdims=True)
    peak_ref[...] = jnp.broadcast_to(longest, (8, LANES))
    copy.wait()

    def one_group(group):
        part = pl.ds(group * PER_GROUP, PER_GROUP)
        return pltpu.make_async_copy(send.at[part], send_ref.at[part], send_sems.at[group])

    for group in range(groups):
        for peer in range(group * PER_GROUP, (group + 1) * PER_GROUP):
            line, first = group * halves, peer % PER_GROUP * SLOT_PITCH
            for at in range(cap):
                send[peer, at] = strips_ref[places[line + at // SLOT_PITCH, first + at % SLOT_PITCH]]
        one_group(group).start()
    for group in range(groups):
        one_group(group).wait()


def whole(shape):
    return pl.BlockSpec(shape, lambda i, *_: (0,) * len(shape))


def list_scratch(groups, peers, cap):
    lists = pltpu.VMEM((groups * peers, LANES), jnp.float32)
    return [lists, lists, pltpu.VMEM((groups * padded(cap, 8), LANES), jnp.float32)]


def plan(strips, base, rows, peers, cap):
    strip, order = strips.shape[1:]
    groups = peers // PER_GROUP
    lines = groups * pl.cdiv(cap, SLOT_PITCH)
    send = (peers, cap, strip, order)
    blocks = peers * 8
    shapes = [
        (send, jnp.float32), ((lines, LANES), jnp.int32), ((8, LANES), jnp.int32), ((8, LANES), jnp.float32),
        ((blocks, blocks), jnp.bfloat16), ((blocks, blocks), jnp.bfloat16),
    ]
    return pl.pallas_call(
        functools.partial(plan_body, rows),
        grid_spec=pltpu.PrefetchScalarGridSpec(
            num_scalar_prefetch=1,
            grid=(1,),
            in_specs=[whole(strips.shape)],
            out_specs=[HBM] + [whole(shape) for shape, _ in shapes[1:]],
            scratch_shapes=[
                pltpu.VMEM((blocks, blocks), jnp.float32),
                *list_scratch(groups, peers, cap),
                pltpu.VMEM((lines, LANES), jnp.int32),
                pltpu.VMEM(send, jnp.float32),
                pltpu.SMEM((lines, LANES), jnp.int32),
                pltpu.SemaphoreType.DMA,
                pltpu.SemaphoreType.DMA((groups,)),
            ],
        ),
        out_shape=[pltpu.HBM(*shapes[0])] + [jax.ShapeDtypeStruct(*shape) for shape in shapes[1:]],
        compiler_params=LIMIT,
    )(base.reshape(1), pltpu.with_memory_space_constraint(strips, pltpu.VMEM))


def collect_body(rows, base_ref, by_col_ref, by_row_ref, mates_ref, peak_ref, *refs):
    piece_refs, right_refs = refs[:rows], refs[rows:2 * rows]
    values, keys, picks, places_vmem, panel, places, sem = refs[2 * rows:]
    row_index = lax.axis_index("row")
    count, strip, _ = piece_refs[0].shape
    cap = right_refs[0].shape[0] - 1

    def place_of(name):
        name = (name.astype(jnp.int32) >> 9) - 1
        return (name - (SLOT_PITCH - count) * (name >> 4)).astype(jnp.float32)

    lines, _ = list_products(
        by_col_ref[...], by_row_ref[...], [(mates_ref[2:3, :], mates_ref[3:4, :])],
        place_of, base_ref[0], cap, values, keys, picks,
    )
    lines += lines[-1:] * (places_vmem.shape[0] - len(lines))
    places_vmem[...] = jnp.concatenate(lines, axis=0).astype(jnp.int32)
    copy = pltpu.make_async_copy(places_vmem, places, sem)
    copy.start()
    for away, piece_ref in enumerate(piece_refs):
        start = (row_index + rows - away) % rows * count
        for tile in range(count):
            panel[start + tile] = piece_ref[tile]
    copy.wait()
    for away, right_ref in enumerate(right_refs):
        lane = (row_index + away) % rows * SLOT_PITCH
        for at in range(cap):
            right_ref[at] = panel[places[at // SLOT_PITCH, lane + at % SLOT_PITCH]]
        right_ref[cap, 0:8, :] = peak_ref[...]
        right_ref[cap, 8:16, :] = peak_ref[...]


def collect(tables, mates, peak, pieces, base, peers, cap):
    rows = len(pieces)
    count, strip, order = pieces[0].shape
    right = (cap + 1, strip, order)
    operands = (*tables, mates, peak, *pieces)
    return pl.pallas_call(
        functools.partial(collect_body, rows),
        grid_spec=pltpu.PrefetchScalarGridSpec(
            num_scalar_prefetch=1,
            grid=(1,),
            in_specs=[whole(operand.shape) for operand in operands],
            out_specs=[whole(right)] * rows,
            scratch_shapes=[
                *list_scratch(1, peers, cap),
                pltpu.VMEM((8, LANES), jnp.int32),
                pltpu.VMEM((rows * count, strip, order), jnp.float32),
                pltpu.SMEM((8, LANES), jnp.int32),
                pltpu.SemaphoreType.DMA,
            ],
        ),
        out_shape=[jax.ShapeDtypeStruct(right, jnp.float32)] * rows,
        compiler_params=LIMIT,
    )(base.reshape(1), *tables, mates, peak, *in_hbm(*pieces))


def peak_body(*refs):
    *right_refs, most_ref = refs
    cap = right_refs[0].shape[0] - 1
    most = right_refs[0][cap, 0:8, :]
    for right_ref in right_refs[1:]:
        most = jnp.maximum(most, right_ref[cap, 0:8, :])
    most_ref[...] = most.astype(jnp.int32)


def product_body(first, rows, scalars, codes, counts, left_ref, *refs):
    right_refs, refs = refs[:rows], refs[rows:]
    out_ref, right = refs[-2:]
    out_ref[...] = jnp.zeros_like(out_ref) if first else refs[0][...]
    row_index, own, base = lax.axis_index("row"), lax.axis_index(GROUP), scalars[0]
    peers, cap = left_ref.shape[:2]
    tall_strip = right_refs[0].shape[1]
    line = (own >> 3) * pl.cdiv(cap, SLOT_PITCH)
    lane = (own & (PER_GROUP - 1)) * SLOT_PITCH
    todo = jnp.clip(counts[own >> 3, lane] - base, 0, cap)
    bf16 = jnp.bfloat16

    def product(at, half):
        for away, right_ref in enumerate(right_refs):
            start = pl.multiple_of((row_index + rows - away) % rows * tall_strip, tall_strip)
            right[half, pl.ds(start, tall_strip), :] = right_ref[at]
        a, b = jnp.concatenate([left_ref[peer, at] for peer in range(peers)], axis=0), right[half]
        a_high, b_high = a.astype(bf16), b.astype(bf16)
        a_low = (a - a_high.astype(jnp.float32)).astype(bf16)
        b_low = (b - b_high.astype(jnp.float32)).astype(bf16)
        return jnp.dot(
            jnp.concatenate([a_high, a_low, a_high], axis=1),
            jnp.concatenate([b_high, b_high, b_low], axis=0),
            preferred_element_type=jnp.float32,
        )

    def target(at):
        return codes[line + (at >> 4), lane + (at & (SLOT_PITCH - 1))] >> 16

    def several(step, carry):
        at = TOGETHER * step
        sums = [product(at + n, n) for n in range(TOGETHER)]
        out_ref[target(at)] += sums[0]
        for n in range(1, TOGETHER):
            @pl.when(at + n < todo)
            def _():
                out_ref[target(at + n)] += sums[n]

        return carry

    lax.fori_loop(0, (todo + TOGETHER - 1) // TOGETHER, several, 0)


def multiply_round(left, right, codes, counts, base, running, kept):
    order = left.shape[-1]
    first = running is None
    tiles = (kept, order, order)
    most = pl.pallas_call(
        peak_body, out_shape=jax.ShapeDtypeStruct((8, LANES), jnp.int32), compiler_params=LIMIT
    )(*right)[0, 0]
    operands = [pltpu.with_memory_space_constraint(x, pltpu.VMEM) for x in (left, *right)] + ([] if first else [running])
    summed = pl.pallas_call(
        functools.partial(product_body, first, len(right)),
        grid_spec=pltpu.PrefetchScalarGridSpec(
            num_scalar_prefetch=3,
            grid=(1,),
            in_specs=[whole(operand.shape) for operand in operands],
            out_specs=whole(tiles),
            scratch_shapes=[pltpu.VMEM((TOGETHER, order, order), jnp.float32)],
        ),
        out_shape=jax.ShapeDtypeStruct(tiles, jnp.float32),
        compiler_params=LIMIT,
    )(jnp.stack([base, most]), codes, counts, *operands)
    return summed, most


def shift_all(pieces):
    rows = len(pieces)
    return [pieces[0]] + [
        lax.ppermute(pieces[by], "row", [(i, (i + by) % rows) for i in range(rows)]) for by in range(1, rows)
    ]


def local(tile_values, tile_rows, tile_cols, tile_counts, out_rows, out_cols):
    order = tile_values.shape[-1]
    kept = out_rows.shape[-1]
    rows = lax.axis_size("row")
    peers = lax.axis_size(GROUP)
    tiles = tile_values.reshape(-1, order, order)

    listed, wanted = label(tile_rows, tile_cols, tile_counts, out_rows, out_cols)
    listed = listed + lax.ppermute(listed, "row", [(i, i ^ 1) for i in range(rows)])
    others = [lax.ppermute(listed, "row", [(i, (i + by) % rows) for i in range(rows)]) for by in range(2, rows, 2)]
    strips, mates = stamp([listed, *others], wanted, pack(tiles, peers))
    pieces = shift_all(pack_right(tiles, rows))
    strips = lax.all_to_all(strips, GROUP, 0, 0, tiled=True)
    strips, pieces = lax.optimization_barrier((strips, pieces))
    strips = strips.reshape(-1, order // peers, order)

    def one_round(base, running):
        send, codes, counts, peak, *tables = plan(strips, base, rows, peers, ROUND_CAP)
        left = lax.all_to_all(send, GROUP, 0, 0, tiled=True)
        right = shift_all(collect(tables, mates, peak, pieces, base, peers, ROUND_CAP))
        return multiply_round(left, right, codes, counts, base, running, kept)

    summed, most = one_round(jnp.zeros((), jnp.int32), None)

    def unfinished(state):
        return state[0] < most

    def further(state):
        return state[0] + ROUND_CAP, one_round(*state)[0]

    unused, summed = lax.while_loop(unfinished, further, (jnp.int32(ROUND_CAP), summed))
    return summed.reshape(1, 1, kept, order, order)


def solution(mesh):
    in_specs = (
        P("row", GROUP, None, None, None, None),
        P("row", GROUP, None, None),
        P("row", GROUP, None, None),
        P("row", GROUP, None),
        P("row", "col", None, None),
        P("row", "col", None, None),
    )
    out_specs = P("row", GROUP, None, None, None)
    return jax.shard_map(local, mesh=mesh, in_specs=in_specs, out_specs=out_specs, check_vma=False)
```

```python
import functools

import jax
import jax.numpy as jnp
from jax import lax
from jax.experimental import pallas as pl
from jax.experimental.pallas import tpu as pltpu
from jax.sharding import PartitionSpec as P

GROUP = ("col", "layer")
LANES = 128
SLOT_PITCH = 16
PER_GROUP = LANES // SLOT_PITCH
ROUND_CAP = 20
TOGETHER = 2
LIMIT = pltpu.CompilerParams(vmem_limit_bytes=20 * 2**20)
HBM = pl.BlockSpec(memory_space=pltpu.HBM)


def in_hbm(*arrays):
    return [pltpu.with_memory_space_constraint(array, pltpu.HBM) for array in arrays]


def padded(size, unit):
    return unit * pl.cdiv(size, unit)


def label_body(*refs):
    sources, listed_ref, wanted_ref, sems, copies = refs[:5], refs[5], refs[6], refs[7], refs[8:]
    moves = [pltpu.make_async_copy(a, b, sems.at[n]) for n, (a, b) in enumerate(zip(sources, copies))]
    for move in moves:
        move.start()
    for move in moves:
        move.wait()
    tile_rows, tile_cols, counts, out_rows, out_cols = copies
    lists, capacity = tile_rows.shape[2:]
    row_index, layer_index = lax.axis_index("row"), lax.axis_index("layer")
    in_group = lax.axis_index(GROUP) % PER_GROUP
    lane = lax.broadcasted_iota(jnp.int32, (1, LANES), 1)
    nothing = jnp.zeros((1, LANES), jnp.int32)
    rows, cols, kept_rows, kept_cols = nothing, nothing, nothing, nothing
    mate_rows, mate_cols = nothing, nothing
    for at in range(lists):
        for slot in range(capacity):
            live = slot < counts[0, 0, at]
            here = lane == jnp.where(live, row_index * SLOT_PITCH + at * capacity + slot, -1)
            rows = jnp.where(here, tile_rows[0, 0, at, slot] + 1, rows)
            cols = jnp.where(here, tile_cols[0, 0, at, slot] + 1, cols)
    for at in range(out_rows.shape[3]):
        target_row, target_col = out_rows[0, 0, layer_index, at] + 1, out_cols[0, 0, layer_index, at] + 1
        here = lane == in_group * SLOT_PITCH + at
        kept_rows = jnp.where(here, target_row, kept_rows)
        kept_cols = jnp.where(here, target_col, kept_cols)
        here = lane == row_index * SLOT_PITCH + at
        mate_rows = jnp.where(here, target_row, mate_rows)
        mate_cols = jnp.where(here, target_col, mate_cols)
    listed_ref[...] = jnp.concatenate([rows, cols, mate_rows, mate_cols]).astype(jnp.float32)
    wanted_ref[...] = jnp.concatenate([kept_rows, kept_cols]).astype(jnp.float32)


def label(tile_rows, tile_cols, tile_counts, out_rows, out_cols):
    operands = (tile_rows, tile_cols, tile_counts, out_rows, out_cols)
    return pl.pallas_call(
        label_body,
        in_specs=[HBM] * 5,
        out_shape=[jax.ShapeDtypeStruct((n, LANES), jnp.float32) for n in (4, 2)],
        scratch_shapes=[pltpu.SemaphoreType.DMA((5,))] + [pltpu.SMEM(x.shape, jnp.int32) for x in operands],
        compiler_params=LIMIT,
    )(*in_hbm(*operands))


def pack_body(tiles_hbm, out_ref, tiles, sems):
    peers, per_peer, strip, _ = out_ref.shape
    for tile in range(per_peer - 1):
        pltpu.make_async_copy(tiles_hbm.at[tile], tiles.at[tile], sems.at[tile]).start()

    def one_tile(tile, carry):
        pltpu.make_async_copy(tiles_hbm.at[tile], tiles.at[tile], sems.at[tile]).wait()
        for peer in range(peers):
            out_ref[peer, tile] = tiles[tile, peer * strip:(peer + 1) * strip, :]
        return carry

    lax.fori_loop(0, per_peer - 1, one_tile, 0)


def pack(tiles, peers):
    count, order = tiles.shape[:2]
    shape = (peers, count + 1, order // peers, order)
    return pl.pallas_call(
        pack_body,
        in_specs=[HBM],
        out_shape=pltpu.HBM(shape, jnp.float32),
        scratch_shapes=[pltpu.VMEM(tiles.shape, jnp.float32), pltpu.SemaphoreType.DMA((count,))],
        compiler_params=LIMIT,
    )(*in_hbm(tiles))


def stamp_body(one_ref, other_ref, wanted_ref, strips_in, strips_out, total_ref, meta, sem):
    peers, per_peer = strips_out.shape[:2]
    total = one_ref[...] + other_ref[...]
    total_ref[...] = total
    full = jnp.concatenate([total[0:2, :], wanted_ref[...]])
    for peer in range(peers):
        meta[peer] = full
    copy = pltpu.make_async_copy(meta, strips_out.at[:, per_peer - 1], sem)
    copy.start()
    copy.wait()


def stamp(one, other, wanted, strips):
    peers, _, strip, order = strips.shape
    vmem = pl.BlockSpec(memory_space=pltpu.VMEM)
    return pl.pallas_call(
        stamp_body,
        in_specs=[vmem, vmem, vmem, HBM],
        out_specs=[HBM, vmem],
        out_shape=[pltpu.HBM(strips.shape, jnp.float32), jax.ShapeDtypeStruct(one.shape, jnp.float32)],
        input_output_aliases={3: 0},
        scratch_shapes=[pltpu.VMEM((peers, strip, order), jnp.float32), pltpu.SemaphoreType.DMA],
        compiler_params=LIMIT,
    )(one, other, wanted, *in_hbm(strips))


def pack_right_body(tiles_ref, *out_refs):
    count, strip, _ = out_refs[0].shape
    row_index = lax.axis_index("row")
    for away, out_ref in enumerate(out_refs):
        start = pl.multiple_of((row_index + away) % len(out_refs) * strip, strip)
        for tile in range(count):
            out_ref[tile] = tiles_ref[tile, pl.ds(start, strip), :]


def pack_right(tiles, rows):
    count, order = tiles.shape[:2]
    shape = (count, order // rows, order)
    return pl.pallas_call(
        pack_right_body, out_shape=[jax.ShapeDtypeStruct(shape, jnp.float32)] * rows, compiler_params=LIMIT
    )(*in_hbm(tiles))


def list_products(by_col, by_row, targets, value_of, base, cap, values, keys, picks):
    blocks = by_col.shape[0]
    groups = len(targets)
    bands = values.shape[0] // groups
    deep = picks.shape[0] // groups
    f32, bf16 = jnp.float32, jnp.bfloat16
    iota = functools.partial(lax.broadcasted_iota, jnp.int32)
    one, zero = jnp.ones((blocks, LANES), bf16), jnp.zeros((blocks, LANES), bf16)
    tall = (iota((blocks, LANES), 0) + 1).astype(f32).astype(bf16)
    below = jnp.where(iota((bands, bands), 0) >= iota((bands, bands), 1), 1.0, 0.0).astype(bf16)
    lane_from, lane_to = iota((LANES, LANES), 0), iota((LANES, LANES), 1)
    same_peer = lane_from // SLOT_PITCH == lane_to // SLOT_PITCH
    earlier = jnp.where(same_peer & (lane_from < lane_to), 1.0, 0.0).astype(bf16)
    together = jnp.where(same_peer, 1.0, 0.0)

    everything = []
    for group, (target_rows, target_cols) in enumerate(targets):
        def hot(target):
            few = jnp.broadcast_to(target, (16, LANES)).astype(bf16)
            return jnp.where(tall == jnp.concatenate([few] * (blocks // 16), axis=0), one, zero)

        left = jnp.dot(by_col, hot(target_rows), preferred_element_type=f32)
        right = jnp.dot(by_row, hot(target_cols), preferred_element_type=f32)
        pair = jnp.where(left * right > 0.0, left + right * 512.0, 0.0)
        name = pair[0:bands, :]
        for place in range(1, blocks // bands):
            name = name + pair[place * bands:(place + 1) * bands, :]
        hit = name > 0.0
        ranks = jnp.dot(below, jnp.where(hit, 1.0, 0.0).astype(bf16), preferred_element_type=f32)
        everything.append(ranks[bands - 1:bands, :])
        keys[group * bands:(group + 1) * bands, :] = jnp.where(hit, ranks, 0.0)
        values[group * bands:(group + 1) * bands, :] = value_of(name)
    found = jnp.concatenate(everything + everything[-1:] * (8 - len(everything)), axis=0)
    ahead = jnp.dot(found.astype(bf16), earlier, preferred_element_type=f32) - base.astype(f32)
    counts = jnp.dot(found.astype(bf16), together.astype(bf16), preferred_element_type=f32)
    picks[...] = jnp.zeros_like(picks)
    depth = jnp.max(found).astype(jnp.int32)
    slot_at = iota((deep, LANES), 0).astype(f32)

    def one_depth(level, carry):
        level_f = level.astype(f32)
        for group in range(groups):
            span = slice(group * bands, (group + 1) * bands)
            value = jnp.sum(jnp.where(keys[span, :] == level_f + 1.0, values[span, :], 0.0), axis=0, keepdims=True)
            place = jnp.where(found[group:group + 1, :] > level_f, ahead[group:group + 1, :] + level_f, -1.0)
            span = slice(group * deep, (group + 1) * deep)
            picks[span, :] = picks[span, :] + jnp.where(slot_at == place, value, 0.0)
        return carry

    lax.fori_loop(0, depth, one_depth, 0)
    spread = jnp.dot(picks[...], together, precision=lax.Precision.HIGHEST, preferred_element_type=f32)
    mine = iota((deep, LANES), 0) % SLOT_PITCH == iota((deep, LANES), 1) % SLOT_PITCH
    lines = []
    for group in range(groups):
        chosen = jnp.where(mine, spread[group * deep:(group + 1) * deep, :], 0.0)
        for half in range(pl.cdiv(cap, SLOT_PITCH)):
            lines.append(jnp.sum(chosen[half * SLOT_PITCH:(half + 1) * SLOT_PITCH, :], axis=0, keepdims=True))
    return lines, counts


def plan_body(
    rows, base_ref, strips_ref,
    send_ref, codes_ref, counts_ref, peak_ref, by_col_ref, by_row_ref,
    table, values, keys, picks, places_vmem, send, places, sem, send_sems,
):
    row_index, base = lax.axis_index("row"), base_ref[0]
    peers, cap = send_ref.shape[:2]
    per_peer = strips_ref.shape[0] // peers
    band = 8
    blocks = peers * band
    band_rows = blocks // rows
    groups = peers // PER_GROUP
    halves = pl.cdiv(cap, SLOT_PITCH)
    f32, bf16 = jnp.float32, jnp.bfloat16
    iota = functools.partial(lax.broadcasted_iota, jnp.int32)

    in_band = iota((band_rows, LANES), 0).astype(f32)
    band_start = (iota((1, LANES), 1) // SLOT_PITCH * band_rows + 1).astype(f32)
    band_mask = jnp.where(iota((blocks, LANES), 0) // band_rows == iota((blocks, LANES), 1) // SLOT_PITCH, 1.0, 0.0)
    band_mask = band_mask.astype(bf16)
    short = iota((band, LANES), 0).astype(f32) + 1.0
    names = iota((band, LANES), 1).astype(f32) + 1.0
    targets = []
    for peer in range(peers):
        meta = strips_ref[peer * per_peer + per_peer - 1]
        row_hot = jnp.where(in_band == meta[0:1, :] - band_start, 1.0, 0.0).astype(bf16)
        row_hot = jnp.concatenate([row_hot] * rows, axis=0) * band_mask
        col_hot = jnp.where(short + float(peer * band) == meta[1:2, :], names, 0.0).astype(bf16)
        table[peer * band:(peer + 1) * band, :] = lax.dot_general(
            col_hot, row_hot, (((1,), (1,)), ((), ())), preferred_element_type=f32
        )
        if peer % PER_GROUP == 0:
            targets.append(meta)
        else:
            targets[-1] = targets[-1] + meta
    by_index = table[...].astype(bf16)
    index = iota((blocks, blocks), 0)
    order = jnp.where(index % peers * band + index // peers == iota((blocks, blocks), 1), 1.0, 0.0).astype(bf16)
    by_col = jnp.dot(order, by_index, preferred_element_type=f32).astype(bf16)
    by_row = lax.dot_general(order, by_index, (((1,), (1,)), ((), ())), preferred_element_type=f32).astype(bf16)
    by_col_ref[...] = by_col
    by_row_ref[...] = by_row

    fixed = iota((peers, LANES), 0) * per_peer + ((iota((peers, LANES), 1) % SLOT_PITCH) << 16)
    fixed = (fixed - (SLOT_PITCH * row_index + 1 + 512)).astype(f32)
    lines, counts = list_products(
        by_col, by_row, [(meta[2:3, :], meta[3:4, :]) for meta in targets],
        lambda name: name + fixed, base, cap, values, keys, picks,
    )
    codes = jnp.concatenate(lines, axis=0).astype(jnp.int32)
    places_vmem[...] = codes & 511
    copy = pltpu.make_async_copy(places_vmem, places, sem)
    copy.start()
    codes_ref[...] = codes
    counts_ref[...] = counts.astype(jnp.int32)
    longest = jnp.max(jnp.max(counts[0:groups, :], axis=0, keepdims=True), axis=1, keepdims=True)
    peak_ref[...] = jnp.broadcast_to(longest, (8, LANES))
    copy.wait()

    def one_group(group):
        part = pl.ds(group * PER_GROUP, PER_GROUP)
        return pltpu.make_async_copy(send.at[part], send_ref.at[part], send_sems.at[group])

    for group in range(groups):
        for peer in range(group * PER_GROUP, (group + 1) * PER_GROUP):
            line, first = group * halves, peer % PER_GROUP * SLOT_PITCH
            for at in range(cap):
                send[peer, at] = strips_ref[places[line + at // SLOT_PITCH, first + at % SLOT_PITCH]]
        one_group(group).start()
    for group in range(groups):
        one_group(group).wait()


def whole(shape):
    return pl.BlockSpec(shape, lambda i, *_: (0,) * len(shape))


def list_scratch(groups, peers, cap):
    lists = pltpu.VMEM((groups * peers, LANES), jnp.float32)
    return [lists, lists, pltpu.VMEM((groups * padded(cap, 8), LANES), jnp.float32)]


def plan(strips, base, rows, peers, cap):
    strip, order = strips.shape[1:]
    groups = peers // PER_GROUP
    lines = groups * pl.cdiv(cap, SLOT_PITCH)
    send = (peers, cap, strip, order)
    blocks = peers * 8
    shapes = [
        (send, jnp.float32), ((lines, LANES), jnp.int32), ((8, LANES), jnp.int32), ((8, LANES), jnp.float32),
        ((blocks, blocks), jnp.bfloat16), ((blocks, blocks), jnp.bfloat16),
    ]
    return pl.pallas_call(
        functools.partial(plan_body, rows),
        grid_spec=pltpu.PrefetchScalarGridSpec(
            num_scalar_prefetch=1,
            grid=(1,),
            in_specs=[whole(strips.shape)],
            out_specs=[HBM] + [whole(shape) for shape, _ in shapes[1:]],
            scratch_shapes=[
                pltpu.VMEM((blocks, blocks), jnp.float32),
                *list_scratch(groups, peers, cap),
                pltpu.VMEM((lines, LANES), jnp.int32),
                pltpu.VMEM(send, jnp.float32),
                pltpu.SMEM((lines, LANES), jnp.int32),
                pltpu.SemaphoreType.DMA,
                pltpu.SemaphoreType.DMA((groups,)),
            ],
        ),
        out_shape=[pltpu.HBM(*shapes[0])] + [jax.ShapeDtypeStruct(*shape) for shape in shapes[1:]],
        compiler_params=LIMIT,
    )(base.reshape(1), pltpu.with_memory_space_constraint(strips, pltpu.VMEM))


def collect_body(rows, base_ref, by_col_ref, by_row_ref, mates_ref, peak_ref, *refs):
    piece_refs, right_refs = refs[:rows], refs[rows:2 * rows]
    values, keys, picks, places_vmem, panel, places, sem = refs[2 * rows:]
    row_index = lax.axis_index("row")
    count, strip, _ = piece_refs[0].shape
    cap = right_refs[0].shape[0] - 1

    def place_of(name):
        name = (name.astype(jnp.int32) >> 9) - 1
        return (name - (SLOT_PITCH - count) * (name >> 4)).astype(jnp.float32)

    lines, _ = list_products(
        by_col_ref[...], by_row_ref[...], [(mates_ref[2:3, :], mates_ref[3:4, :])],
        place_of, base_ref[0], cap, values, keys, picks,
    )
    lines += lines[-1:] * (places_vmem.shape[0] - len(lines))
    places_vmem[...] = jnp.concatenate(lines, axis=0).astype(jnp.int32)
    copy = pltpu.make_async_copy(places_vmem, places, sem)
    copy.start()
    for away, piece_ref in enumerate(piece_refs):
        start = (row_index + rows - away) % rows * count
        for tile in range(count):
            panel[start + tile] = piece_ref[tile]
    copy.wait()
    for away, right_ref in enumerate(right_refs):
        lane = (row_index + away) % rows * SLOT_PITCH
        for at in range(cap):
            right_ref[at] = panel[places[at // SLOT_PITCH, lane + at % SLOT_PITCH]]
        right_ref[cap, 0:8, :] = peak_ref[...]
        right_ref[cap, 8:16, :] = peak_ref[...]


def collect(tables, mates, peak, pieces, base, peers, cap):
    rows = len(pieces)
    count, strip, order = pieces[0].shape
    right = (cap + 1, strip, order)
    operands = (*tables, mates, peak, *pieces)
    return pl.pallas_call(
        functools.partial(collect_body, rows),
        grid_spec=pltpu.PrefetchScalarGridSpec(
            num_scalar_prefetch=1,
            grid=(1,),
            in_specs=[whole(operand.shape) for operand in operands],
            out_specs=[whole(right)] * rows,
            scratch_shapes=[
                *list_scratch(1, peers, cap),
                pltpu.VMEM((8, LANES), jnp.int32),
                pltpu.VMEM((rows * count, strip, order), jnp.float32),
                pltpu.SMEM((8, LANES), jnp.int32),
                pltpu.SemaphoreType.DMA,
            ],
        ),
        out_shape=[jax.ShapeDtypeStruct(right, jnp.float32)] * rows,
        compiler_params=LIMIT,
    )(base.reshape(1), *tables, mates, peak, *in_hbm(*pieces))


def peak_body(*refs):
    *right_refs, most_ref = refs
    cap = right_refs[0].shape[0] - 1
    most = right_refs[0][cap, 0:8, :]
    for right_ref in right_refs[1:]:
        most = jnp.maximum(most, right_ref[cap, 0:8, :])
    most_ref[...] = most.astype(jnp.int32)


def product_body(first, rows, scalars, codes, counts, left_ref, *refs):
    right_refs, refs = refs[:rows], refs[rows:]
    out_hbm, right, out_ref, sems = refs[-4:]
    out_ref[...] = jnp.zeros_like(out_ref) if first else refs[0][...]
    kept = out_ref.shape[0]
    row_index, own, base = lax.axis_index("row"), lax.axis_index(GROUP), scalars[0]
    peers, cap = left_ref.shape[:2]
    tall_strip = right_refs[0].shape[1]
    line = (own >> 3) * pl.cdiv(cap, SLOT_PITCH)
    lane = (own & (PER_GROUP - 1)) * SLOT_PITCH
    todo = jnp.clip(counts[own >> 3, lane] - base, 0, cap)
    bf16 = jnp.bfloat16

    def product(at, half):
        for away, right_ref in enumerate(right_refs):
            start = pl.multiple_of((row_index + rows - away) % rows * tall_strip, tall_strip)
            right[half, pl.ds(start, tall_strip), :] = right_ref[at]
        a, b = jnp.concatenate([left_ref[peer, at] for peer in range(peers)], axis=0), right[half]
        a_high, b_high = a.astype(bf16), b.astype(bf16)
        a_low = (a - a_high.astype(jnp.float32)).astype(bf16)
        b_low = (b - b_high.astype(jnp.float32)).astype(bf16)
        return jnp.dot(
            jnp.concatenate([a_high, a_low, a_high], axis=1),
            jnp.concatenate([b_high, b_high, b_low], axis=0),
            preferred_element_type=jnp.float32,
        )

    def target(at):
        return codes[line + (at >> 4), lane + (at & (SLOT_PITCH - 1))] >> 16

    def write(tile):
        return pltpu.make_async_copy(out_ref.at[tile], out_hbm.at[tile], sems.at[tile])

    def start(tile, carry):
        write(tile).start()
        return carry

    def several(step, finished):
        at = TOGETHER * step
        lax.fori_loop(finished, target(at), start, 0)
        sums = [product(at + n, n) for n in range(TOGETHER)]
        out_ref[target(at)] += sums[0]
        for n in range(1, TOGETHER):
            @pl.when(at + n < todo)
            def _():
                out_ref[target(at + n)] += sums[n]

        return target(at)

    finished = lax.fori_loop(0, (todo + TOGETHER - 1) // TOGETHER, several, jnp.int32(0))
    lax.fori_loop(finished, kept, start, 0)
    for tile in range(kept):
        write(tile).wait()


def multiply_round(left, right, codes, counts, base, running, kept):
    order = left.shape[-1]
    first = running is None
    tiles = (kept, order, order)
    most = pl.pallas_call(
        peak_body, out_shape=jax.ShapeDtypeStruct((8, LANES), jnp.int32), compiler_params=LIMIT
    )(*right)[0, 0]
    operands = [pltpu.with_memory_space_constraint(x, pltpu.VMEM) for x in (left, *right)] + ([] if first else [running])
    summed = pl.pallas_call(
        functools.partial(product_body, first, len(right)),
        grid_spec=pltpu.PrefetchScalarGridSpec(
            num_scalar_prefetch=3,
            grid=(1,),
            in_specs=[whole(operand.shape) for operand in operands],
            out_specs=HBM,
            scratch_shapes=[
                pltpu.VMEM((TOGETHER, order, order), jnp.float32),
                pltpu.VMEM(tiles, jnp.float32),
                pltpu.SemaphoreType.DMA((kept,)),
            ],
        ),
        out_shape=pltpu.HBM(tiles, jnp.float32),
        compiler_params=LIMIT,
    )(jnp.stack([base, most]), codes, counts, *operands)
    return summed, most


def shift_all(pieces):
    rows = len(pieces)
    return [pieces[0]] + [
        lax.ppermute(pieces[by], "row", [(i, (i + by) % rows) for i in range(rows)]) for by in range(1, rows)
    ]


def swap_rows(array, rows, by):
    return lax.ppermute(array, "row", [(i, i ^ by) for i in range(rows)])


def local(tile_values, tile_rows, tile_cols, tile_counts, out_rows, out_cols):
    order = tile_values.shape[-1]
    kept = out_rows.shape[-1]
    rows = lax.axis_size("row")
    peers = lax.axis_size(GROUP)
    tiles = tile_values.reshape(-1, order, order)

    listed, wanted = label(tile_rows, tile_cols, tile_counts, out_rows, out_cols)
    for by in (1, 2):
        listed = listed + swap_rows(listed, rows, by)
    listed, strips = lax.optimization_barrier((listed, pack(tiles, peers)))
    strips, mates = stamp(listed, swap_rows(listed, rows, rows - 2), wanted, strips)
    pieces = shift_all(pack_right(tiles, rows))
    strips = lax.all_to_all(strips, GROUP, 0, 0, tiled=True)
    strips, pieces = lax.optimization_barrier((strips, pieces))
    strips = strips.reshape(-1, order // peers, order)

    def one_round(base, running):
        send, codes, counts, peak, *tables = plan(strips, base, rows, peers, ROUND_CAP)
        left = lax.all_to_all(send, GROUP, 0, 0, tiled=True)
        right = shift_all(collect(tables, mates, peak, pieces, base, peers, ROUND_CAP))
        return multiply_round(left, right, codes, counts, base, running, kept)

    summed, most = one_round(jnp.zeros((), jnp.int32), None)

    def unfinished(state):
        return state[0] < most

    def further(state):
        return state[0] + ROUND_CAP, one_round(*state)[0]

    unused, summed = lax.while_loop(unfinished, further, (jnp.int32(ROUND_CAP), summed))
    return summed.reshape(1, 1, kept, order, order)


def solution(mesh):
    in_specs = (
        P("row", GROUP, None, None, None, None),
        P("row", GROUP, None, None),
        P("row", GROUP, None, None),
        P("row", GROUP, None),
        P("row", "col", None, None),
        P("row", "col", None, None),
    )
    out_specs = P("row", GROUP, None, None, None)
    return jax.shard_map(local, mesh=mesh, in_specs=in_specs, out_specs=out_specs, check_vma=False)
```

```python
import functools

import jax
import jax.numpy as jnp
from jax import lax
from jax.experimental import pallas as pl
from jax.experimental.pallas import tpu as pltpu
from jax.sharding import PartitionSpec as P

GROUP = ("col", "layer")
LANES = 128
SLOT_PITCH = 16
PER_GROUP = LANES // SLOT_PITCH
ROUND_CAP = 20
TOGETHER = 2
LIMIT = pltpu.CompilerParams(vmem_limit_bytes=20 * 2**20)
HBM = pl.BlockSpec(memory_space=pltpu.HBM)


def in_hbm(*arrays):
    return [pltpu.with_memory_space_constraint(array, pltpu.HBM) for array in arrays]


def padded(size, unit):
    return unit * pl.cdiv(size, unit)


def label_body(*refs):
    sources, listed_ref, wanted_ref, sems, copies = refs[:5], refs[5], refs[6], refs[7], refs[8:]
    moves = [pltpu.make_async_copy(a, b, sems.at[n]) for n, (a, b) in enumerate(zip(sources, copies))]
    for move in moves:
        move.start()
    for move in moves:
        move.wait()
    tile_rows, tile_cols, counts, out_rows, out_cols = copies
    lists, capacity = tile_rows.shape[2:]
    row_index, layer_index = lax.axis_index("row"), lax.axis_index("layer")
    in_group = lax.axis_index(GROUP) % PER_GROUP
    lane = lax.broadcasted_iota(jnp.int32, (1, LANES), 1)
    nothing = jnp.zeros((1, LANES), jnp.int32)
    rows, cols, kept_rows, kept_cols = nothing, nothing, nothing, nothing
    mate_rows, mate_cols = nothing, nothing
    for at in range(lists):
        for slot in range(capacity):
            live = slot < counts[0, 0, at]
            here = lane == jnp.where(live, row_index * SLOT_PITCH + at * capacity + slot, -1)
            rows = jnp.where(here, tile_rows[0, 0, at, slot] + 1, rows)
            cols = jnp.where(here, tile_cols[0, 0, at, slot] + 1, cols)
    for at in range(out_rows.shape[3]):
        target_row, target_col = out_rows[0, 0, layer_index, at] + 1, out_cols[0, 0, layer_index, at] + 1
        here = lane == in_group * SLOT_PITCH + at
        kept_rows = jnp.where(here, target_row, kept_rows)
        kept_cols = jnp.where(here, target_col, kept_cols)
        here = lane == row_index * SLOT_PITCH + at
        mate_rows = jnp.where(here, target_row, mate_rows)
        mate_cols = jnp.where(here, target_col, mate_cols)
    listed_ref[...] = jnp.concatenate([rows, cols, mate_rows, mate_cols]).astype(jnp.float32)
    wanted_ref[...] = jnp.concatenate([kept_rows, kept_cols]).astype(jnp.float32)


def label(tile_rows, tile_cols, tile_counts, out_rows, out_cols):
    operands = (tile_rows, tile_cols, tile_counts, out_rows, out_cols)
    return pl.pallas_call(
        label_body,
        in_specs=[HBM] * 5,
        out_shape=[jax.ShapeDtypeStruct((n, LANES), jnp.float32) for n in (4, 2)],
        scratch_shapes=[pltpu.SemaphoreType.DMA((5,))] + [pltpu.SMEM(x.shape, jnp.int32) for x in operands],
        compiler_params=LIMIT,
    )(*in_hbm(*operands))


def pack_body(tiles_hbm, out_ref, tiles, sems):
    peers, per_peer, strip, _ = out_ref.shape
    for tile in range(per_peer - 1):
        pltpu.make_async_copy(tiles_hbm.at[tile], tiles.at[tile], sems.at[tile]).start()

    def one_tile(tile, carry):
        pltpu.make_async_copy(tiles_hbm.at[tile], tiles.at[tile], sems.at[tile]).wait()
        for peer in range(peers):
            out_ref[peer, tile] = tiles[tile, peer * strip:(peer + 1) * strip, :]
        return carry

    lax.fori_loop(0, per_peer - 1, one_tile, 0)


def pack(tiles, peers):
    count, order = tiles.shape[:2]
    shape = (peers, count + 1, order // peers, order)
    return pl.pallas_call(
        pack_body,
        in_specs=[HBM],
        out_shape=pltpu.HBM(shape, jnp.float32),
        scratch_shapes=[pltpu.VMEM(tiles.shape, jnp.float32), pltpu.SemaphoreType.DMA((count,))],
        compiler_params=LIMIT,
    )(*in_hbm(tiles))


def stamp_body(one_ref, other_ref, wanted_ref, strips_in, strips_out, total_ref, meta, sem):
    peers, per_peer = strips_out.shape[:2]
    total = one_ref[...] + other_ref[...]
    total_ref[...] = total
    full = jnp.concatenate([total[0:2, :], wanted_ref[...]])
    for peer in range(peers):
        meta[peer] = full
    copy = pltpu.make_async_copy(meta, strips_out.at[:, per_peer - 1], sem)
    copy.start()
    copy.wait()


def stamp(one, other, wanted, strips):
    peers, _, strip, order = strips.shape
    vmem = pl.BlockSpec(memory_space=pltpu.VMEM)
    return pl.pallas_call(
        stamp_body,
        in_specs=[vmem, vmem, vmem, HBM],
        out_specs=[HBM, vmem],
        out_shape=[pltpu.HBM(strips.shape, jnp.float32), jax.ShapeDtypeStruct(one.shape, jnp.float32)],
        input_output_aliases={3: 0},
        scratch_shapes=[pltpu.VMEM((peers, strip, order), jnp.float32), pltpu.SemaphoreType.DMA],
        compiler_params=LIMIT,
    )(one, other, wanted, *in_hbm(strips))


def pack_right_body(tiles_ref, *out_refs):
    count, strip, _ = out_refs[0].shape
    row_index = lax.axis_index("row")
    for away, out_ref in enumerate(out_refs):
        start = pl.multiple_of((row_index + away) % len(out_refs) * strip, strip)
        for tile in range(count):
            out_ref[tile] = tiles_ref[tile, pl.ds(start, strip), :]


def pack_right(tiles, rows):
    count, order = tiles.shape[:2]
    shape = (count, order // rows, order)
    return pl.pallas_call(
        pack_right_body, out_shape=[jax.ShapeDtypeStruct(shape, jnp.float32)] * rows, compiler_params=LIMIT
    )(*in_hbm(tiles))


def list_products(by_col, by_row, targets, value_of, base, cap, values, keys, picks):
    blocks = by_col.shape[0]
    groups = len(targets)
    bands = values.shape[0] // groups
    deep = picks.shape[0] // groups
    f32, bf16 = jnp.float32, jnp.bfloat16
    iota = functools.partial(lax.broadcasted_iota, jnp.int32)
    one, zero = jnp.ones((blocks, LANES), bf16), jnp.zeros((blocks, LANES), bf16)
    tall = (iota((blocks, LANES), 0) + 1).astype(f32).astype(bf16)
    below = jnp.where(iota((bands, bands), 0) >= iota((bands, bands), 1), 1.0, 0.0).astype(bf16)
    lane_from, lane_to = iota((LANES, LANES), 0), iota((LANES, LANES), 1)
    same_peer = lane_from // SLOT_PITCH == lane_to // SLOT_PITCH
    earlier = jnp.where(same_peer & (lane_from < lane_to), 1.0, 0.0).astype(bf16)
    together = jnp.where(same_peer, 1.0, 0.0)

    everything = []
    for group, (target_rows, target_cols) in enumerate(targets):
        def hot(target):
            few = jnp.broadcast_to(target, (16, LANES)).astype(bf16)
            return jnp.where(tall == jnp.concatenate([few] * (blocks // 16), axis=0), one, zero)

        left = jnp.dot(by_col, hot(target_rows), preferred_element_type=f32)
        right = jnp.dot(by_row, hot(target_cols), preferred_element_type=f32)
        pair = jnp.where(left * right > 0.0, left + right * 512.0, 0.0)
        name = pair[0:bands, :]
        for place in range(1, blocks // bands):
            name = name + pair[place * bands:(place + 1) * bands, :]
        hit = name > 0.0
        ranks = jnp.dot(below, jnp.where(hit, 1.0, 0.0).astype(bf16), preferred_element_type=f32)
        everything.append(ranks[bands - 1:bands, :])
        keys[group * bands:(group + 1) * bands, :] = jnp.where(hit, ranks, 0.0)
        values[group * bands:(group + 1) * bands, :] = value_of(name)
    found = jnp.concatenate(everything + everything[-1:] * (8 - len(everything)), axis=0)
    ahead = jnp.dot(found.astype(bf16), earlier, preferred_element_type=f32) - base.astype(f32)
    counts = jnp.dot(found.astype(bf16), together.astype(bf16), preferred_element_type=f32)
    picks[...] = jnp.zeros_like(picks)
    depth = jnp.max(found).astype(jnp.int32)
    slot_at = iota((deep, LANES), 0).astype(f32)

    def one_depth(level, carry):
        level_f = level.astype(f32)
        for group in range(groups):
            span = slice(group * bands, (group + 1) * bands)
            value = jnp.sum(jnp.where(keys[span, :] == level_f + 1.0, values[span, :], 0.0), axis=0, keepdims=True)
            place = jnp.where(found[group:group + 1, :] > level_f, ahead[group:group + 1, :] + level_f, -1.0)
            span = slice(group * deep, (group + 1) * deep)
            picks[span, :] = picks[span, :] + jnp.where(slot_at == place, value, 0.0)
        return carry

    lax.fori_loop(0, depth, one_depth, 0)
    spread = jnp.dot(picks[...], together, precision=lax.Precision.HIGHEST, preferred_element_type=f32)
    mine = iota((deep, LANES), 0) % SLOT_PITCH == iota((deep, LANES), 1) % SLOT_PITCH
    lines = []
    for group in range(groups):
        chosen = jnp.where(mine, spread[group * deep:(group + 1) * deep, :], 0.0)
        for half in range(pl.cdiv(cap, SLOT_PITCH)):
            lines.append(jnp.sum(chosen[half * SLOT_PITCH:(half + 1) * SLOT_PITCH, :], axis=0, keepdims=True))
    return lines, counts


def plan_body(
    rows, base_ref, strips_ref,
    send_ref, codes_ref, counts_ref, peak_ref, by_col_ref, by_row_ref,
    table, values, keys, picks, places_vmem, send, places, sem, send_sems,
):
    row_index, base = lax.axis_index("row"), base_ref[0]
    peers, cap = send_ref.shape[:2]
    per_peer = strips_ref.shape[0] // peers
    band = 8
    blocks = peers * band
    band_rows = blocks // rows
    groups = peers // PER_GROUP
    halves = pl.cdiv(cap, SLOT_PITCH)
    f32, bf16 = jnp.float32, jnp.bfloat16
    iota = functools.partial(lax.broadcasted_iota, jnp.int32)

    in_band = iota((band_rows, LANES), 0).astype(f32)
    band_start = (iota((1, LANES), 1) // SLOT_PITCH * band_rows + 1).astype(f32)
    band_mask = jnp.where(iota((blocks, LANES), 0) // band_rows == iota((blocks, LANES), 1) // SLOT_PITCH, 1.0, 0.0)
    band_mask = band_mask.astype(bf16)
    short = iota((band, LANES), 0).astype(f32) + 1.0
    names = iota((band, LANES), 1).astype(f32) + 1.0
    targets = []
    for peer in range(peers):
        meta = strips_ref[peer * per_peer + per_peer - 1]
        row_hot = jnp.where(in_band == meta[0:1, :] - band_start, 1.0, 0.0).astype(bf16)
        row_hot = jnp.concatenate([row_hot] * rows, axis=0) * band_mask
        col_hot = jnp.where(short + float(peer * band) == meta[1:2, :], names, 0.0).astype(bf16)
        table[peer * band:(peer + 1) * band, :] = lax.dot_general(
            col_hot, row_hot, (((1,), (1,)), ((), ())), preferred_element_type=f32
        )
        if peer % PER_GROUP == 0:
            targets.append(meta)
        else:
            targets[-1] = targets[-1] + meta
    by_index = table[...].astype(bf16)
    index = iota((blocks, blocks), 0)
    order = jnp.where(index % peers * band + index // peers == iota((blocks, blocks), 1), 1.0, 0.0).astype(bf16)
    by_col = jnp.dot(order, by_index, preferred_element_type=f32).astype(bf16)
    by_row = lax.dot_general(order, by_index, (((1,), (1,)), ((), ())), preferred_element_type=f32).astype(bf16)
    by_col_ref[...] = by_col
    by_row_ref[...] = by_row

    fixed = iota((peers, LANES), 0) * per_peer + ((iota((peers, LANES), 1) % SLOT_PITCH) << 16)
    fixed = (fixed - (SLOT_PITCH * row_index + 1 + 512)).astype(f32)
    lines, counts = list_products(
        by_col, by_row, [(meta[2:3, :], meta[3:4, :]) for meta in targets],
        lambda name: name + fixed, base, cap, values, keys, picks,
    )
    codes = jnp.concatenate(lines, axis=0).astype(jnp.int32)
    places_vmem[...] = codes & 511
    copy = pltpu.make_async_copy(places_vmem, places, sem)
    copy.start()
    codes_ref[...] = codes
    counts_ref[...] = counts.astype(jnp.int32)
    longest = jnp.max(jnp.max(counts[0:groups, :], axis=0, keepdims=True), axis=1, keepdims=True)
    peak_ref[...] = jnp.broadcast_to(longest, (8, LANES))
    copy.wait()

    def one_group(group):
        part = pl.ds(group * PER_GROUP, PER_GROUP)
        return pltpu.make_async_copy(send.at[part], send_ref.at[part], send_sems.at[group])

    for group in range(groups):
        for peer in range(group * PER_GROUP, (group + 1) * PER_GROUP):
            line, first = group * halves, peer % PER_GROUP * SLOT_PITCH
            for at in range(cap):
                send[peer, at] = strips_ref[places[line + at // SLOT_PITCH, first + at % SLOT_PITCH]]
        one_group(group).start()
    for group in range(groups):
        one_group(group).wait()


def whole(shape):
    return pl.BlockSpec(shape, lambda i, *_: (0,) * len(shape))


def list_scratch(groups, peers, cap):
    lists = pltpu.VMEM((groups * peers, LANES), jnp.float32)
    return [lists, lists, pltpu.VMEM((groups * padded(cap, 8), LANES), jnp.float32)]


def plan(strips, base, rows, peers, cap):
    strip, order = strips.shape[1:]
    groups = peers // PER_GROUP
    lines = groups * pl.cdiv(cap, SLOT_PITCH)
    send = (peers, cap, strip, order)
    blocks = peers * 8
    shapes = [
        (send, jnp.float32), ((lines, LANES), jnp.int32), ((8, LANES), jnp.int32), ((8, LANES), jnp.float32),
        ((blocks, blocks), jnp.bfloat16), ((blocks, blocks), jnp.bfloat16),
    ]
    return pl.pallas_call(
        functools.partial(plan_body, rows),
        grid_spec=pltpu.PrefetchScalarGridSpec(
            num_scalar_prefetch=1,
            grid=(1,),
            in_specs=[whole(strips.shape)],
            out_specs=[HBM] + [whole(shape) for shape, _ in shapes[1:]],
            scratch_shapes=[
                pltpu.VMEM((blocks, blocks), jnp.float32),
                *list_scratch(groups, peers, cap),
                pltpu.VMEM((lines, LANES), jnp.int32),
                pltpu.VMEM(send, jnp.float32),
                pltpu.SMEM((lines, LANES), jnp.int32),
                pltpu.SemaphoreType.DMA,
                pltpu.SemaphoreType.DMA((groups,)),
            ],
        ),
        out_shape=[pltpu.HBM(*shapes[0])] + [jax.ShapeDtypeStruct(*shape) for shape in shapes[1:]],
        compiler_params=LIMIT,
    )(base.reshape(1), pltpu.with_memory_space_constraint(strips, pltpu.VMEM))


def collect_body(rows, base_ref, by_col_ref, by_row_ref, mates_ref, peak_ref, *refs):
    piece_refs, right_refs = refs[:rows], refs[rows:2 * rows]
    values, keys, picks, places_vmem, panel, places, sem = refs[2 * rows:]
    row_index = lax.axis_index("row")
    count, strip, _ = piece_refs[0].shape
    cap = right_refs[0].shape[0] - 1

    def place_of(name):
        name = (name.astype(jnp.int32) >> 9) - 1
        return (name - (SLOT_PITCH - count) * (name >> 4)).astype(jnp.float32)

    lines, _ = list_products(
        by_col_ref[...], by_row_ref[...], [(mates_ref[2:3, :], mates_ref[3:4, :])],
        place_of, base_ref[0], cap, values, keys, picks,
    )
    lines += lines[-1:] * (places_vmem.shape[0] - len(lines))
    places_vmem[...] = jnp.concatenate(lines, axis=0).astype(jnp.int32)
    copy = pltpu.make_async_copy(places_vmem, places, sem)
    copy.start()
    for away, piece_ref in enumerate(piece_refs):
        start = (row_index + rows - away) % rows * count
        for tile in range(count):
            panel[start + tile] = piece_ref[tile]
    copy.wait()
    for away, right_ref in enumerate(right_refs):
        lane = (row_index + away) % rows * SLOT_PITCH
        for at in range(cap):
            right_ref[at] = panel[places[at // SLOT_PITCH, lane + at % SLOT_PITCH]]
        right_ref[cap, 0:8, :] = peak_ref[...]
        right_ref[cap, 8:16, :] = peak_ref[...]


def collect(tables, mates, peak, pieces, base, peers, cap):
    rows = len(pieces)
    count, strip, order = pieces[0].shape
    right = (cap + 1, strip, order)
    operands = (*tables, mates, peak, *pieces)
    return pl.pallas_call(
        functools.partial(collect_body, rows),
        grid_spec=pltpu.PrefetchScalarGridSpec(
            num_scalar_prefetch=1,
            grid=(1,),
            in_specs=[whole(operand.shape) for operand in operands],
            out_specs=[whole(right)] * rows,
            scratch_shapes=[
                *list_scratch(1, peers, cap),
                pltpu.VMEM((8, LANES), jnp.int32),
                pltpu.VMEM((rows * count, strip, order), jnp.float32),
                pltpu.SMEM((8, LANES), jnp.int32),
                pltpu.SemaphoreType.DMA,
            ],
        ),
        out_shape=[jax.ShapeDtypeStruct(right, jnp.float32)] * rows,
        compiler_params=LIMIT,
    )(base.reshape(1), *tables, mates, peak, *in_hbm(*pieces))


def peak_body(*refs):
    *right_refs, most_ref = refs
    cap = right_refs[0].shape[0] - 1
    most = right_refs[0][cap, 0:8, :]
    for right_ref in right_refs[1:]:
        most = jnp.maximum(most, right_ref[cap, 0:8, :])
    most_ref[...] = most.astype(jnp.int32)


def product_body(first, rows, scalars, codes, counts, left_ref, *refs):
    right_refs, refs = refs[:rows], refs[rows:]
    out_ref, right = refs[-2:]
    out_ref[...] = jnp.zeros_like(out_ref) if first else refs[0][...]
    row_index, own, base = lax.axis_index("row"), lax.axis_index(GROUP), scalars[0]
    peers, cap = left_ref.shape[:2]
    tall_strip = right_refs[0].shape[1]
    line = (own >> 3) * pl.cdiv(cap, SLOT_PITCH)
    lane = (own & (PER_GROUP - 1)) * SLOT_PITCH
    todo = jnp.clip(counts[own >> 3, lane] - base, 0, cap)
    bf16 = jnp.bfloat16

    def product(at, half):
        for away, right_ref in enumerate(right_refs):
            start = pl.multiple_of((row_index + rows - away) % rows * tall_strip, tall_strip)
            right[half, pl.ds(start, tall_strip), :] = right_ref[at]
        a, b = jnp.concatenate([left_ref[peer, at] for peer in range(peers)], axis=0), right[half]
        a_high, b_high = a.astype(bf16), b.astype(bf16)
        a_low = (a - a_high.astype(jnp.float32)).astype(bf16)
        b_low = (b - b_high.astype(jnp.float32)).astype(bf16)
        return jnp.dot(
            jnp.concatenate([a_high, a_low, a_high], axis=1),
            jnp.concatenate([b_high, b_high, b_low], axis=0),
            preferred_element_type=jnp.float32,
        )

    def target(at):
        return codes[line + (at >> 4), lane + (at & (SLOT_PITCH - 1))] >> 16

    def several(step, carry):
        at = TOGETHER * step
        sums = [product(at + n, n) for n in range(TOGETHER)]
        out_ref[target(at)] += sums[0]
        for n in range(1, TOGETHER):
            @pl.when(at + n < todo)
            def _():
                out_ref[target(at + n)] += sums[n]

        return carry

    lax.fori_loop(0, (todo + TOGETHER - 1) // TOGETHER, several, 0)


def multiply_round(left, right, codes, counts, base, running, kept):
    order = left.shape[-1]
    first = running is None
    tiles = (kept, order, order)
    most = pl.pallas_call(
        peak_body, out_shape=jax.ShapeDtypeStruct((8, LANES), jnp.int32), compiler_params=LIMIT
    )(*right)[0, 0]
    operands = [pltpu.with_memory_space_constraint(x, pltpu.VMEM) for x in (left, *right)] + ([] if first else [running])
    summed = pl.pallas_call(
        functools.partial(product_body, first, len(right)),
        grid_spec=pltpu.PrefetchScalarGridSpec(
            num_scalar_prefetch=3,
            grid=(1,),
            in_specs=[whole(operand.shape) for operand in operands],
            out_specs=whole(tiles),
            scratch_shapes=[pltpu.VMEM((TOGETHER, order, order), jnp.float32)],
        ),
        out_shape=jax.ShapeDtypeStruct(tiles, jnp.float32),
        compiler_params=LIMIT,
    )(jnp.stack([base, most]), codes, counts, *operands)
    return summed, most


def shift_all(pieces):
    rows = len(pieces)
    return [pieces[0]] + [
        lax.ppermute(pieces[by], "row", [(i, (i + by) % rows) for i in range(rows)]) for by in range(1, rows)
    ]


def swap_rows(array, rows, by):
    return lax.ppermute(array, "row", [(i, i ^ by) for i in range(rows)])


def local(tile_values, tile_rows, tile_cols, tile_counts, out_rows, out_cols):
    order = tile_values.shape[-1]
    kept = out_rows.shape[-1]
    rows = lax.axis_size("row")
    peers = lax.axis_size(GROUP)
    tiles = tile_values.reshape(-1, order, order)

    listed, wanted = label(tile_rows, tile_cols, tile_counts, out_rows, out_cols)
    for by in (1, 2):
        listed = listed + swap_rows(listed, rows, by)
    listed, strips = lax.optimization_barrier((listed, pack(tiles, peers)))
    strips, right_strips = lax.optimization_barrier((strips, pack_right(tiles, rows)))
    strips, mates = stamp(listed, swap_rows(listed, rows, rows - 2), wanted, strips)
    pieces = shift_all(right_strips)
    strips = lax.all_to_all(strips, GROUP, 0, 0, tiled=True)
    strips, pieces = lax.optimization_barrier((strips, pieces))
    strips = strips.reshape(-1, order // peers, order)

    def one_round(base, running):
        send, codes, counts, peak, *tables = plan(strips, base, rows, peers, ROUND_CAP)
        left = lax.all_to_all(send, GROUP, 0, 0, tiled=True)
        right = shift_all(collect(tables, mates, peak, pieces, base, peers, ROUND_CAP))
        return multiply_round(left, right, codes, counts, base, running, kept)

    summed, most = one_round(jnp.zeros((), jnp.int32), None)

    def unfinished(state):
        return state[0] < most

    def further(state):
        return state[0] + ROUND_CAP, one_round(*state)[0]

    unused, summed = lax.while_loop(unfinished, further, (jnp.int32(ROUND_CAP), summed))
    return summed.reshape(1, 1, kept, order, order)


def solution(mesh):
    in_specs = (
        P("row", GROUP, None, None, None, None),
        P("row", GROUP, None, None),
        P("row", GROUP, None, None),
        P("row", GROUP, None),
        P("row", "col", None, None),
        P("row", "col", None, None),
    )
    out_specs = P("row", GROUP, None, None, None)
    return jax.shard_map(local, mesh=mesh, in_specs=in_specs, out_specs=out_specs, check_vma=False)
```

```python
import functools

import jax
import jax.numpy as jnp
from jax import lax
from jax.experimental import pallas as pl
from jax.experimental.pallas import tpu as pltpu
from jax.sharding import PartitionSpec as P

GROUP = ("col", "layer")
LANES = 128
SLOT_PITCH = 16
PER_GROUP = LANES // SLOT_PITCH
ROUND_CAP = 20
TOGETHER = 2
LIMIT = pltpu.CompilerParams(vmem_limit_bytes=20 * 2**20)
HBM = pl.BlockSpec(memory_space=pltpu.HBM)


def in_hbm(*arrays):
    return [pltpu.with_memory_space_constraint(array, pltpu.HBM) for array in arrays]


def padded(size, unit):
    return unit * pl.cdiv(size, unit)


def label_body(*refs):
    sources, listed_ref, wanted_ref, sems, copies = refs[:5], refs[5], refs[6], refs[7], refs[8:]
    moves = [pltpu.make_async_copy(a, b, sems.at[n]) for n, (a, b) in enumerate(zip(sources, copies))]
    for move in moves:
        move.start()
    for move in moves:
        move.wait()
    tile_rows, tile_cols, counts, out_rows, out_cols = copies
    lists, capacity = tile_rows.shape[2:]
    row_index, layer_index = lax.axis_index("row"), lax.axis_index("layer")
    in_group = lax.axis_index(GROUP) % PER_GROUP
    lane = lax.broadcasted_iota(jnp.int32, (1, LANES), 1)
    nothing = jnp.zeros((1, LANES), jnp.int32)
    rows, cols, kept_rows, kept_cols = nothing, nothing, nothing, nothing
    mate_rows, mate_cols = nothing, nothing
    for at in range(lists):
        for slot in range(capacity):
            live = slot < counts[0, 0, at]
            here = lane == jnp.where(live, row_index * SLOT_PITCH + at * capacity + slot, -1)
            rows = jnp.where(here, tile_rows[0, 0, at, slot] + 1, rows)
            cols = jnp.where(here, tile_cols[0, 0, at, slot] + 1, cols)
    for at in range(out_rows.shape[3]):
        target_row, target_col = out_rows[0, 0, layer_index, at] + 1, out_cols[0, 0, layer_index, at] + 1
        here = lane == in_group * SLOT_PITCH + at
        kept_rows = jnp.where(here, target_row, kept_rows)
        kept_cols = jnp.where(here, target_col, kept_cols)
        here = lane == row_index * SLOT_PITCH + at
        mate_rows = jnp.where(here, target_row, mate_rows)
        mate_cols = jnp.where(here, target_col, mate_cols)
    listed_ref[...] = jnp.concatenate([rows, cols, mate_rows, mate_cols]).astype(jnp.float32)
    wanted_ref[...] = jnp.concatenate([kept_rows, kept_cols]).astype(jnp.float32)


def label(tile_rows, tile_cols, tile_counts, out_rows, out_cols):
    operands = (tile_rows, tile_cols, tile_counts, out_rows, out_cols)
    return pl.pallas_call(
        label_body,
        in_specs=[HBM] * 5,
        out_shape=[jax.ShapeDtypeStruct((n, LANES), jnp.float32) for n in (4, 2)],
        scratch_shapes=[pltpu.SemaphoreType.DMA((5,))] + [pltpu.SMEM(x.shape, jnp.int32) for x in operands],
        compiler_params=LIMIT,
    )(*in_hbm(*operands))


def pack_body(tiles_hbm, out_ref, tiles, sems):
    peers, per_peer, strip, _ = out_ref.shape
    for tile in range(per_peer - 1):
        pltpu.make_async_copy(tiles_hbm.at[tile], tiles.at[tile], sems.at[tile]).start()

    def one_tile(tile, carry):
        pltpu.make_async_copy(tiles_hbm.at[tile], tiles.at[tile], sems.at[tile]).wait()
        for peer in range(peers):
            out_ref[peer, tile] = tiles[tile, peer * strip:(peer + 1) * strip, :]
        return carry

    lax.fori_loop(0, per_peer - 1, one_tile, 0)


def pack(tiles, peers):
    count, order = tiles.shape[:2]
    shape = (peers, count + 1, order // peers, order)
    return pl.pallas_call(
        pack_body,
        in_specs=[HBM],
        out_shape=pltpu.HBM(shape, jnp.float32),
        scratch_shapes=[pltpu.VMEM(tiles.shape, jnp.float32), pltpu.SemaphoreType.DMA((count,))],
        compiler_params=LIMIT,
    )(*in_hbm(tiles))


def stamp_body(one_ref, other_ref, wanted_ref, strips_in, strips_out, total_ref, meta, sem):
    peers, per_peer = strips_out.shape[:2]
    total = one_ref[...] + other_ref[...]
    total_ref[...] = total
    full = jnp.concatenate([total[0:2, :], wanted_ref[...]])
    for peer in range(peers):
        meta[peer] = full
    copy = pltpu.make_async_copy(meta, strips_out.at[:, per_peer - 1], sem)
    copy.start()
    copy.wait()


def stamp(one, other, wanted, strips):
    peers, _, strip, order = strips.shape
    vmem = pl.BlockSpec(memory_space=pltpu.VMEM)
    return pl.pallas_call(
        stamp_body,
        in_specs=[vmem, vmem, vmem, HBM],
        out_specs=[HBM, vmem],
        out_shape=[pltpu.HBM(strips.shape, jnp.float32), jax.ShapeDtypeStruct(one.shape, jnp.float32)],
        input_output_aliases={3: 0},
        scratch_shapes=[pltpu.VMEM((peers, strip, order), jnp.float32), pltpu.SemaphoreType.DMA],
        compiler_params=LIMIT,
    )(one, other, wanted, *in_hbm(strips))


def pack_right_body(tiles_ref, *out_refs):
    count, strip, _ = out_refs[0].shape
    row_index = lax.axis_index("row")
    for away, out_ref in enumerate(out_refs):
        start = pl.multiple_of((row_index + away) % len(out_refs) * strip, strip)
        for tile in range(count):
            out_ref[tile] = tiles_ref[tile, pl.ds(start, strip), :]


def pack_right(tiles, rows):
    count, order = tiles.shape[:2]
    shape = (count, order // rows, order)
    return pl.pallas_call(
        pack_right_body, out_shape=[jax.ShapeDtypeStruct(shape, jnp.float32)] * rows, compiler_params=LIMIT
    )(*in_hbm(tiles))


def list_products(by_col, by_row, targets, value_of, base, cap, values, keys, picks):
    blocks = by_col.shape[0]
    groups = len(targets)
    bands = values.shape[0] // groups
    deep = picks.shape[0] // groups
    f32, bf16 = jnp.float32, jnp.bfloat16
    iota = functools.partial(lax.broadcasted_iota, jnp.int32)
    one, zero = jnp.ones((blocks, LANES), bf16), jnp.zeros((blocks, LANES), bf16)
    tall = (iota((blocks, LANES), 0) + 1).astype(f32).astype(bf16)
    below = jnp.where(iota((bands, bands), 0) >= iota((bands, bands), 1), 1.0, 0.0).astype(bf16)
    lane_from, lane_to = iota((LANES, LANES), 0), iota((LANES, LANES), 1)
    same_peer = lane_from // SLOT_PITCH == lane_to // SLOT_PITCH
    earlier = jnp.where(same_peer & (lane_from < lane_to), 1.0, 0.0).astype(bf16)
    together = jnp.where(same_peer, 1.0, 0.0)

    everything = []
    for group, (target_rows, target_cols) in enumerate(targets):
        def hot(target):
            few = jnp.broadcast_to(target, (16, LANES)).astype(bf16)
            return jnp.where(tall == jnp.concatenate([few] * (blocks // 16), axis=0), one, zero)

        left = jnp.dot(by_col, hot(target_rows), preferred_element_type=f32)
        right = jnp.dot(by_row, hot(target_cols), preferred_element_type=f32)
        pair = jnp.where(left * right > 0.0, left + right * 512.0, 0.0)
        name = pair[0:bands, :]
        for place in range(1, blocks // bands):
            name = name + pair[place * bands:(place + 1) * bands, :]
        hit = name > 0.0
        ranks = jnp.dot(below, jnp.where(hit, 1.0, 0.0).astype(bf16), preferred_element_type=f32)
        everything.append(ranks[bands - 1:bands, :])
        keys[group * bands:(group + 1) * bands, :] = jnp.where(hit, ranks, 0.0)
        values[group * bands:(group + 1) * bands, :] = value_of(name)
    found = jnp.concatenate(everything + everything[-1:] * (8 - len(everything)), axis=0)
    ahead = jnp.dot(found.astype(bf16), earlier, preferred_element_type=f32) - base.astype(f32)
    counts = jnp.dot(found.astype(bf16), together.astype(bf16), preferred_element_type=f32)
    picks[...] = jnp.zeros_like(picks)
    depth = jnp.max(found).astype(jnp.int32)
    slot_at = iota((deep, LANES), 0).astype(f32)

    def one_depth(level, carry):
        level_f = level.astype(f32)
        for group in range(groups):
            span = slice(group * bands, (group + 1) * bands)
            value = jnp.sum(jnp.where(keys[span, :] == level_f + 1.0, values[span, :], 0.0), axis=0, keepdims=True)
            place = jnp.where(found[group:group + 1, :] > level_f, ahead[group:group + 1, :] + level_f, -1.0)
            span = slice(group * deep, (group + 1) * deep)
            picks[span, :] = picks[span, :] + jnp.where(slot_at == place, value, 0.0)
        return carry

    lax.fori_loop(0, depth, one_depth, 0)
    spread = jnp.dot(picks[...], together, precision=lax.Precision.HIGHEST, preferred_element_type=f32)
    mine = iota((deep, LANES), 0) % SLOT_PITCH == iota((deep, LANES), 1) % SLOT_PITCH
    lines = []
    for group in range(groups):
        chosen = jnp.where(mine, spread[group * deep:(group + 1) * deep, :], 0.0)
        for half in range(pl.cdiv(cap, SLOT_PITCH)):
            lines.append(jnp.sum(chosen[half * SLOT_PITCH:(half + 1) * SLOT_PITCH, :], axis=0, keepdims=True))
    return lines, counts


def plan_body(
    rows, base_ref, strips_ref,
    send_ref, codes_ref, counts_ref, peak_ref, by_col_ref, by_row_ref,
    table, values, keys, picks, places_vmem, send, places, sem, send_sems,
):
    row_index, base = lax.axis_index("row"), base_ref[0]
    peers, cap = send_ref.shape[:2]
    per_peer = strips_ref.shape[0] // peers
    band = 8
    blocks = peers * band
    band_rows = blocks // rows
    groups = peers // PER_GROUP
    halves = pl.cdiv(cap, SLOT_PITCH)
    f32, bf16 = jnp.float32, jnp.bfloat16
    iota = functools.partial(lax.broadcasted_iota, jnp.int32)

    in_band = iota((band_rows, LANES), 0).astype(f32)
    band_start = (iota((1, LANES), 1) // SLOT_PITCH * band_rows + 1).astype(f32)
    band_mask = jnp.where(iota((blocks, LANES), 0) // band_rows == iota((blocks, LANES), 1) // SLOT_PITCH, 1.0, 0.0)
    band_mask = band_mask.astype(bf16)
    short = iota((band, LANES), 0).astype(f32) + 1.0
    names = iota((band, LANES), 1).astype(f32) + 1.0
    targets = []
    for peer in range(peers):
        meta = strips_ref[peer * per_peer + per_peer - 1]
        row_hot = jnp.where(in_band == meta[0:1, :] - band_start, 1.0, 0.0).astype(bf16)
        row_hot = jnp.concatenate([row_hot] * rows, axis=0) * band_mask
        col_hot = jnp.where(short + float(peer * band) == meta[1:2, :], names, 0.0).astype(bf16)
        table[peer * band:(peer + 1) * band, :] = lax.dot_general(
            col_hot, row_hot, (((1,), (1,)), ((), ())), preferred_element_type=f32
        )
        if peer % PER_GROUP == 0:
            targets.append(meta)
        else:
            targets[-1] = targets[-1] + meta
    by_index = table[...].astype(bf16)
    index = iota((blocks, blocks), 0)
    order = jnp.where(index % peers * band + index // peers == iota((blocks, blocks), 1), 1.0, 0.0).astype(bf16)
    by_col = jnp.dot(order, by_index, preferred_element_type=f32).astype(bf16)
    by_row = lax.dot_general(order, by_index, (((1,), (1,)), ((), ())), preferred_element_type=f32).astype(bf16)
    by_col_ref[...] = by_col
    by_row_ref[...] = by_row

    fixed = iota((peers, LANES), 0) * per_peer + ((iota((peers, LANES), 1) % SLOT_PITCH) << 16)
    fixed = (fixed - (SLOT_PITCH * row_index + 1 + 512)).astype(f32)
    lines, counts = list_products(
        by_col, by_row, [(meta[2:3, :], meta[3:4, :]) for meta in targets],
        lambda name: name + fixed, base, cap, values, keys, picks,
    )
    codes = jnp.concatenate(lines, axis=0).astype(jnp.int32)
    places_vmem[...] = codes & 511
    copy = pltpu.make_async_copy(places_vmem, places, sem)
    copy.start()
    codes_ref[...] = codes
    counts_ref[...] = counts.astype(jnp.int32)
    longest = jnp.max(jnp.max(counts[0:groups, :], axis=0, keepdims=True), axis=1, keepdims=True)
    peak_ref[...] = jnp.broadcast_to(longest, (8, LANES))
    copy.wait()

    def one_group(group):
        part = pl.ds(group * PER_GROUP // 2, PER_GROUP // 2)
        return pltpu.make_async_copy(send.at[part], send_ref.at[part], send_sems.at[group])

    for group in range(2 * groups):
        for peer in range(group * PER_GROUP // 2, (group + 1) * PER_GROUP // 2):
            line, first = peer // PER_GROUP * halves, peer % PER_GROUP * SLOT_PITCH
            for at in range(cap):
                send[peer, at] = strips_ref[places[line + at // SLOT_PITCH, first + at % SLOT_PITCH]]
        one_group(group).start()
    for group in range(2 * groups):
        one_group(group).wait()


def whole(shape):
    return pl.BlockSpec(shape, lambda i, *_: (0,) * len(shape))


def list_scratch(groups, peers, cap):
    lists = pltpu.VMEM((groups * peers, LANES), jnp.float32)
    return [lists, lists, pltpu.VMEM((groups * padded(cap, 8), LANES), jnp.float32)]


def plan(strips, base, rows, peers, cap):
    strip, order = strips.shape[1:]
    groups = peers // PER_GROUP
    lines = groups * pl.cdiv(cap, SLOT_PITCH)
    send = (peers, cap, strip, order)
    blocks = peers * 8
    shapes = [
        (send, jnp.float32), ((lines, LANES), jnp.int32), ((8, LANES), jnp.int32), ((8, LANES), jnp.float32),
        ((blocks, blocks), jnp.bfloat16), ((blocks, blocks), jnp.bfloat16),
    ]
    return pl.pallas_call(
        functools.partial(plan_body, rows),
        grid_spec=pltpu.PrefetchScalarGridSpec(
            num_scalar_prefetch=1,
            grid=(1,),
            in_specs=[whole(strips.shape)],
            out_specs=[HBM] + [whole(shape) for shape, _ in shapes[1:]],
            scratch_shapes=[
                pltpu.VMEM((blocks, blocks), jnp.float32),
                *list_scratch(groups, peers, cap),
                pltpu.VMEM((lines, LANES), jnp.int32),
                pltpu.VMEM(send, jnp.float32),
                pltpu.SMEM((lines, LANES), jnp.int32),
                pltpu.SemaphoreType.DMA,
                pltpu.SemaphoreType.DMA((2 * groups,)),
            ],
        ),
        out_shape=[pltpu.HBM(*shapes[0])] + [jax.ShapeDtypeStruct(*shape) for shape in shapes[1:]],
        compiler_params=LIMIT,
    )(base.reshape(1), pltpu.with_memory_space_constraint(strips, pltpu.VMEM))


def collect_body(rows, base_ref, by_col_ref, by_row_ref, mates_ref, peak_ref, *refs):
    piece_refs, right_refs = refs[:rows], refs[rows:2 * rows]
    values, keys, picks, places_vmem, panel, places, sem = refs[2 * rows:]
    row_index = lax.axis_index("row")
    count, strip, _ = piece_refs[0].shape
    cap = right_refs[0].shape[0] - 1

    def place_of(name):
        name = (name.astype(jnp.int32) >> 9) - 1
        return (name - (SLOT_PITCH - count) * (name >> 4)).astype(jnp.float32)

    lines, _ = list_products(
        by_col_ref[...], by_row_ref[...], [(mates_ref[2:3, :], mates_ref[3:4, :])],
        place_of, base_ref[0], cap, values, keys, picks,
    )
    lines += lines[-1:] * (places_vmem.shape[0] - len(lines))
    places_vmem[...] = jnp.concatenate(lines, axis=0).astype(jnp.int32)
    copy = pltpu.make_async_copy(places_vmem, places, sem)
    copy.start()
    for away, piece_ref in enumerate(piece_refs):
        start = (row_index + rows - away) % rows * count
        for tile in range(count):
            panel[start + tile] = piece_ref[tile]
    copy.wait()
    for away, right_ref in enumerate(right_refs):
        lane = (row_index + away) % rows * SLOT_PITCH
        for at in range(cap):
            right_ref[at] = panel[places[at // SLOT_PITCH, lane + at % SLOT_PITCH]]
        right_ref[cap, 0:8, :] = peak_ref[...]
        right_ref[cap, 8:16, :] = peak_ref[...]


def collect(tables, mates, peak, pieces, base, peers, cap):
    rows = len(pieces)
    count, strip, order = pieces[0].shape
    right = (cap + 1, strip, order)
    operands = (*tables, mates, peak, *pieces)
    return pl.pallas_call(
        functools.partial(collect_body, rows),
        grid_spec=pltpu.PrefetchScalarGridSpec(
            num_scalar_prefetch=1,
            grid=(1,),
            in_specs=[whole(operand.shape) for operand in operands],
            out_specs=[whole(right)] * rows,
            scratch_shapes=[
                *list_scratch(1, peers, cap),
                pltpu.VMEM((8, LANES), jnp.int32),
                pltpu.VMEM((rows * count, strip, order), jnp.float32),
                pltpu.SMEM((8, LANES), jnp.int32),
                pltpu.SemaphoreType.DMA,
            ],
        ),
        out_shape=[jax.ShapeDtypeStruct(right, jnp.float32)] * rows,
        compiler_params=LIMIT,
    )(base.reshape(1), *tables, mates, peak, *in_hbm(*pieces))


def peak_body(*refs):
    *right_refs, most_ref = refs
    cap = right_refs[0].shape[0] - 1
    most = right_refs[0][cap, 0:8, :]
    for right_ref in right_refs[1:]:
        most = jnp.maximum(most, right_ref[cap, 0:8, :])
    most_ref[...] = most.astype(jnp.int32)


def product_body(first, rows, scalars, codes, counts, left_ref, *refs):
    right_refs, refs = refs[:rows], refs[rows:]
    out_ref, right = refs[-2:]
    out_ref[...] = jnp.zeros_like(out_ref) if first else refs[0][...]
    row_index, own, base = lax.axis_index("row"), lax.axis_index(GROUP), scalars[0]
    peers, cap = left_ref.shape[:2]
    tall_strip = right_refs[0].shape[1]
    line = (own >> 3) * pl.cdiv(cap, SLOT_PITCH)
    lane = (own & (PER_GROUP - 1)) * SLOT_PITCH
    todo = jnp.clip(counts[own >> 3, lane] - base, 0, cap)
    bf16 = jnp.bfloat16

    def product(at, half):
        for away, right_ref in enumerate(right_refs):
            start = pl.multiple_of((row_index + rows - away) % rows * tall_strip, tall_strip)
            right[half, pl.ds(start, tall_strip), :] = right_ref[at]
        a, b = jnp.concatenate([left_ref[peer, at] for peer in range(peers)], axis=0), right[half]
        a_high, b_high = a.astype(bf16), b.astype(bf16)
        a_low = (a - a_high.astype(jnp.float32)).astype(bf16)
        b_low = (b - b_high.astype(jnp.float32)).astype(bf16)
        return jnp.dot(
            jnp.concatenate([a_high, a_low, a_high], axis=1),
            jnp.concatenate([b_high, b_high, b_low], axis=0),
            preferred_element_type=jnp.float32,
        )

    def target(at):
        return codes[line + (at >> 4), lane + (at & (SLOT_PITCH - 1))] >> 16

    def several(step, carry):
        at = TOGETHER * step
        sums = [product(at + n, n) for n in range(TOGETHER)]
        out_ref[target(at)] += sums[0]
        for n in range(1, TOGETHER):
            @pl.when(at + n < todo)
            def _():
                out_ref[target(at + n)] += sums[n]

        return carry

    lax.fori_loop(0, (todo + TOGETHER - 1) // TOGETHER, several, 0)


def multiply_round(left, right, codes, counts, base, running, kept):
    order = left.shape[-1]
    first = running is None
    tiles = (kept, order, order)
    most = pl.pallas_call(
        peak_body, out_shape=jax.ShapeDtypeStruct((8, LANES), jnp.int32), compiler_params=LIMIT
    )(*right)[0, 0]
    operands = [pltpu.with_memory_space_constraint(x, pltpu.VMEM) for x in (left, *right)] + ([] if first else [running])
    summed = pl.pallas_call(
        functools.partial(product_body, first, len(right)),
        grid_spec=pltpu.PrefetchScalarGridSpec(
            num_scalar_prefetch=3,
            grid=(1,),
            in_specs=[whole(operand.shape) for operand in operands],
            out_specs=whole(tiles),
            scratch_shapes=[pltpu.VMEM((TOGETHER, order, order), jnp.float32)],
        ),
        out_shape=jax.ShapeDtypeStruct(tiles, jnp.float32),
        compiler_params=LIMIT,
    )(jnp.stack([base, most]), codes, counts, *operands)
    return summed, most


def shift_all(pieces):
    rows = len(pieces)
    return [pieces[0]] + [
        lax.ppermute(pieces[by], "row", [(i, (i + by) % rows) for i in range(rows)]) for by in range(1, rows)
    ]


def swap_rows(array, rows, by):
    return lax.ppermute(array, "row", [(i, i ^ by) for i in range(rows)])


def local(tile_values, tile_rows, tile_cols, tile_counts, out_rows, out_cols):
    order = tile_values.shape[-1]
    kept = out_rows.shape[-1]
    rows = lax.axis_size("row")
    peers = lax.axis_size(GROUP)
    tiles = tile_values.reshape(-1, order, order)

    listed, wanted = label(tile_rows, tile_cols, tile_counts, out_rows, out_cols)
    for by in (1, 2):
        listed = listed + swap_rows(listed, rows, by)
    listed, strips = lax.optimization_barrier((listed, pack(tiles, peers)))
    strips, mates = stamp(listed, swap_rows(listed, rows, rows - 2), wanted, strips)
    pieces = shift_all(pack_right(tiles, rows))
    strips = lax.all_to_all(strips, GROUP, 0, 0, tiled=True)
    strips, pieces = lax.optimization_barrier((strips, pieces))
    strips = strips.reshape(-1, order // peers, order)

    def one_round(base, running):
        send, codes, counts, peak, *tables = plan(strips, base, rows, peers, ROUND_CAP)
        left = lax.all_to_all(send, GROUP, 0, 0, tiled=True)
        right = shift_all(collect(tables, mates, peak, pieces, base, peers, ROUND_CAP))
        return multiply_round(left, right, codes, counts, base, running, kept)

    summed, most = one_round(jnp.zeros((), jnp.int32), None)

    def unfinished(state):
        return state[0] < most

    def further(state):
        return state[0] + ROUND_CAP, one_round(*state)[0]

    unused, summed = lax.while_loop(unfinished, further, (jnp.int32(ROUND_CAP), summed))
    return summed.reshape(1, 1, kept, order, order)


def solution(mesh):
    in_specs = (
        P("row", GROUP, None, None, None, None),
        P("row", GROUP, None, None),
        P("row", GROUP, None, None),
        P("row", GROUP, None),
        P("row", "col", None, None),
        P("row", "col", None, None),
    )
    out_specs = P("row", GROUP, None, None, None)
    return jax.shard_map(local, mesh=mesh, in_specs=in_specs, out_specs=out_specs, check_vma=False)
```
